32 devices in a mesh: dp: 16 (over z, y, core), mp: 2 (over x).
Axes of the slice: x: 2, y: 2, z: 4, core: 2. Of those that a mesh axis runs over, the one named last changes fastest.
Arguments:
- hidden_in: bfloat16 [32768, 1024], P(('dp', 'mp')), may hold values from -6 to 6
- out_grad: bfloat16 [32768, 1024], P(('dp', 'mp')), may hold values from -6 to 6
- ln1_gain: float32 [1024], replicated, may hold values from 0.5 to 1.5
- ln1_bias: float32 [1024], replicated, may hold values from -3 to 3
- w_query: bfloat16 [1024, 1024], P(None, 'mp'), may hold values from -0.1875 to 0.1875
- w_key: bfloat16 [1024, 1024], P(None, 'mp'), may hold values from -0.1875 to 0.1875
- w_value: bfloat16 [1024, 1024], P(None, 'mp'), may hold values from -0.1875 to 0.1875
- w_out: bfloat16 [1024, 1024], P('mp'), may hold values from -1.5 to 1.5
- ln2_gain: float32 [1024], replicated, may hold values from 0.5 to 1.5
- ln2_bias: float32 [1024], replicated, may hold values from -3 to 3
- w_up: bfloat16 [1024, 4096], P(None, 'mp'), may hold values from -0.1875 to 0.1875
- b_up: float32 [4096], P('mp'), may hold values from -3 to 3
- w_down: bfloat16 [4096, 1024], P('mp'), may hold values from -0.09375 to 0.09375
- b_down: float32 [1024], replicated, may hold values from -3 to 3
- rand_blocks: int32 [16, 16, 3], P('mp'), may hold values from 0 to 15
Outputs:
- output: bfloat16 [32768, 1024], P(('dp', 'mp'))
- input_grad: float32 [32768, 1024], P(('dp', 'mp'))
- grad_ln1_gain: float32 [1024], replicated
- grad_ln1_bias: float32 [1024], replicated
- grad_w_query: float32 [1024, 1024], P(None, 'mp')
- grad_w_key: float32 [1024, 1024], P(None, 'mp')
- grad_w_value: float32 [1024, 1024], P(None, 'mp')
- grad_w_out: float32 [1024, 1024], P('mp')
- grad_ln2_gain: float32 [1024], replicated
- grad_ln2_bias: float32 [1024], replicated
- grad_w_up: float32 [1024, 4096], P(None, 'mp')
- grad_b_up: float32 [4096], P('mp')
- grad_w_down: float32 [4096, 1024], P('mp')
- grad_b_down: float32 [1024], replicated
The draws below stay inside these ranges and needn't reach their ends.
Inputs may be any that keep to these rules, and one draw needn't show every extreme that they name: rand_blocks[h, i, r] is a key block of the same sequence; entries may repeat or fall on window or global blocks, and those of the first and last query blocks have no effect.
All inputs are finite; a program needn't handle non-finite values.
Results may differ from the reference program's by a relative error of at most 0.02.
Values may be sent and summed in bfloat16 or wider, within the bound.
A program may use at most 320 MiB of HBM per device.

```python
import jax
import jax.numpy as jnp
from jax import lax

D = 1024
HEADS = 16
HD = 64
FF = 4096
BLOCK = 64
RAND = 3
SEQ = 1024
SEQ_DEV = 2
NB = 16
TOKENS = 32768
N_DP = 16


def with_ends(array, own_key, least, top_value):
    longest = array.shape.index(max(array.shape))
    spots = []
    for shift in (0, 1):
        where = [jax.random.randint(jax.random.fold_in(own_key, axis), (), 0, length) for axis, length in enumerate(array.shape)]
        where[longest] = (where[longest] + shift) % array.shape[longest]
        spots.append(tuple(where))
    return array.at[spots[0]].set(least).at[spots[1]].set(top_value)


def steps_of(key, extent, pieces, smallest, largest):
    def one(dim, blocks):
        steps = jax.random.uniform(jax.random.fold_in(jax.random.fold_in(key, 6), dim), (blocks,), jnp.float32, smallest / len(pieces), largest / len(pieces))
        return jnp.repeat(jnp.exp(steps), extent[dim] // blocks).reshape((-1,) + (1,) * (len(extent) - dim - 1))

    loudness = one(*pieces[0])
    for cut in pieces[1:]:
        loudness = loudness * one(*cut)
    return loudness


def bell_draw(key, dims, scale, bound, split=(), dtype=jnp.bfloat16):
    drawn = jax.random.normal(key, dims, jnp.float32) * scale
    if len(split) > 0:
        drawn = steps_of(key, dims, split, -0.22, 0.18) * drawn
    return jnp.clip(drawn, min=-bound, max=bound).astype(dtype)


def setup_inputs(seed: int = 0) -> dict:
    key_of = jax.random.split(jax.random.key(seed), 16)
    return {
        "hidden_in": bell_draw(key_of[0], (TOKENS, D), 1.0, 6.0, ((0, 32),)),
        "out_grad": bell_draw(key_of[1], (TOKENS, D), 1.0, 6.0, ((0, 32),)),
        "ln1_gain": jnp.clip(1.0 + 0.1 * jax.random.normal(key_of[2], (D,), jnp.float32), 0.5, 1.5),
        "ln1_bias": bell_draw(key_of[3], (D,), 0.5, 3.0, (), jnp.float32),
        "w_query": bell_draw(key_of[4], (D, HEADS * HD), D ** -0.5, 0.1875, ((1, 2),)),
        "w_key": bell_draw(key_of[5], (D, HEADS * HD), D ** -0.5, 0.1875, ((1, 2),)),
        "w_value": bell_draw(key_of[6], (D, HEADS * HD), D ** -0.5, 0.1875, ((1, 2),)),
        "w_out": bell_draw(key_of[7], (HEADS * HD, D), (max(1, HEADS * HD // 64)) ** -0.5, 1.5, ((0, 2),)),
        "ln2_gain": jnp.clip(1.0 + 0.1 * jax.random.normal(key_of[8], (D,), jnp.float32), 0.5, 1.5),
        "ln2_bias": bell_draw(key_of[9], (D,), 0.5, 3.0, (), jnp.float32),
        "w_up": bell_draw(key_of[10], (D, FF), D ** -0.5, 0.1875, ((1, 2),)),
        "b_up": bell_draw(key_of[11], (FF,), 0.5, 3.0, ((0, 2),), jnp.float32),
        "w_down": bell_draw(key_of[12], (FF, D), FF ** -0.5, 0.09375, ((0, 2),)),
        "b_down": bell_draw(key_of[13], (D,), 0.5, 3.0, (), jnp.float32),
        "rand_blocks": with_ends(jax.random.randint(key_of[14], (HEADS, NB, RAND), 0, SEQ // BLOCK), jax.random.fold_in(key_of[14], 1), 0, (SEQ // BLOCK) - 1).astype(jnp.int32),
    }


HIGHEST = lax.Precision.HIGHEST

@jax.custom_vjp
def low(v):
    return lax.optimization_barrier(v.astype(jnp.bfloat16)).astype(jnp.float32)

@jax.custom_vjp
def low_back(v):
    return v

def low_keep(v):
    return (low(v), None)

def low_pass(kept, grad):
    return (grad,)

def back_keep(v):
    return (v, None)

def back_low(kept, grad):
    return (low(grad),)
low.defvjp(low_keep, low_pass)
low_back.defvjp(back_keep, back_low)

def layer_norm(values, norm_gain, norm_bias):
    center = values - lax.optimization_barrier(jnp.mean(values, axis=-1, keepdims=True))
    spread = lax.optimization_barrier(jnp.mean(center * center, axis=-1, keepdims=True))
    return center * lax.rsqrt(spread + 1e-05) * norm_gain + norm_bias

def block_mask(rand_blocks):
    blocks = SEQ // BLOCK
    row_ids = jnp.arange(blocks)[:, None]
    col_ids = jnp.arange(blocks)[None, :]
    window = (jnp.abs(row_ids - col_ids) <= 1) | (col_ids == 0) | (col_ids == blocks - 1) | (row_ids == 0) | (row_ids == blocks - 1)
    picked = jnp.any(rand_blocks[:, :, :, None] == jnp.arange(blocks)[None, None, None, :], axis=2)
    allowed = window[None] | picked
    return jnp.repeat(jnp.repeat(allowed, BLOCK, axis=1), BLOCK, axis=2)

def matmul(former, latter):
    return jnp.dot(former, latter, precision=HIGHEST)

def attend(queries, key_rows, value_rows, allowed):
    scaling = HD ** (-0.5)
    scores = low_back(jnp.einsum('qhd,khd->hqk', queries, key_rows, precision=HIGHEST) * scaling)
    scores = jnp.where(allowed, scores, -1e+30)
    attn_probs = jax.nn.softmax(scores, axis=-1)
    return jnp.einsum('hqk,khd->qhd', low(attn_probs), value_rows, precision=HIGHEST)

def forward(inputs, allowed, ln1_gain, ln1_bias, w_query, w_key, w_value, w_out, ln2_gain, ln2_bias, w_up, b_up, w_down, b_down):
    seq_count = inputs.shape[0] // SEQ
    normed_one = low(layer_norm(inputs, ln1_gain, ln1_bias))
    queries = low_back(low(matmul(normed_one, w_query))).reshape(seq_count, SEQ, HEADS, HD)
    key_rows = low_back(low(matmul(normed_one, w_key))).reshape(seq_count, SEQ, HEADS, HD)
    value_rows = low_back(low(matmul(normed_one, w_value))).reshape(seq_count, SEQ, HEADS, HD)
    context = lax.map(lambda triple: jax.checkpoint(attend)(triple[0], triple[1], triple[2], allowed), (queries, key_rows, value_rows))
    context = low_back(low(context.reshape(seq_count * SEQ, HEADS * HD)))
    attn_out = low_back(matmul(context, w_out))
    middle = inputs + attn_out
    normed_two = low(layer_norm(middle, ln2_gain, ln2_bias))
    up_pre = low_back(matmul(normed_two, w_up) + b_up)
    hidden = low(jax.nn.gelu(up_pre, approximate=True))
    ffn_out = low_back(matmul(hidden, w_down) + b_down)
    return middle + ffn_out

def reference(hidden_in, out_grad, ln1_gain, ln1_bias, w_query, w_key, w_value, w_out, ln2_gain, ln2_bias, w_up, b_up, w_down, b_down, rand_blocks):
    allowed = block_mask(rand_blocks)
    params = tuple((tensor.astype(jnp.float32) for tensor in (ln1_gain, ln1_bias, w_query, w_key, w_value, w_out, ln2_gain, ln2_bias, w_up, b_up, w_down, b_down)))
    inputs = hidden_in.astype(jnp.float32).reshape(N_DP, SEQ_DEV * SEQ, D)
    cotangent = out_grad.astype(jnp.float32).reshape(N_DP, SEQ_DEV * SEQ, D)

    def group_step(running, group_rows):

        def run_layer(row_block, *weights):
            return forward(row_block, allowed, *weights)
        result, pullback = jax.vjp(run_layer, group_rows[0], *params)
        gradients = pullback(group_rows[1])
        running = tuple((summed + addend for summed, addend in zip(running, gradients[1:])))
        return (running, (result, gradients[0]))
    initial = tuple((jnp.zeros_like(tensor) for tensor in params))
    totals, (results, input_grads) = lax.scan(group_step, initial, (inputs, cotangent))
    return (results.reshape(TOKENS, D).astype(jnp.bfloat16), input_grads.reshape(TOKENS, D), totals[0], totals[1], totals[2], totals[3], totals[4], totals[5], totals[6], totals[7], totals[8], totals[9], totals[10], totals[11])
```

```python
import jax
import jax.numpy as jnp
from jax import lax
from jax.experimental import pallas as pl
from jax.experimental.pallas import tpu as pltpu
from jax.sharding import PartitionSpec as P

HD = 64
BLOCK = 64
SEQ = 1024
PAIR = 2 * HD
BF16 = jnp.bfloat16
F32 = jnp.float32
NT = (((1,), (1,)), ((), ()))
TN = (((0,), (0,)), ((), ()))


def layer_norm(values, norm_gain, norm_bias):
    center = values - jnp.mean(values, axis=-1, keepdims=True)
    spread = jnp.mean(center * center, axis=-1, keepdims=True)
    return center * lax.rsqrt(spread + 1e-05) * norm_gain + norm_bias


def block_mask(rand_blocks):
    blocks = SEQ // BLOCK
    row_ids = jnp.arange(blocks)[:, None]
    col_ids = jnp.arange(blocks)[None, :]
    window = (
        (jnp.abs(row_ids - col_ids) <= 1)
        | (col_ids == 0)
        | (col_ids == blocks - 1)
        | (row_ids == 0)
        | (row_ids == blocks - 1)
    )
    picked = jnp.any(rand_blocks[:, :, :, None] == jnp.arange(blocks)[None, None, None, :], axis=2)
    allowed = window[None] | picked
    return jnp.repeat(jnp.repeat(allowed, BLOCK, axis=1), BLOCK, axis=2)


def attend_forward_split(joined_seq, allowed, scaling):
    queries = joined_seq[:, 0]
    key_rows = joined_seq[:, 1]
    value_rows = joined_seq[:, 2]
    scores = (
        jnp.einsum("qhd,khd->hqk", queries, key_rows, preferred_element_type=jnp.float32) * scaling
    )
    scores = jnp.where(allowed, scores, -1e30)
    highest = jnp.max(scores, axis=-1, keepdims=True)
    shifted = jnp.exp(scores - highest)
    row_totals = jnp.sum(shifted, axis=-1, keepdims=True)
    attn_probs = (shifted / row_totals).astype(jnp.bfloat16)
    context = jnp.einsum("hqk,khd->qhd", attn_probs, value_rows, preferred_element_type=jnp.float32)
    return (context.astype(jnp.bfloat16), (highest + jnp.log(row_totals))[..., 0])


def attend_backward_split(seq_items, allowed, scaling):
    joined_seq, grad_context, row_lse = seq_items
    queries = joined_seq[:, 0]
    key_rows = joined_seq[:, 1]
    value_rows = joined_seq[:, 2]
    scores = (
        jnp.einsum("qhd,khd->hqk", queries, key_rows, preferred_element_type=jnp.float32) * scaling
    )
    scores = jnp.where(allowed, scores, -1e30)
    attn_probs = jnp.exp(scores - row_lse[..., None])
    grad_values = jnp.einsum(
        "hqk,qhd->khd",
        attn_probs.astype(jnp.bfloat16),
        grad_context,
        preferred_element_type=jnp.float32,
    ).astype(jnp.bfloat16)
    grad_probs = jnp.einsum(
        "qhd,khd->hqk", grad_context, value_rows, preferred_element_type=jnp.float32
    )
    row_inner = jnp.sum(grad_probs * attn_probs, axis=-1, keepdims=True)
    grad_scores = (attn_probs * (grad_probs - row_inner)).astype(jnp.bfloat16)
    grad_queries = (
        jnp.einsum("hqk,khd->qhd", grad_scores, key_rows, preferred_element_type=jnp.float32)
        * scaling
    ).astype(jnp.bfloat16)
    grad_keys = (
        jnp.einsum("hqk,qhd->khd", grad_scores, queries, preferred_element_type=jnp.float32)
        * scaling
    ).astype(jnp.bfloat16)
    return jnp.stack([grad_queries, grad_keys, grad_values], axis=1)


def split_sequence(
    hidden_in,
    out_grad,
    ln1_gain,
    ln1_bias,
    w_query,
    w_key,
    w_value,
    w_out,
    ln2_gain,
    ln2_bias,
    w_up,
    b_up,
    w_down,
    b_down,
    rand_blocks,
):
    local_heads = rand_blocks.shape[0]
    head_width = local_heads * HD
    local_rows = hidden_in.shape[0]
    seq_count = local_rows * lax.axis_size("mp") // SEQ
    scaling = HD ** (-0.5)
    allowed = block_mask(rand_blocks)
    inputs = hidden_in.astype(jnp.float32)
    w_joined = jnp.concatenate([w_query, w_key, w_value], axis=1)
    normed_one = layer_norm(inputs, ln1_gain, ln1_bias).astype(jnp.bfloat16)
    rows_one = lax.all_gather(normed_one, "mp", axis=0, tiled=True)
    joined = jnp.dot(rows_one, w_joined, preferred_element_type=jnp.float32).astype(jnp.bfloat16)
    joined_seq = joined.reshape(seq_count, SEQ, 3, local_heads, HD)
    context, row_lse = lax.map(
        lambda seq_block: attend_forward_split(seq_block, allowed, scaling), joined_seq
    )
    context_rows = context.reshape(seq_count * SEQ, head_width)
    middle = inputs + lax.psum_scatter(
        jnp.dot(context_rows, w_out, preferred_element_type=jnp.float32).astype(jnp.bfloat16),
        "mp",
        scatter_dimension=0,
        tiled=True,
    ).astype(jnp.float32)
    normed_two = layer_norm(middle, ln2_gain, ln2_bias).astype(jnp.bfloat16)
    rows_two = lax.all_gather(normed_two, "mp", axis=0, tiled=True)
    up_pre = jnp.dot(rows_two, w_up, preferred_element_type=jnp.float32) + b_up
    hidden = jax.nn.gelu(up_pre, approximate=True).astype(jnp.bfloat16)
    output = (
        middle
        + (
            lax.psum_scatter(
                jnp.dot(hidden, w_down, preferred_element_type=jnp.float32).astype(jnp.bfloat16),
                "mp",
                scatter_dimension=0,
                tiled=True,
            ).astype(jnp.float32)
            + b_down
        )
    ).astype(jnp.bfloat16)
    grad_out = out_grad.astype(jnp.float32)
    bias_down = jnp.sum(grad_out, axis=0)
    rows_ffn = lax.all_gather(out_grad, "mp", axis=0, tiled=True)
    grad_hidden = jnp.einsum("nd,fd->nf", rows_ffn, w_down, preferred_element_type=jnp.float32)
    grad_down = jnp.einsum("nf,nd->fd", hidden, rows_ffn, preferred_element_type=jnp.float32)
    gelu_value, gelu_pull = jax.vjp(lambda pre_act: jax.nn.gelu(pre_act, approximate=True), up_pre)
    grad_up = gelu_pull(grad_hidden)[0].astype(jnp.bfloat16)
    bias_up = jnp.sum(grad_up, axis=0, dtype=jnp.float32)
    grad_up_weight = jnp.einsum("nd,nf->df", rows_two, grad_up, preferred_element_type=jnp.float32)
    grad_normed_two = lax.psum_scatter(
        jnp.einsum("nf,df->nd", grad_up, w_up, preferred_element_type=jnp.float32).astype(
            jnp.bfloat16
        ),
        "mp",
        scatter_dimension=0,
        tiled=True,
    ).astype(jnp.float32)
    norm_value_two, norm_pull_two = jax.vjp(layer_norm, middle, ln2_gain, ln2_bias)
    grad_mid_norm, gain_two, bias_two = norm_pull_two(grad_normed_two)
    grad_middle = grad_out + grad_mid_norm
    grad_attn = grad_middle.astype(jnp.bfloat16)
    rows_attn = lax.all_gather(grad_attn, "mp", axis=0, tiled=True)
    grad_context = jnp.einsum(
        "nd,ed->ne", rows_attn, w_out, preferred_element_type=jnp.float32
    ).astype(jnp.bfloat16)
    grad_out_weight = jnp.einsum(
        "ne,nd->ed", context_rows, rows_attn, preferred_element_type=jnp.float32
    )
    grad_joined = lax.map(
        lambda seq_items: attend_backward_split(seq_items, allowed, scaling),
        (joined_seq, grad_context.reshape(seq_count, SEQ, local_heads, HD), row_lse),
    )
    grad_joined = grad_joined.reshape(seq_count * SEQ, 3 * head_width)
    grad_joined_weight = jnp.einsum(
        "nd,ne->de", rows_one, grad_joined, preferred_element_type=jnp.float32
    )
    grad_normed_one = lax.psum_scatter(
        jnp.einsum("ne,de->nd", grad_joined, w_joined, preferred_element_type=jnp.float32).astype(
            jnp.bfloat16
        ),
        "mp",
        scatter_dimension=0,
        tiled=True,
    ).astype(jnp.float32)
    norm_value_one, norm_pull_one = jax.vjp(layer_norm, inputs, ln1_gain, ln1_bias)
    grad_in_norm, gain_one, bias_one = norm_pull_one(grad_normed_one)
    input_grad = grad_middle + grad_in_norm
    grad_joined_weight, grad_out_weight, grad_up_weight, bias_up, grad_down = (
        lax.psum(grad_joined_weight.astype(jnp.bfloat16), "dp").astype(jnp.float32),
        lax.psum(grad_out_weight.astype(jnp.bfloat16), "dp").astype(jnp.float32),
        lax.psum(grad_up_weight.astype(jnp.bfloat16), "dp").astype(jnp.float32),
        lax.psum(bias_up.astype(jnp.bfloat16), "dp").astype(jnp.float32),
        lax.psum(grad_down.astype(jnp.bfloat16), "dp").astype(jnp.float32),
    )
    gain_one, bias_one, gain_two, bias_two, bias_down = lax.psum(
        (gain_one, bias_one, gain_two, bias_two, bias_down), ("dp", "mp")
    )
    grad_query = grad_joined_weight[:, :head_width]
    grad_key = grad_joined_weight[:, head_width : 2 * head_width]
    grad_value = grad_joined_weight[:, 2 * head_width :]
    return (
        output,
        input_grad,
        gain_one,
        bias_one,
        grad_query,
        grad_key,
        grad_value,
        grad_out_weight,
        gain_two,
        bias_two,
        grad_up_weight,
        bias_up,
        grad_down,
        bias_down,
    )


def mm(left, right, dims=(((1,), (0,)), ((), ()))):
    return lax.dot_general(left, right, dims, preferred_element_type=F32)


def head_lanes(rows, head):
    lanes = lax.broadcasted_iota(jnp.int32, rows.shape, 1)
    return jnp.where(lanes // HD == head, rows, jnp.zeros_like(rows))


def masked_scores(key_rows, queries, bias):
    scores = mm(key_rows, queries, NT)
    keys, width = scores.shape
    blocked = scores.reshape(keys // BLOCK, BLOCK, width) + bias[:, None, :]
    return blocked.reshape(keys, width)


def attend_forward_kernel(tile, qkv_ref, bias_ref, context_ref, lse_ref):
    scaling = HD ** (-0.5)
    key_rows = qkv_ref[:, PAIR : 2 * PAIR]
    values_t = qkv_ref[:, 2 * PAIR :].astype(F32).T.astype(BF16)
    for start in range(0, qkv_ref.shape[0], tile):
        rows = slice(start, start + tile)
        queries = qkv_ref[rows, :PAIR] * jnp.asarray(scaling, BF16)
        parts = []
        for head in range(2):
            scores = masked_scores(key_rows, head_lanes(queries, head), bias_ref[head, :, rows])
            highest = jnp.max(scores, axis=0, keepdims=True)
            shifted = jnp.exp(scores - highest)
            totals = jnp.sum(shifted, axis=0, keepdims=True)
            summed = mm(values_t[head * HD : (head + 1) * HD], shifted.astype(BF16))
            parts.append(summed / totals)
            lse_ref[0, head : head + 1, rows] = highest + jnp.log(totals)
        context_ref[rows, :] = jnp.concatenate(parts, axis=0).T.astype(BF16)


def attend_backward_kernel(
    tile, qkv_ref, bias_ref, context_ref, lse_ref, grad_ref, out_ref, key_acc, value_acc
):
    scaling = HD ** (-0.5)
    key_rows = qkv_ref[:, PAIR : 2 * PAIR]
    value_rows = qkv_ref[:, 2 * PAIR :]
    keys_t = key_rows.astype(F32).T.astype(BF16)
    for start in range(0, qkv_ref.shape[0], tile):
        rows = slice(start, start + tile)
        queries = qkv_ref[rows, :PAIR] * jnp.asarray(scaling, BF16)
        grads = grad_ref[rows, :]
        inner_t = (grads.astype(F32) * context_ref[rows, :].astype(F32)).T
        probs, slopes, masked_q, masked_g, parts = [], [], [], [], []
        for head in range(2):
            query_h, grad_h = head_lanes(queries, head), head_lanes(grads, head)
            scores = masked_scores(key_rows, query_h, bias_ref[head, :, rows])
            attn = jnp.exp(scores - lse_ref[0, head : head + 1, rows])
            inner = jnp.sum(inner_t[head * HD : (head + 1) * HD], axis=0, keepdims=True)
            slope = (attn * (mm(value_rows, grad_h, NT) - inner)).astype(BF16)
            parts.append(mm(keys_t[head * HD : (head + 1) * HD], slope) * scaling)
            probs.append(attn.astype(BF16))
            slopes.append(slope)
            masked_q.append(query_h)
            masked_g.append(grad_h)
        out_ref[rows, :PAIR] = jnp.concatenate(parts, axis=0).T.astype(BF16)
        grad_k = mm(jnp.concatenate(slopes, axis=1), jnp.concatenate(masked_q, axis=0))
        grad_v = mm(jnp.concatenate(probs, axis=1), jnp.concatenate(masked_g, axis=0))
        if start == 0:
            key_acc[...] = grad_k
            value_acc[...] = grad_v
        else:
            key_acc[...] += grad_k
            value_acc[...] += grad_v
    out_ref[:, PAIR : 2 * PAIR] = key_acc[...].astype(BF16)
    out_ref[:, 2 * PAIR :] = value_acc[...].astype(BF16)


def attention_cost(pairs, matmuls):
    return pl.CostEstimate(
        flops=matmuls * 2 * pairs * 2 * SEQ * SEQ * 256,
        bytes_accessed=pairs * SEQ * PAIR * 16,
        transcendentals=pairs * 2 * SEQ * SEQ,
    )


VMEM_LIMIT = 48 << 20
TILE = 256


def attend_forward(qkv, bias):
    pairs = qkv.shape[1] // (3 * PAIR)
    blocks = SEQ // BLOCK
    return pl.pallas_call(
        lambda *refs: attend_forward_kernel(TILE, *refs),
        grid=(pairs,),
        in_specs=[
            pl.BlockSpec((SEQ, 3 * PAIR), lambda pair: (0, pair)),
            pl.BlockSpec((2, blocks, SEQ), lambda pair: (pair, 0, 0)),
        ],
        out_specs=[
            pl.BlockSpec((SEQ, PAIR), lambda pair: (0, pair)),
            pl.BlockSpec((1, 2, SEQ), lambda pair: (pair, 0, 0)),
        ],
        out_shape=[
            jax.ShapeDtypeStruct((SEQ, pairs * PAIR), BF16),
            jax.ShapeDtypeStruct((pairs, 2, SEQ), F32),
        ],
        compiler_params=pltpu.CompilerParams(vmem_limit_bytes=VMEM_LIMIT),
        cost_estimate=attention_cost(pairs, 2),
        name="attend_forward",
    )(qkv, bias)


def attend_backward(qkv, bias, context, row_lse, grad_context):
    pairs = qkv.shape[1] // (3 * PAIR)
    blocks = SEQ // BLOCK
    return pl.pallas_call(
        lambda *refs: attend_backward_kernel(TILE, *refs),
        grid=(pairs,),
        in_specs=[
            pl.BlockSpec((SEQ, 3 * PAIR), lambda pair: (0, pair)),
            pl.BlockSpec((2, blocks, SEQ), lambda pair: (pair, 0, 0)),
            pl.BlockSpec((SEQ, PAIR), lambda pair: (0, pair)),
            pl.BlockSpec((1, 2, SEQ), lambda pair: (pair, 0, 0)),
            pl.BlockSpec((SEQ, PAIR), lambda pair: (0, pair)),
        ],
        out_specs=pl.BlockSpec((SEQ, 3 * PAIR), lambda pair: (0, pair)),
        out_shape=jax.ShapeDtypeStruct((SEQ, pairs * 3 * PAIR), BF16),
        scratch_shapes=[pltpu.VMEM((SEQ, PAIR), F32), pltpu.VMEM((SEQ, PAIR), F32)],
        compiler_params=pltpu.CompilerParams(vmem_limit_bytes=VMEM_LIMIT),
        cost_estimate=attention_cost(pairs, 5),
        name="attend_backward",
    )(qkv, bias, context, row_lse, grad_context)


def block_bias(rand_blocks):
    blocks = SEQ // BLOCK
    row_ids = jnp.arange(blocks)[None, :]
    col_ids = jnp.arange(blocks)[:, None]
    window = (
        (jnp.abs(row_ids - col_ids) <= 1)
        | (col_ids == 0)
        | (col_ids == blocks - 1)
        | (row_ids == 0)
        | (row_ids == blocks - 1)
    )
    picked = jnp.any(rand_blocks[:, None, :, :] == col_ids[None, :, :, None], axis=3)
    bias = jnp.where(window[None] | picked, 0.0, -1e30).astype(F32)
    return jnp.repeat(bias, BLOCK, axis=2)


def swap(array, axis, bit):
    size = lax.axis_size(axis)
    return lax.ppermute(array, axis, [(place, place ^ bit) for place in range(size)])


def halves_in_order(mine, other, bit, axis=0):
    return jnp.where(
        bit == 0,
        jnp.concatenate([mine, other], axis=axis),
        jnp.concatenate([other, mine], axis=axis),
    )


def add_up(*terms):
    total = terms[0].astype(F32)
    for term in terms[1:]:
        total = total + term.astype(F32)
    return total.astype(BF16)


def reduce_grads(own_a, own_b, far_a, far_b):
    place = lax.axis_index("dp")
    far = add_up(far_a, swap(far_b, "dp", 1))
    near = add_up(own_a, swap(own_b, "dp", 1), swap(far, "mp", 1))
    bits = []
    step = 2
    while step < lax.axis_size("dp"):
        bits.append(step)
        step *= 2
    for step in bits:
        bit = (place // step) % 2
        rows = near.shape[0] // 2
        keep = lax.dynamic_slice_in_dim(near, bit * rows, rows, 0)
        send = lax.dynamic_slice_in_dim(near, (1 - bit) * rows, rows, 0)
        near = add_up(keep, swap(send, "dp", step))
    for step in reversed(bits):
        bit = (place // step) % 2
        near = halves_in_order(near, swap(near, "dp", step), bit)
    return near, swap(near, "dp", 1)


def whole_sequence(
    hidden_in,
    out_grad,
    ln1_gain,
    ln1_bias,
    w_query,
    w_key,
    w_value,
    w_out,
    ln2_gain,
    ln2_bias,
    w_up,
    b_up,
    w_down,
    b_down,
    rand_blocks,
):
    core = lax.axis_index("dp") % 2
    side = lax.axis_index("mp")

    def piece(array, axis, other):
        size = array.shape[axis] // 2
        return lax.dynamic_slice_in_dim(array, (core ^ other) * size, size, axis)

    def weights_of(other):
        columns = [piece(part, 1, other) for part in (w_query, w_key, w_value)]
        pairs = columns[0].shape[1] // PAIR
        joined = jnp.concatenate(
            [
                part[:, pair * PAIR : (pair + 1) * PAIR]
                for pair in range(pairs)
                for part in columns
            ],
            axis=1,
        )
        return joined, piece(w_out, 0, other), piece(w_up, 1, other), piece(w_down, 0, other)

    own_a, own_b = weights_of(0), weights_of(1)
    far_a = tuple(swap(part, "mp", 1) for part in own_a)
    far_b = tuple(swap(part, "dp", 1) for part in far_a)
    far_bup, far_rand = swap(b_up, "mp", 1), swap(rand_blocks, "mp", 1)
    groups = (own_a, own_b, far_a, far_b)
    joined_w, out_w, up_w, down_w = zip(*groups)
    up_bias = [piece(b_up, 0, 0), piece(b_up, 0, 1), piece(far_bup, 0, 0), piece(far_bup, 0, 1)]
    picks = [
        piece(rand_blocks, 0, 0),
        piece(rand_blocks, 0, 1),
        piece(far_rand, 0, 0),
        piece(far_rand, 0, 1),
    ]
    bias = [block_bias(pick) for pick in picks]
    every = range(4)

    inputs = hidden_in.astype(F32)
    normed_one = layer_norm(inputs, ln1_gain, ln1_bias).astype(BF16)
    qkv = [mm(normed_one, joined_w[g]).astype(BF16) for g in every]
    context, row_lse = zip(*[attend_forward(qkv[g], bias[g]) for g in every])
    middle = inputs
    for g in every:
        middle = middle + mm(context[g], out_w[g])
    normed_two = layer_norm(middle, ln2_gain, ln2_bias).astype(BF16)
    up_pre = [mm(normed_two, up_w[g]) + up_bias[g] for g in every]
    hidden = [jax.nn.gelu(pre, approximate=True).astype(BF16) for pre in up_pre]
    total = middle + b_down
    for g in every:
        total = total + mm(hidden[g], down_w[g])
    output = total.astype(BF16)

    grad_out = out_grad.astype(F32)
    bias_down = jnp.sum(grad_out, axis=0)
    grad_up = []
    for g in every:
        grad_hidden = mm(out_grad, down_w[g], NT)
        pull = jax.vjp(lambda pre: jax.nn.gelu(pre, approximate=True), up_pre[g])[1]
        grad_up.append(pull(grad_hidden)[0].astype(BF16))
    grad_down_w = reduce_grads(*[mm(hidden[g], out_grad, TN).astype(BF16) for g in every])
    bias_up = [jnp.sum(grad_up[g], axis=0, dtype=F32) for g in every]
    grad_up_w = reduce_grads(*[mm(normed_two, grad_up[g], TN).astype(BF16) for g in every])
    grad_normed_two = mm(grad_up[0], up_w[0], NT)
    for g in (1, 2, 3):
        grad_normed_two = grad_normed_two + mm(grad_up[g], up_w[g], NT)
    grad_mid_norm, gain_two, bias_two = jax.vjp(layer_norm, middle, ln2_gain, ln2_bias)[1](
        grad_normed_two
    )
    grad_middle = grad_out + grad_mid_norm
    grad_attn = grad_middle.astype(BF16)
    grad_out_w = reduce_grads(*[mm(context[g], grad_attn, TN).astype(BF16) for g in every])
    grad_qkv = []
    for g in every:
        grad_context = mm(grad_attn, out_w[g], NT).astype(BF16)
        grad_qkv.append(attend_backward(qkv[g], bias[g], context[g], row_lse[g], grad_context))
    grad_joined_w = reduce_grads(*[mm(normed_one, grad_qkv[g], TN).astype(BF16) for g in every])
    grad_normed_one = mm(grad_qkv[0], joined_w[0], NT)
    for g in (1, 2, 3):
        grad_normed_one = grad_normed_one + mm(grad_qkv[g], joined_w[g], NT)
    grad_in_norm, gain_one, bias_one = jax.vjp(layer_norm, inputs, ln1_gain, ln1_bias)[1](
        grad_normed_one
    )
    input_grad = grad_middle + grad_in_norm

    own_bias = halves_in_order(bias_up[0], bias_up[1], core)
    far_bias = halves_in_order(bias_up[2], bias_up[3], core)
    small = lax.psum(
        jnp.concatenate(
            [gain_one, bias_one, gain_two, bias_two, bias_down]
            + [halves_in_order(own_bias, far_bias, side)]
        ),
        ("dp", "mp"),
    )
    width = inputs.shape[1]
    vectors = [small[place * width : (place + 1) * width] for place in range(5)]
    bias_up_sum = lax.dynamic_slice_in_dim(small, 5 * width + side * b_up.shape[0], b_up.shape[0])

    def in_order(pair, axis):
        return halves_in_order(pair[0], pair[1], core, axis).astype(F32)

    def third(pair, which):
        slices = []
        for part in pair:
            pairs = part.shape[1] // (3 * PAIR)
            slices.append(
                jnp.concatenate(
                    [
                        part[:, (3 * place + which) * PAIR : (3 * place + which + 1) * PAIR]
                        for place in range(pairs)
                    ],
                    axis=1,
                )
            )
        return in_order(slices, 1)

    return (
        output,
        input_grad,
        vectors[0],
        vectors[1],
        third(grad_joined_w, 0),
        third(grad_joined_w, 1),
        third(grad_joined_w, 2),
        in_order(grad_out_w, 0),
        vectors[2],
        vectors[3],
        in_order(grad_up_w, 1),
        bias_up_sum,
        in_order(grad_down_w, 0),
        vectors[4],
    )


def solution(mesh):
    in_specs = (
        P(("dp", "mp"), None),
        P(("dp", "mp"), None),
        P(),
        P(),
        P(None, "mp"),
        P(None, "mp"),
        P(None, "mp"),
        P("mp", None),
        P(),
        P(),
        P(None, "mp"),
        P("mp"),
        P("mp", None),
        P(),
        P("mp", None, None),
    )
    out_specs = (
        P(("dp", "mp"), None),
        P(("dp", "mp"), None),
        P(),
        P(),
        P(None, "mp"),
        P(None, "mp"),
        P(None, "mp"),
        P("mp", None),
        P(),
        P(),
        P(None, "mp"),
        P("mp"),
        P("mp", None),
        P(),
    )
    def per_device(hidden_in, *others):
        whole = hidden_in.shape[0] == SEQ and mesh.shape["mp"] == 2
        paired = others[-1].shape[0] % 4 == 0 and mesh.shape["dp"] in (2, 4, 8, 16, 32)
        layer = whole_sequence if whole and paired else split_sequence
        return layer(hidden_in, *others)

    return jax.shard_map(
        per_device, mesh=mesh, in_specs=in_specs, out_specs=out_specs, check_vma=False
    )
```

```python
import jax
import jax.numpy as jnp
from jax import lax
from jax.experimental import pallas as pl
from jax.experimental.pallas import tpu as pltpu
from jax.sharding import PartitionSpec as P

HD = 64
BLOCK = 64
SEQ = 1024
PAIR = 2 * HD
BF16 = jnp.bfloat16
F32 = jnp.float32
NT = (((1,), (1,)), ((), ()))
TN = (((0,), (0,)), ((), ()))


def layer_norm(values, norm_gain, norm_bias):
    center = values - jnp.mean(values, axis=-1, keepdims=True)
    spread = jnp.mean(center * center, axis=-1, keepdims=True)
    return center * lax.rsqrt(spread + 1e-05) * norm_gain + norm_bias


def block_mask(rand_blocks):
    blocks = SEQ // BLOCK
    row_ids = jnp.arange(blocks)[:, None]
    col_ids = jnp.arange(blocks)[None, :]
    window = (
        (jnp.abs(row_ids - col_ids) <= 1)
        | (col_ids == 0)
        | (col_ids == blocks - 1)
        | (row_ids == 0)
        | (row_ids == blocks - 1)
    )
    picked = jnp.any(rand_blocks[:, :, :, None] == jnp.arange(blocks)[None, None, None, :], axis=2)
    allowed = window[None] | picked
    return jnp.repeat(jnp.repeat(allowed, BLOCK, axis=1), BLOCK, axis=2)


def attend_forward_split(joined_seq, allowed, scaling):
    queries = joined_seq[:, 0]
    key_rows = joined_seq[:, 1]
    value_rows = joined_seq[:, 2]
    scores = (
        jnp.einsum("qhd,khd->hqk", queries, key_rows, preferred_element_type=jnp.float32) * scaling
    )
    scores = jnp.where(allowed, scores, -1e30)
    highest = jnp.max(scores, axis=-1, keepdims=True)
    shifted = jnp.exp(scores - highest)
    row_totals = jnp.sum(shifted, axis=-1, keepdims=True)
    attn_probs = (shifted / row_totals).astype(jnp.bfloat16)
    context = jnp.einsum("hqk,khd->qhd", attn_probs, value_rows, preferred_element_type=jnp.float32)
    return (context.astype(jnp.bfloat16), (highest + jnp.log(row_totals))[..., 0])


def attend_backward_split(seq_items, allowed, scaling):
    joined_seq, grad_context, row_lse = seq_items
    queries = joined_seq[:, 0]
    key_rows = joined_seq[:, 1]
    value_rows = joined_seq[:, 2]
    scores = (
        jnp.einsum("qhd,khd->hqk", queries, key_rows, preferred_element_type=jnp.float32) * scaling
    )
    scores = jnp.where(allowed, scores, -1e30)
    attn_probs = jnp.exp(scores - row_lse[..., None])
    grad_values = jnp.einsum(
        "hqk,qhd->khd",
        attn_probs.astype(jnp.bfloat16),
        grad_context,
        preferred_element_type=jnp.float32,
    ).astype(jnp.bfloat16)
    grad_probs = jnp.einsum(
        "qhd,khd->hqk", grad_context, value_rows, preferred_element_type=jnp.float32
    )
    row_inner = jnp.sum(grad_probs * attn_probs, axis=-1, keepdims=True)
    grad_scores = (attn_probs * (grad_probs - row_inner)).astype(jnp.bfloat16)
    grad_queries = (
        jnp.einsum("hqk,khd->qhd", grad_scores, key_rows, preferred_element_type=jnp.float32)
        * scaling
    ).astype(jnp.bfloat16)
    grad_keys = (
        jnp.einsum("hqk,qhd->khd", grad_scores, queries, preferred_element_type=jnp.float32)
        * scaling
    ).astype(jnp.bfloat16)
    return jnp.stack([grad_queries, grad_keys, grad_values], axis=1)


def split_sequence(
    hidden_in,
    out_grad,
    ln1_gain,
    ln1_bias,
    w_query,
    w_key,
    w_value,
    w_out,
    ln2_gain,
    ln2_bias,
    w_up,
    b_up,
    w_down,
    b_down,
    rand_blocks,
):
    local_heads = rand_blocks.shape[0]
    head_width = local_heads * HD
    local_rows = hidden_in.shape[0]
    seq_count = local_rows * lax.axis_size("mp") // SEQ
    scaling = HD ** (-0.5)
    allowed = block_mask(rand_blocks)
    inputs = hidden_in.astype(jnp.float32)
    w_joined = jnp.concatenate([w_query, w_key, w_value], axis=1)
    normed_one = layer_norm(inputs, ln1_gain, ln1_bias).astype(jnp.bfloat16)
    rows_one = lax.all_gather(normed_one, "mp", axis=0, tiled=True)
    joined = jnp.dot(rows_one, w_joined, preferred_element_type=jnp.float32).astype(jnp.bfloat16)
    joined_seq = joined.reshape(seq_count, SEQ, 3, local_heads, HD)
    context, row_lse = lax.map(
        lambda seq_block: attend_forward_split(seq_block, allowed, scaling), joined_seq
    )
    context_rows = context.reshape(seq_count * SEQ, head_width)
    middle = inputs + lax.psum_scatter(
        jnp.dot(context_rows, w_out, preferred_element_type=jnp.float32).astype(jnp.bfloat16),
        "mp",
        scatter_dimension=0,
        tiled=True,
    ).astype(jnp.float32)
    normed_two = layer_norm(middle, ln2_gain, ln2_bias).astype(jnp.bfloat16)
    rows_two = lax.all_gather(normed_two, "mp", axis=0, tiled=True)
    up_pre = jnp.dot(rows_two, w_up, preferred_element_type=jnp.float32) + b_up
    hidden = jax.nn.gelu(up_pre, approximate=True).astype(jnp.bfloat16)
    output = (
        middle
        + (
            lax.psum_scatter(
                jnp.dot(hidden, w_down, preferred_element_type=jnp.float32).astype(jnp.bfloat16),
                "mp",
                scatter_dimension=0,
                tiled=True,
            ).astype(jnp.float32)
            + b_down
        )
    ).astype(jnp.bfloat16)
    grad_out = out_grad.astype(jnp.float32)
    bias_down = jnp.sum(grad_out, axis=0)
    rows_ffn = lax.all_gather(out_grad, "mp", axis=0, tiled=True)
    grad_hidden = jnp.einsum("nd,fd->nf", rows_ffn, w_down, preferred_element_type=jnp.float32)
    grad_down = jnp.einsum("nf,nd->fd", hidden, rows_ffn, preferred_element_type=jnp.float32)
    gelu_value, gelu_pull = jax.vjp(lambda pre_act: jax.nn.gelu(pre_act, approximate=True), up_pre)
    grad_up = gelu_pull(grad_hidden)[0].astype(jnp.bfloat16)
    bias_up = jnp.sum(grad_up, axis=0, dtype=jnp.float32)
    grad_up_weight = jnp.einsum("nd,nf->df", rows_two, grad_up, preferred_element_type=jnp.float32)
    grad_normed_two = lax.psum_scatter(
        jnp.einsum("nf,df->nd", grad_up, w_up, preferred_element_type=jnp.float32).astype(
            jnp.bfloat16
        ),
        "mp",
        scatter_dimension=0,
        tiled=True,
    ).astype(jnp.float32)
    norm_value_two, norm_pull_two = jax.vjp(layer_norm, middle, ln2_gain, ln2_bias)
    grad_mid_norm, gain_two, bias_two = norm_pull_two(grad_normed_two)
    grad_middle = grad_out + grad_mid_norm
    grad_attn = grad_middle.astype(jnp.bfloat16)
    rows_attn = lax.all_gather(grad_attn, "mp", axis=0, tiled=True)
    grad_context = jnp.einsum(
        "nd,ed->ne", rows_attn, w_out, preferred_element_type=jnp.float32
    ).astype(jnp.bfloat16)
    grad_out_weight = jnp.einsum(
        "ne,nd->ed", context_rows, rows_attn, preferred_element_type=jnp.float32
    )
    grad_joined = lax.map(
        lambda seq_items: attend_backward_split(seq_items, allowed, scaling),
        (joined_seq, grad_context.reshape(seq_count, SEQ, local_heads, HD), row_lse),
    )
    grad_joined = grad_joined.reshape(seq_count * SEQ, 3 * head_width)
    grad_joined_weight = jnp.einsum(
        "nd,ne->de", rows_one, grad_joined, preferred_element_type=jnp.float32
    )
    grad_normed_one = lax.psum_scatter(
        jnp.einsum("ne,de->nd", grad_joined, w_joined, preferred_element_type=jnp.float32).astype(
            jnp.bfloat16
        ),
        "mp",
        scatter_dimension=0,
        tiled=True,
    ).astype(jnp.float32)
    norm_value_one, norm_pull_one = jax.vjp(layer_norm, inputs, ln1_gain, ln1_bias)
    grad_in_norm, gain_one, bias_one = norm_pull_one(grad_normed_one)
    input_grad = grad_middle + grad_in_norm
    grad_joined_weight, grad_out_weight, grad_up_weight, bias_up, grad_down = (
        lax.psum(grad_joined_weight.astype(jnp.bfloat16), "dp").astype(jnp.float32),
        lax.psum(grad_out_weight.astype(jnp.bfloat16), "dp").astype(jnp.float32),
        lax.psum(grad_up_weight.astype(jnp.bfloat16), "dp").astype(jnp.float32),
        lax.psum(bias_up.astype(jnp.bfloat16), "dp").astype(jnp.float32),
        lax.psum(grad_down.astype(jnp.bfloat16), "dp").astype(jnp.float32),
    )
    gain_one, bias_one, gain_two, bias_two, bias_down = lax.psum(
        (gain_one, bias_one, gain_two, bias_two, bias_down), ("dp", "mp")
    )
    grad_query = grad_joined_weight[:, :head_width]
    grad_key = grad_joined_weight[:, head_width : 2 * head_width]
    grad_value = grad_joined_weight[:, 2 * head_width :]
    return (
        output,
        input_grad,
        gain_one,
        bias_one,
        grad_query,
        grad_key,
        grad_value,
        grad_out_weight,
        gain_two,
        bias_two,
        grad_up_weight,
        bias_up,
        grad_down,
        bias_down,
    )


VMEM_LIMIT = 56 << 20
TILE = 256
PACE = 0.02


def mm(left, right, dims=(((1,), (0,)), ((), ()))):
    return lax.dot_general(left, right, dims, preferred_element_type=F32)


def call(body, *, grid, in_specs, out_specs, out_shape, micros, name, scratch=(), scalars=1):
    return pl.pallas_call(
        body,
        grid_spec=pltpu.PrefetchScalarGridSpec(
            num_scalar_prefetch=scalars,
            grid=grid,
            in_specs=in_specs,
            out_specs=out_specs,
            scratch_shapes=list(scratch),
        ),
        out_shape=out_shape,
        compiler_params=pltpu.CompilerParams(vmem_limit_bytes=VMEM_LIMIT),
        cost_estimate=pl.CostEstimate(
            flops=int(micros * PACE * 1e9), bytes_accessed=0, transcendentals=0
        ),
        name=name,
    )


def shape(rows, columns, dtype=BF16):
    return jax.ShapeDtypeStruct((rows, columns), dtype)


def row_tile(width, dtype=None):
    return pl.BlockSpec((TILE, width), lambda i, s: (i, 0))


def column_tile(height):
    return pl.BlockSpec((height, TILE), lambda i, s: (0, i))


def resident(rows, columns):
    return pl.BlockSpec((rows, columns), lambda i, s: (0, 0))


def norm_parts(values):
    center = values - jnp.mean(values, axis=-1, keepdims=True)
    spread = jnp.mean(center * center, axis=-1, keepdims=True)
    return center, lax.rsqrt(spread + 1e-05)


def norm_backward(values, gain, grads):
    center, scale = norm_parts(values)
    unit = center * scale
    scaled = grads * gain
    mean_g = jnp.mean(scaled, axis=-1, keepdims=True)
    mean_gu = jnp.mean(scaled * unit, axis=-1, keepdims=True)
    grad_in = scale * (scaled - mean_g - unit * mean_gu)
    return (
        grad_in,
        jnp.sum(grads * unit, axis=0, keepdims=True),
        jnp.sum(grads, axis=0, keepdims=True),
    )


def flipped(rows):
    return rows.astype(F32).T.astype(BF16)


def accumulate(ref, value):
    @pl.when(pl.program_id(0) == 0)
    def _():
        ref[...] = value

    @pl.when(pl.program_id(0) > 0)
    def _():
        ref[...] += value


def norm_in_kernel(s, x_ref, g_ref, gain_ref, bias_ref, n_ref, nt_ref, gt_ref, sum_ref):
    center, scale = norm_parts(x_ref[...].astype(F32))
    normed = center * scale * gain_ref[...] + bias_ref[...]
    n_ref[...] = normed.astype(BF16)
    nt_ref[...] = flipped(n_ref[...])
    grads = g_ref[...]
    gt_ref[...] = flipped(grads)
    accumulate(sum_ref, jnp.sum(grads.astype(F32), axis=0, keepdims=True))


def norm_in(place, hidden_in, out_grad, gain, bias):
    rows, width = hidden_in.shape
    return call(
        norm_in_kernel,
        grid=(rows // TILE,),
        in_specs=[row_tile(width), row_tile(width), resident(1, width), resident(1, width)],
        out_specs=[row_tile(width), column_tile(width), column_tile(width), resident(1, width)],
        out_shape=[shape(rows, width), shape(width, rows), shape(width, rows), shape(1, width, F32)],
        micros=5,
        name="norm_in",
    )(place, hidden_in, out_grad, gain, bias)


def head_lanes(rows, head):
    lanes = lax.broadcasted_iota(jnp.int32, rows.shape, 1)
    return jnp.where(lanes // HD == head, rows, jnp.zeros_like(rows))


def masked_scores(key_rows, queries, bias):
    scores = mm(key_rows, queries, NT)
    keys, width = scores.shape
    blocked = scores.reshape(keys // BLOCK, BLOCK, width) + bias[:, None, :]
    return blocked.reshape(keys, width)


def attend_forward_kernel(s, q_ref, k_ref, v_ref, bias_ref, context_ref, lse_ref):
    scaling = HD ** (-0.5)
    key_rows = k_ref[...]
    values_t = flipped(v_ref[...])
    for start in range(0, q_ref.shape[0], TILE):
        rows = slice(start, start + TILE)
        queries = q_ref[rows, :] * jnp.asarray(scaling, BF16)
        parts = []
        for head in range(2):
            scores = masked_scores(key_rows, head_lanes(queries, head), bias_ref[head, :, rows])
            highest = jnp.max(scores, axis=0, keepdims=True)
            shifted = jnp.exp(scores - highest)
            totals = jnp.sum(shifted, axis=0, keepdims=True)
            summed = mm(values_t[head * HD : (head + 1) * HD], shifted.astype(BF16))
            parts.append(summed / totals)
            lse_ref[0, head : head + 1, rows] = highest + jnp.log(totals)
        context_ref[rows, :] = jnp.concatenate(parts, axis=0).T.astype(BF16)


def thin_block(column):
    return pl.BlockSpec((SEQ, PAIR), lambda p, s: (0, column(p)))


def attend_forward(place, which, qkv, bias):
    pairs = 2
    blocks = SEQ // BLOCK
    return call(
        attend_forward_kernel,
        grid=(pairs,),
        in_specs=[
            thin_block(lambda p: p),
            thin_block(lambda p: pairs + p),
            thin_block(lambda p: 2 * pairs + p),
            pl.BlockSpec((2, blocks, SEQ), lambda p, s: (s[which % 2] * pairs + p, 0, 0)),
        ],
        out_specs=[thin_block(lambda p: p), pl.BlockSpec((1, 2, SEQ), lambda p, s: (p, 0, 0))],
        out_shape=[shape(SEQ, pairs * PAIR), jax.ShapeDtypeStruct((pairs, 2, SEQ), F32)],
        micros=12,
        name="attend_forward",
    )(place, qkv, qkv, qkv, bias)


def attend_backward_kernel(
    s, q_ref, k_ref, v_ref, grad_ref, context_ref, lse_ref, bias_ref, out_ref, key_acc, value_acc
):
    scaling = HD ** (-0.5)
    key_rows = k_ref[...]
    value_rows = v_ref[...]
    keys_t = flipped(key_rows)
    for start in range(0, q_ref.shape[0], TILE):
        rows = slice(start, start + TILE)
        queries = q_ref[rows, :] * jnp.asarray(scaling, BF16)
        grads = grad_ref[rows, :]
        inner_t = (grads.astype(F32) * context_ref[rows, :].astype(F32)).T
        probs, slopes, masked_q, masked_g, parts = [], [], [], [], []
        for head in range(2):
            query_h, grad_h = head_lanes(queries, head), head_lanes(grads, head)
            scores = masked_scores(key_rows, query_h, bias_ref[head, :, rows])
            attn = jnp.exp(scores - lse_ref[0, head : head + 1, rows])
            inner = jnp.sum(inner_t[head * HD : (head + 1) * HD], axis=0, keepdims=True)
            slope = (attn * (mm(value_rows, grad_h, NT) - inner)).astype(BF16)
            parts.append(mm(keys_t[head * HD : (head + 1) * HD], slope) * scaling)
            probs.append(attn.astype(BF16))
            slopes.append(slope)
            masked_q.append(query_h)
            masked_g.append(grad_h)
        out_ref[rows, :PAIR] = jnp.concatenate(parts, axis=0).T.astype(BF16)
        grad_k = mm(jnp.concatenate(slopes, axis=1), jnp.concatenate(masked_q, axis=0))
        grad_v = mm(jnp.concatenate(probs, axis=1), jnp.concatenate(masked_g, axis=0))
        if start == 0:
            key_acc[...] = grad_k
            value_acc[...] = grad_v
        else:
            key_acc[...] += grad_k
            value_acc[...] += grad_v
    out_ref[:, PAIR : 2 * PAIR] = key_acc[...].astype(BF16)
    out_ref[:, 2 * PAIR :] = value_acc[...].astype(BF16)


def attend_backward(place, which, pair, qkv, grad_context, context, row_lse, bias):
    pairs = 2
    blocks = SEQ // BLOCK
    return call(
        attend_backward_kernel,
        grid=(1,),
        in_specs=[
            thin_block(lambda p: pair),
            thin_block(lambda p: pairs + pair),
            thin_block(lambda p: 2 * pairs + pair),
            thin_block(lambda p: pair),
            thin_block(lambda p: pair),
            pl.BlockSpec((1, 2, SEQ), lambda p, s: (pair, 0, 0)),
            pl.BlockSpec((2, blocks, SEQ), lambda p, s: (s[which % 2] * pairs + pair, 0, 0)),
        ],
        out_specs=pl.BlockSpec((SEQ, 3 * PAIR), lambda p, s: (0, 0)),
        out_shape=shape(SEQ, 3 * PAIR),
        scratch=[pltpu.VMEM((SEQ, PAIR), F32), pltpu.VMEM((SEQ, PAIR), F32)],
        micros=8,
        name="attend_backward",
    )(place, qkv, qkv, qkv, grad_context, context, row_lse, bias)


def project_out_kernel(s, x_ref, *refs):
    contexts, weights = refs[:4], refs[4:8]
    gain_ref, bias_ref, middle_ref, n_ref, nt_ref = refs[8:]
    middle = x_ref[...].astype(F32)
    for context_ref, w_ref in zip(contexts, weights):
        middle = middle + mm(context_ref[...], w_ref[...])
    middle_ref[...] = middle
    center, scale = norm_parts(middle)
    normed = (center * scale * gain_ref[...] + bias_ref[...]).astype(BF16)
    n_ref[...] = normed
    nt_ref[...] = flipped(normed)


def own_then_far(block, along):
    specs = []
    for which in range(4):
        if along == 0:
            specs.append(pl.BlockSpec(block, lambda i, s, which=which: (s[which], 0)))
        else:
            specs.append(pl.BlockSpec(block, lambda i, s, which=which: (0, s[which])))
    return specs


def project_out(place, hidden_in, contexts, weights, gain, bias):
    rows, width = hidden_in.shape
    return call(
        project_out_kernel,
        grid=(rows // TILE,),
        in_specs=[row_tile(width)]
        + [row_tile(2 * PAIR)] * 4
        + own_then_far((2 * PAIR, width), 0)
        + [resident(1, width)] * 2,
        out_specs=[row_tile(width), row_tile(width), column_tile(width)],
        out_shape=[shape(rows, width, F32), shape(rows, width), shape(width, rows)],
        micros=7,
        name="project_out",
    )(place, hidden_in, *contexts, *weights, gain, bias)


def gelu_and_slope(pre):
    root, cubic = 0.7978845608028654, 0.044715
    square = pre * pre
    bent = jnp.tanh(root * (pre + cubic * pre * square))
    half = 0.5 * pre
    slope = 0.5 * (1.0 + bent) + half * (1.0 - bent * bent) * (root * (1.0 + 3.0 * cubic * square))
    return half + half * bent, slope


def feed_forward_kernel(tiles, s, n_ref, g_ref, bias_ref, *refs):
    ups, downs = refs[: len(refs) // 2 - 1], refs[len(refs) // 2 - 1 : -3]
    h_ref, gu_ref, sum_ref = refs[-3:]

    def run(up_ref, down_ref):
        pre = mm(n_ref[...], up_ref[...]) + bias_ref[...]
        grad_hidden = mm(g_ref[...], down_ref[...], NT)
        value, slope = gelu_and_slope(pre)
        h_ref[...] = value.astype(BF16)
        grad_up = (grad_hidden * slope).astype(BF16)
        gu_ref[...] = grad_up
        sum_ref[...] = jnp.sum(grad_up.astype(F32), axis=0, keepdims=True)

    if len(ups) == 1:
        run(ups[0], downs[0])
    else:
        mine = pl.program_id(0) // (tiles // 2) == s[4]

        @pl.when(mine)
        def _():
            run(ups[0], downs[0])

        @pl.when(jnp.logical_not(mine))
        def _():
            run(ups[1], downs[1])


def feed_forward(place, which, normed, out_grad, w_up, b_up, w_down):
    rows, width = normed.shape
    units = b_up.shape[1] // 2
    tiles = units // TILE
    if which < 2:
        columns = [lambda i, s: (0, s[which] * tiles + i)]
        lines = [lambda i, s: (s[which] * tiles + i, 0)]
    else:
        columns = [lambda i, s: (0, i % (tiles // 2))] * 2
        lines = [lambda i, s: (i % (tiles // 2), 0)] * 2
    return call(
        lambda *refs: feed_forward_kernel(tiles, *refs),
        grid=(tiles,),
        in_specs=[
            resident(rows, width),
            resident(rows, width),
            pl.BlockSpec((1, TILE), lambda i, s: (0, s[which % 2] * tiles + i)),
        ]
        + [pl.BlockSpec((width, TILE), column) for column in columns]
        + [pl.BlockSpec((TILE, width), line) for line in lines],
        out_specs=[column_tile(rows), column_tile(rows), column_tile(1)],
        out_shape=[shape(rows, units), shape(rows, units), shape(1, units, F32)],
        micros=12,
        name="feed_forward",
    )(place, normed, out_grad, b_up, *w_up, *w_down)


def unit_blocks(units, width, along):
    half = units // 2
    rows = [pl.BlockSpec((TILE, units), lambda i, s: (i, 0))] * 2
    rows += [
        pl.BlockSpec((TILE, half), lambda i, s: (i, s[4])),
        pl.BlockSpec((TILE, half), lambda i, s: (i, 1 - s[4])),
    ] * 2
    if along == 0:
        own = [
            pl.BlockSpec((units, width), lambda i, s, which=which: (s[which], 0)) for which in (0, 1)
        ]
        return rows + own + [resident(half, width)] * 4
    own = [pl.BlockSpec((width, units), lambda i, s, which=which: (0, s[which])) for which in (0, 1)]
    return rows + own + [resident(width, half)] * 4


def unit_arrays(slices, weights):
    own_a, own_b, far_a, far_b = slices
    return [own_a, own_b, far_a, far_a, far_b, far_b] + [part for group in weights for part in group]


def middle_back_kernel(s, g_ref, middle_ref, gain_ref, *refs):
    grads, weights = refs[:6], refs[6:12]
    gm_ref, ga_ref, gat_ref, gain_sum, bias_sum = refs[12:]
    total = mm(grads[0][...], weights[0][...], NT)
    for grad_ref, w_ref in zip(grads[1:], weights[1:]):
        total = total + mm(grad_ref[...], w_ref[...], NT)
    grad_in, gain, bias = norm_backward(middle_ref[...], gain_ref[...], total)
    grad_middle = g_ref[...].astype(F32) + grad_in
    gm_ref[...] = grad_middle
    ga_ref[...] = grad_middle.astype(BF16)
    gat_ref[...] = flipped(ga_ref[...])
    accumulate(gain_sum, gain)
    accumulate(bias_sum, bias)


def middle_back(place, out_grad, middle, gain, grad_up, weights):
    rows, width = middle.shape
    units = grad_up[0].shape[1]
    return call(
        middle_back_kernel,
        grid=(rows // TILE,),
        in_specs=[row_tile(width), row_tile(width), resident(1, width)]
        + unit_blocks(units, width, 1),
        out_specs=[row_tile(width), row_tile(width), column_tile(width)] + [resident(1, width)] * 2,
        out_shape=[shape(rows, width, F32), shape(rows, width), shape(width, rows)]
        + [shape(1, width, F32)] * 2,
        micros=18,
        name="middle_back",
    )(place, out_grad, middle, gain, *unit_arrays(grad_up, weights))


def input_back_kernel(s, x_ref, gm_ref, gain_ref, *refs):
    grads, weights = refs[:8], refs[8:12]
    out_ref, gain_sum, bias_sum = refs[12:]
    total = None
    for group in range(4):
        pair_0, pair_1 = grads[2 * group][...], grads[2 * group + 1][...]
        joined = jnp.concatenate(
            [
                pair[:, part * PAIR : (part + 1) * PAIR]
                for part in range(3)
                for pair in (pair_0, pair_1)
            ],
            axis=1,
        )
        product = mm(joined, weights[group][...], NT)
        total = product if total is None else total + product
    grad_in, gain, bias = norm_backward(x_ref[...].astype(F32), gain_ref[...], total)
    out_ref[...] = gm_ref[...] + grad_in
    accumulate(gain_sum, gain)
    accumulate(bias_sum, bias)


def input_back(place, hidden_in, grad_middle, gain, grads, weights):
    rows, width = hidden_in.shape
    return call(
        input_back_kernel,
        grid=(rows // TILE,),
        in_specs=[row_tile(width), row_tile(width), resident(1, width)]
        + [row_tile(3 * PAIR)] * 8
        + [resident(width, 6 * PAIR)] * 4,
        out_specs=[row_tile(width)] + [resident(1, width)] * 2,
        out_shape=[shape(rows, width, F32)] + [shape(1, width, F32)] * 2,
        micros=15,
        name="input_back",
    )(place, hidden_in, grad_middle, gain, *grads, *weights)


def project_down_kernel(s, middle_ref, bias_ref, *refs):
    hidden, weights, out_ref = refs[:6], refs[6:12], refs[12]
    total = middle_ref[...] + bias_ref[...]
    for h_ref, w_ref in zip(hidden, weights):
        total = total + mm(h_ref[...], w_ref[...])
    out_ref[...] = total.astype(BF16)


def project_down(place, middle, bias, hidden, weights):
    rows, width = middle.shape
    units = hidden[0].shape[1]
    return call(
        project_down_kernel,
        grid=(rows // TILE,),
        in_specs=[row_tile(width), resident(1, width)] + unit_blocks(units, width, 0),
        out_specs=row_tile(width),
        out_shape=shape(rows, width),
        micros=15,
        name="project_down",
    )(place, middle, bias, *unit_arrays(hidden, weights))


def block_bias(rand_blocks):
    blocks = SEQ // BLOCK
    row_ids = jnp.arange(blocks)[None, :]
    col_ids = jnp.arange(blocks)[:, None]
    window = (
        (jnp.abs(row_ids - col_ids) <= 1)
        | (col_ids == 0)
        | (col_ids == blocks - 1)
        | (row_ids == 0)
        | (row_ids == blocks - 1)
    )
    picked = jnp.any(rand_blocks[:, None, :, :] == col_ids[None, :, :, None], axis=3)
    bias = jnp.where(window[None] | picked, 0.0, -1e30).astype(F32)
    return jnp.repeat(bias, BLOCK, axis=2)


def swap(array, axis, bit):
    size = lax.axis_size(axis)
    return lax.ppermute(array, axis, [(place, place ^ bit) for place in range(size)])


def halves_in_order(mine, other, bit, axis=0):
    return jnp.where(
        bit == 0,
        jnp.concatenate([mine, other], axis=axis),
        jnp.concatenate([other, mine], axis=axis),
    )


def add_up(*terms):
    total = terms[0].astype(F32)
    for term in terms[1:]:
        total = total + term.astype(F32)
    return total.astype(terms[0].dtype)


def half_of(array, bit):
    rows = array.shape[-2] // 2
    return lax.dynamic_slice_in_dim(array, bit * rows, rows, array.ndim - 2)


class Sum:
    def __init__(self, order):
        self.plan = ["cores"]
        self.plan += [step if step == "mp" else ("halve", step) for step in order]
        self.plan += [("join", step) for step in reversed(order) if step != "mp"]
        self.plan += ["finish"]
        self.moving = None

    def feed(self, own_a, own_b, far_a, far_b):
        self.parts = own_a, own_b, far_a, far_b

    def issue(self):
        step = self.plan[0]
        if step == "cores":
            self.moving = swap(self.parts[1], "dp", 1), swap(self.parts[3], "dp", 1)
        elif step == "mp":
            self.moving = swap(self.state[1], "mp", 1)
        elif step == "finish":
            self.moving = swap(self.state, "dp", 1)
        elif step[0] == "halve":
            bit = (lax.axis_index("dp") // step[1]) % 2
            self.moving = swap(half_of(self.state, 1 - bit), "dp", step[1])
        else:
            self.moving = swap(self.state, "dp", step[1])

    def collect(self):
        step = self.plan.pop(0)
        if step == "cores":
            own_a, own_b, far_a, far_b = self.parts
            self.state = jnp.stack([add_up(own_a, self.moving[0]), add_up(far_a, self.moving[1])])
        elif step == "mp":
            self.state = add_up(self.state[0], self.moving)
        elif step == "finish":
            self.other = self.moving
        elif step[0] == "halve":
            bit = (lax.axis_index("dp") // step[1]) % 2
            self.state = add_up(half_of(self.state, bit), self.moving)
        else:
            bit = (lax.axis_index("dp") // step[1]) % 2
            self.state = halves_in_order(self.state, self.moving, bit)


def tied(*values):
    return lax.optimization_barrier(values)


def turn(value, *sums):
    for each in sums:
        each.collect()
    kept = tied(value, *[each.state for each in sums])
    for each, state in zip(sums, kept[1:]):
        each.state = state
        if each.plan:
            each.issue()
    return kept[0]


class Small(Sum):
    def __init__(self, state, plan):
        self.state, self.plan = state, list(plan)

    def issue(self):
        self.moving = swap(self.state, *self.plan[0])

    def collect(self):
        self.plan.pop(0)
        self.state = self.state + self.moving


def whole_sequence(
    hidden_in,
    out_grad,
    ln1_gain,
    ln1_bias,
    w_query,
    w_key,
    w_value,
    w_out,
    ln2_gain,
    ln2_bias,
    w_up,
    b_up,
    w_down,
    b_down,
    rand_blocks,
):
    device = lax.axis_index("dp")
    core, over_y, side = device % 2, (device // 2) % 2, lax.axis_index("mp")
    zero = 0 * core
    place = jnp.stack([core, 1 - core, zero, zero, over_y]).astype(jnp.int32)

    def part(array, axis, index, count):
        size = array.shape[axis] // count
        return lax.dynamic_slice_in_dim(array, index * size, size, axis)

    def joined(other):
        return jnp.concatenate(
            [part(each, 1, core ^ other, 2) for each in (w_query, w_key, w_value)], axis=1
        )

    def row(vector):
        return vector.reshape(1, -1)

    own_ja, own_jb = joined(0), joined(1)
    quarter = 2 * core + over_y
    out_piece, up_piece = part(w_out, 0, core, 2), part(w_up, 1, quarter, 4)
    down_piece = part(w_down, 0, quarter, 4)
    far_ja = swap(own_ja, "mp", 1)
    far_rand, far_bup = swap(rand_blocks, "mp", 1), swap(b_up, "mp", 1)
    own_bias, far_bias = block_bias(rand_blocks), block_bias(far_rand)
    bias = [own_bias, own_bias, far_bias, far_bias]
    normed_one, normed_one_t, out_grad_t, bias_down = norm_in(
        place, hidden_in, out_grad, row(ln1_gain), row(ln1_bias)
    )
    qkv, context, row_lse = [None] * 4, [None] * 4, [None] * 4

    def attend(g, normed, weights):
        qkv[g] = mm(normed, weights).astype(BF16)
        context[g], row_lse[g] = attend_forward(place, g, qkv[g], bias[g])

    attend(0, normed_one, own_ja)
    attend(1, tied(normed_one, context[0])[0], own_jb)
    normed, far_ja, out_piece, _ = tied(normed_one, far_ja, out_piece, context[1])
    far_jb, far_out_a = swap(far_ja, "dp", 1), swap(out_piece, "mp", 1)
    attend(2, normed, far_ja)
    normed, far_jb, far_out_a, up_piece, _ = tied(
        normed_one, far_jb, far_out_a, up_piece, context[2]
    )
    far_out_b, up_mine = swap(far_out_a, "dp", 1), swap(up_piece, "mp", 1)
    attend(3, normed, far_jb)
    context[3], far_out_b = tied(context[3], far_out_b)
    joined_w = [own_ja, own_jb, far_ja, far_jb]
    out_w = [w_out, w_out, far_out_a, far_out_b]
    middle, normed_two, normed_two_t = project_out(
        place, hidden_in, context, out_w, row(ln2_gain), row(ln2_bias)
    )

    hidden, grad_up, bias_up, down_g, up_g = ([None] * 4 for _ in range(5))
    up_bias = [row(b_up), row(b_up), row(far_bup), row(far_bup)]

    def feed(g, normed, up, down):
        hidden[g], grad_up[g], bias_up[g] = feed_forward(
            place, g, normed, out_grad, up, up_bias[g], down
        )

    def down_grad(g, left):
        down_g[g] = mm(left, hidden[g]).astype(BF16)

    def up_grad(g, left):
        up_g[g] = mm(left, grad_up[g]).astype(BF16)

    normed, up_mine, down_piece = tied(normed_two, up_mine, down_piece)
    up_other, down_mine = swap(up_mine, "dp", 2), swap(down_piece, "mp", 1)
    feed(0, normed, (w_up,), (w_down,))
    feed(1, tied(normed, grad_up[0])[0], (w_up,), (w_down,))
    left_down, left_up, up_mine, up_other, down_mine, _ = tied(
        out_grad_t, normed_two_t, up_mine, up_other, down_mine, grad_up[1]
    )
    up_far = [swap(up_mine, "dp", 1), swap(up_other, "dp", 1)]
    down_other = swap(down_mine, "dp", 2)
    for g in (1, 0):
        down_grad(g, left_down)
        up_grad(g, left_up)
    normed, down_mine, down_other, *_ = tied(
        normed_two, down_mine, down_other, *up_far, *down_g[:2], *up_g[:2]
    )
    down_far = [swap(down_mine, "dp", 1), swap(down_other, "dp", 1)]
    up_w = [(w_up,), (w_up,), (up_mine, up_other), tuple(up_far)]
    down_w = [(w_down,), (w_down,), (down_mine, down_other), tuple(down_far)]
    feed(2, normed, up_w[2], down_w[2])
    normed, down_fa, down_fb, _ = tied(normed_two, *down_far, grad_up[2])
    down_w[3] = (down_fa, down_fb)
    feed(3, normed, up_w[3], down_w[3])
    left_down, _ = tied(out_grad_t, grad_up[3])
    down_grad(3, left_down)
    down_grad(2, left_down)
    down_sum = Sum(["mp", 2, 4, 8])
    up_sum = Sum([4, "mp", 2, 8])
    first_sum = Sum(["mp", 2, 4, 8])
    second_sum = Sum(["mp", 4, 2, 8])
    *down_g, left_up = tied(*down_g, normed_two_t)
    down_sum.feed(*down_g)
    down_sum.issue()
    up_grad(3, left_up)
    up_grad(2, left_up)
    *up_g, grads_in = tied(*up_g, out_grad)
    up_sum.feed(*up_g)
    up_sum.issue()

    grads_in = turn(grads_in, down_sum)
    grad_middle, grad_attn, grad_attn_t, gain_two, bias_two = middle_back(
        place, grads_in, middle, row(ln2_gain), grad_up, up_w
    )
    grad_attn = turn(grad_attn, up_sum)
    out_g = [mm(grad_attn_t, context[g]).astype(BF16) for g in range(4)]
    out_w[0], out_w[1] = out_piece, part(w_out, 0, 1 - core, 2)
    grad_context = [mm(grad_attn, out_w[g], NT).astype(BF16) for g in range(4)]
    grads, joined_g = [None] * 8, [None] * 8

    def attend_back(g, pair, grad_in):
        grads[2 * g + pair] = attend_backward(
            place, g, pair, qkv[g], grad_in, context[g], row_lse[g], bias[g]
        )

    def joined_grads(pair, groups, left):
        for g in groups:
            joined_g[2 * g + pair] = mm(left, grads[2 * g + pair]).astype(BF16)

    grad_in, *_ = tied(grad_context[3], *grad_context[:3], *out_g)
    attend_back(3, 0, grad_in)
    attend_back(2, 0, tied(grad_context[2], grads[6])[0])
    grad_in = turn(tied(grad_context[1], grads[4])[0], down_sum)
    attend_back(1, 0, grad_in)
    attend_back(0, 0, tied(grad_context[0], grads[2])[0])
    joined_grads(0, (3, 2, 1, 0), tied(normed_one_t, grads[0])[0])
    first_sum.feed(
        *[jnp.concatenate([joined_g[2 * g], out_g[g]], axis=1) for g in range(4)]
    )
    first_sum.parts = tied(*first_sum.parts)
    first_sum.issue()
    grad_in = turn(tied(grad_context[3], *first_sum.parts)[0], up_sum, down_sum)
    attend_back(3, 1, grad_in)
    attend_back(2, 1, tied(grad_context[2], grads[7])[0])
    grad_in = turn(tied(grad_context[1], grads[5])[0], down_sum, first_sum)
    attend_back(1, 1, grad_in)
    grad_in = turn(tied(grad_context[0], grads[3])[0], up_sum, down_sum)
    attend_back(0, 1, grad_in)
    joined_grads(1, (3, 2, 1, 0), tied(normed_one_t, grads[1])[0])
    *parts, grad_in = tied(*joined_g[1::2], grad_middle)
    second_sum.feed(*parts)
    second_sum.issue()
    grad_in = turn(grad_in, up_sum, down_sum)
    input_grad, gain_one, bias_one = input_back(
        place, hidden_in, grad_in, row(ln1_gain), grads, joined_w
    )
    own_up = halves_in_order(bias_up[0], bias_up[1], core, 1)
    far_up = halves_in_order(bias_up[2], bias_up[3], core, 1)
    width = hidden_in.shape[1]
    small = Small(
        jnp.concatenate(
            [gain_one, bias_one, gain_two, bias_two, bias_down]
            + [halves_in_order(own_up, far_up, side, 1).reshape(-1, width)]
        ),
        [("dp", 1), ("mp", 1), ("dp", 2), ("dp", 4), ("dp", 8)],
    )
    total, small.state, _ = tied(middle, small.state, input_grad)
    small.issue()
    total = turn(total, first_sum, second_sum, up_sum, down_sum)
    output = project_down(place, total, row(b_down), hidden, down_w)
    output = turn(output, small, second_sum, first_sum, up_sum, down_sum)
    while second_sum.plan:
        for each in (second_sum, small, first_sum, up_sum, down_sum):
            if each.plan:
                each.collect()
                if each.plan:
                    each.issue()

    def in_order(total, first, last):
        return halves_in_order(
            total.state[:, first:last], total.other[:, first:last], core, 1
        ).astype(F32)

    def both_pairs(part_index):
        columns = slice(part_index * PAIR, (part_index + 1) * PAIR)
        mine = [each.state[:, columns] for each in (first_sum, second_sum)]
        other = [each.other[:, columns] for each in (first_sum, second_sum)]
        ordered = halves_in_order(
            jnp.concatenate(mine, axis=1), jnp.concatenate(other, axis=1), core, 1
        )
        return ordered.astype(F32)

    units = down_g[0].shape[1]
    sums = small.state
    up_rows = b_up.shape[0] // width
    bias_up_sum = lax.dynamic_slice_in_dim(sums, 5 + side * up_rows, up_rows).reshape(-1)
    return (
        output,
        input_grad,
        sums[0],
        sums[1],
        both_pairs(0),
        both_pairs(1),
        both_pairs(2),
        in_order(first_sum, 3 * PAIR, 5 * PAIR).T,
        sums[2],
        sums[3],
        in_order(up_sum, 0, units),
        bias_up_sum,
        in_order(down_sum, 0, units).T,
        sums[4],
    )


def solution(mesh):
    in_specs = (
        P(("dp", "mp"), None),
        P(("dp", "mp"), None),
        P(),
        P(),
        P(None, "mp"),
        P(None, "mp"),
        P(None, "mp"),
        P("mp", None),
        P(),
        P(),
        P(None, "mp"),
        P("mp"),
        P("mp", None),
        P(),
        P("mp", None, None),
    )
    out_specs = (
        P(("dp", "mp"), None),
        P(("dp", "mp"), None),
        P(),
        P(),
        P(None, "mp"),
        P(None, "mp"),
        P(None, "mp"),
        P("mp", None),
        P(),
        P(),
        P(None, "mp"),
        P("mp"),
        P("mp", None),
        P(),
    )
    def per_device(hidden_in, *others):
        w_query, w_up, rand_blocks = others[3], others[9], others[13]
        whole = hidden_in.shape[0] == SEQ and mesh.shape["mp"] == 2
        halved = mesh.shape["dp"] == 16 and rand_blocks.shape[0] == 8
        sized = w_query.shape == (1024, 512) and w_up.shape == (1024, 2048)
        layer = whole_sequence if whole and halved and sized else split_sequence
        return layer(hidden_in, *others)

    return jax.shard_map(
        per_device, mesh=mesh, in_specs=in_specs, out_specs=out_specs, check_vma=False
    )
```

```python
import jax
import jax.numpy as jnp
from jax import lax
from jax.experimental import pallas as pl
from jax.experimental.pallas import tpu as pltpu
from jax.sharding import PartitionSpec as P

HD = 64
BLOCK = 64
SEQ = 1024
PAIR = 2 * HD
BF16 = jnp.bfloat16
F32 = jnp.float32
NT = (((1,), (1,)), ((), ()))
TN = (((0,), (0,)), ((), ()))


def layer_norm(values, norm_gain, norm_bias):
    center = values - jnp.mean(values, axis=-1, keepdims=True)
    spread = jnp.mean(center * center, axis=-1, keepdims=True)
    return center * lax.rsqrt(spread + 1e-05) * norm_gain + norm_bias


def block_mask(rand_blocks):
    blocks = SEQ // BLOCK
    row_ids = jnp.arange(blocks)[:, None]
    col_ids = jnp.arange(blocks)[None, :]
    window = (
        (jnp.abs(row_ids - col_ids) <= 1)
        | (col_ids == 0)
        | (col_ids == blocks - 1)
        | (row_ids == 0)
        | (row_ids == blocks - 1)
    )
    picked = jnp.any(rand_blocks[:, :, :, None] == jnp.arange(blocks)[None, None, None, :], axis=2)
    allowed = window[None] | picked
    return jnp.repeat(jnp.repeat(allowed, BLOCK, axis=1), BLOCK, axis=2)


def attend_forward_split(joined_seq, allowed, scaling):
    queries = joined_seq[:, 0]
    key_rows = joined_seq[:, 1]
    value_rows = joined_seq[:, 2]
    scores = (
        jnp.einsum("qhd,khd->hqk", queries, key_rows, preferred_element_type=jnp.float32) * scaling
    )
    scores = jnp.where(allowed, scores, -1e30)
    highest = jnp.max(scores, axis=-1, keepdims=True)
    shifted = jnp.exp(scores - highest)
    row_totals = jnp.sum(shifted, axis=-1, keepdims=True)
    attn_probs = (shifted / row_totals).astype(jnp.bfloat16)
    context = jnp.einsum("hqk,khd->qhd", attn_probs, value_rows, preferred_element_type=jnp.float32)
    return (context.astype(jnp.bfloat16), (highest + jnp.log(row_totals))[..., 0])


def attend_backward_split(seq_items, allowed, scaling):
    joined_seq, grad_context, row_lse = seq_items
    queries = joined_seq[:, 0]
    key_rows = joined_seq[:, 1]
    value_rows = joined_seq[:, 2]
    scores = (
        jnp.einsum("qhd,khd->hqk", queries, key_rows, preferred_element_type=jnp.float32) * scaling
    )
    scores = jnp.where(allowed, scores, -1e30)
    attn_probs = jnp.exp(scores - row_lse[..., None])
    grad_values = jnp.einsum(
        "hqk,qhd->khd",
        attn_probs.astype(jnp.bfloat16),
        grad_context,
        preferred_element_type=jnp.float32,
    ).astype(jnp.bfloat16)
    grad_probs = jnp.einsum(
        "qhd,khd->hqk", grad_context, value_rows, preferred_element_type=jnp.float32
    )
    row_inner = jnp.sum(grad_probs * attn_probs, axis=-1, keepdims=True)
    grad_scores = (attn_probs * (grad_probs - row_inner)).astype(jnp.bfloat16)
    grad_queries = (
        jnp.einsum("hqk,khd->qhd", grad_scores, key_rows, preferred_element_type=jnp.float32)
        * scaling
    ).astype(jnp.bfloat16)
    grad_keys = (
        jnp.einsum("hqk,qhd->khd", grad_scores, queries, preferred_element_type=jnp.float32)
        * scaling
    ).astype(jnp.bfloat16)
    return jnp.stack([grad_queries, grad_keys, grad_values], axis=1)


def split_sequence(
    hidden_in,
    out_grad,
    ln1_gain,
    ln1_bias,
    w_query,
    w_key,
    w_value,
    w_out,
    ln2_gain,
    ln2_bias,
    w_up,
    b_up,
    w_down,
    b_down,
    rand_blocks,
):
    local_heads = rand_blocks.shape[0]
    head_width = local_heads * HD
    local_rows = hidden_in.shape[0]
    seq_count = local_rows * lax.axis_size("mp") // SEQ
    scaling = HD ** (-0.5)
    allowed = block_mask(rand_blocks)
    inputs = hidden_in.astype(jnp.float32)
    w_joined = jnp.concatenate([w_query, w_key, w_value], axis=1)
    normed_one = layer_norm(inputs, ln1_gain, ln1_bias).astype(jnp.bfloat16)
    rows_one = lax.all_gather(normed_one, "mp", axis=0, tiled=True)
    joined = jnp.dot(rows_one, w_joined, preferred_element_type=jnp.float32).astype(jnp.bfloat16)
    joined_seq = joined.reshape(seq_count, SEQ, 3, local_heads, HD)
    context, row_lse = lax.map(
        lambda seq_block: attend_forward_split(seq_block, allowed, scaling), joined_seq
    )
    context_rows = context.reshape(seq_count * SEQ, head_width)
    middle = inputs + lax.psum_scatter(
        jnp.dot(context_rows, w_out, preferred_element_type=jnp.float32).astype(jnp.bfloat16),
        "mp",
        scatter_dimension=0,
        tiled=True,
    ).astype(jnp.float32)
    normed_two = layer_norm(middle, ln2_gain, ln2_bias).astype(jnp.bfloat16)
    rows_two = lax.all_gather(normed_two, "mp", axis=0, tiled=True)
    up_pre = jnp.dot(rows_two, w_up, preferred_element_type=jnp.float32) + b_up
    hidden = jax.nn.gelu(up_pre, approximate=True).astype(jnp.bfloat16)
    output = (
        middle
        + (
            lax.psum_scatter(
                jnp.dot(hidden, w_down, preferred_element_type=jnp.float32).astype(jnp.bfloat16),
                "mp",
                scatter_dimension=0,
                tiled=True,
            ).astype(jnp.float32)
            + b_down
        )
    ).astype(jnp.bfloat16)
    grad_out = out_grad.astype(jnp.float32)
    bias_down = jnp.sum(grad_out, axis=0)
    rows_ffn = lax.all_gather(out_grad, "mp", axis=0, tiled=True)
    grad_hidden = jnp.einsum("nd,fd->nf", rows_ffn, w_down, preferred_element_type=jnp.float32)
    grad_down = jnp.einsum("nf,nd->fd", hidden, rows_ffn, preferred_element_type=jnp.float32)
    gelu_value, gelu_pull = jax.vjp(lambda pre_act: jax.nn.gelu(pre_act, approximate=True), up_pre)
    grad_up = gelu_pull(grad_hidden)[0].astype(jnp.bfloat16)
    bias_up = jnp.sum(grad_up, axis=0, dtype=jnp.float32)
    grad_up_weight = jnp.einsum("nd,nf->df", rows_two, grad_up, preferred_element_type=jnp.float32)
    grad_normed_two = lax.psum_scatter(
        jnp.einsum("nf,df->nd", grad_up, w_up, preferred_element_type=jnp.float32).astype(
            jnp.bfloat16
        ),
        "mp",
        scatter_dimension=0,
        tiled=True,
    ).astype(jnp.float32)
    norm_value_two, norm_pull_two = jax.vjp(layer_norm, middle, ln2_gain, ln2_bias)
    grad_mid_norm, gain_two, bias_two = norm_pull_two(grad_normed_two)
    grad_middle = grad_out + grad_mid_norm
    grad_attn = grad_middle.astype(jnp.bfloat16)
    rows_attn = lax.all_gather(grad_attn, "mp", axis=0, tiled=True)
    grad_context = jnp.einsum(
        "nd,ed->ne", rows_attn, w_out, preferred_element_type=jnp.float32
    ).astype(jnp.bfloat16)
    grad_out_weight = jnp.einsum(
        "ne,nd->ed", context_rows, rows_attn, preferred_element_type=jnp.float32
    )
    grad_joined = lax.map(
        lambda seq_items: attend_backward_split(seq_items, allowed, scaling),
        (joined_seq, grad_context.reshape(seq_count, SEQ, local_heads, HD), row_lse),
    )
    grad_joined = grad_joined.reshape(seq_count * SEQ, 3 * head_width)
    grad_joined_weight = jnp.einsum(
        "nd,ne->de", rows_one, grad_joined, preferred_element_type=jnp.float32
    )
    grad_normed_one = lax.psum_scatter(
        jnp.einsum("ne,de->nd", grad_joined, w_joined, preferred_element_type=jnp.float32).astype(
            jnp.bfloat16
        ),
        "mp",
        scatter_dimension=0,
        tiled=True,
    ).astype(jnp.float32)
    norm_value_one, norm_pull_one = jax.vjp(layer_norm, inputs, ln1_gain, ln1_bias)
    grad_in_norm, gain_one, bias_one = norm_pull_one(grad_normed_one)
    input_grad = grad_middle + grad_in_norm
    grad_joined_weight, grad_out_weight, grad_up_weight, bias_up, grad_down = (
        lax.psum(grad_joined_weight.astype(jnp.bfloat16), "dp").astype(jnp.float32),
        lax.psum(grad_out_weight.astype(jnp.bfloat16), "dp").astype(jnp.float32),
        lax.psum(grad_up_weight.astype(jnp.bfloat16), "dp").astype(jnp.float32),
        lax.psum(bias_up.astype(jnp.bfloat16), "dp").astype(jnp.float32),
        lax.psum(grad_down.astype(jnp.bfloat16), "dp").astype(jnp.float32),
    )
    gain_one, bias_one, gain_two, bias_two, bias_down = lax.psum(
        (gain_one, bias_one, gain_two, bias_two, bias_down), ("dp", "mp")
    )
    grad_query = grad_joined_weight[:, :head_width]
    grad_key = grad_joined_weight[:, head_width : 2 * head_width]
    grad_value = grad_joined_weight[:, 2 * head_width :]
    return (
        output,
        input_grad,
        gain_one,
        bias_one,
        grad_query,
        grad_key,
        grad_value,
        grad_out_weight,
        gain_two,
        bias_two,
        grad_up_weight,
        bias_up,
        grad_down,
        bias_down,
    )


VMEM_LIMIT = 56 << 20
TILE = 256
SPAN = 512
WIDE = 512
PACE = 0.02


def mm(left, right, dims=(((1,), (0,)), ((), ()))):
    return lax.dot_general(left, right, dims, preferred_element_type=F32)


def call(body, *, grid, in_specs, out_specs, out_shape, micros, name, scratch=(), scalars=1):
    return pl.pallas_call(
        body,
        grid_spec=pltpu.PrefetchScalarGridSpec(
            num_scalar_prefetch=scalars,
            grid=grid,
            in_specs=in_specs,
            out_specs=out_specs,
            scratch_shapes=list(scratch),
        ),
        out_shape=out_shape,
        compiler_params=pltpu.CompilerParams(vmem_limit_bytes=VMEM_LIMIT),
        cost_estimate=pl.CostEstimate(
            flops=int(micros * PACE * 1e9), bytes_accessed=0, transcendentals=0
        ),
        name=name,
    )


def shape(rows, columns, dtype=BF16):
    return jax.ShapeDtypeStruct((rows, columns), dtype)


def row_tile(width, dtype=None):
    return pl.BlockSpec((TILE, width), lambda i, s: (i, 0))


def column_tile(height):
    return pl.BlockSpec((height, TILE), lambda i, s: (0, i))


def resident(rows, columns):
    return pl.BlockSpec((rows, columns), lambda i, s: (0, 0))


def norm_parts(values):
    center = values - jnp.mean(values, axis=-1, keepdims=True)
    spread = jnp.mean(center * center, axis=-1, keepdims=True)
    return center, lax.rsqrt(spread + 1e-05)


def norm_backward(values, gain, grads):
    center, scale = norm_parts(values)
    unit = center * scale
    scaled = grads * gain
    mean_g = jnp.mean(scaled, axis=-1, keepdims=True)
    mean_gu = jnp.mean(scaled * unit, axis=-1, keepdims=True)
    grad_in = scale * (scaled - mean_g - unit * mean_gu)
    return (
        grad_in,
        jnp.sum(grads * unit, axis=0, keepdims=True),
        jnp.sum(grads, axis=0, keepdims=True),
    )


def flipped(rows):
    return rows.astype(F32).T.astype(BF16)


def accumulate(ref, value):
    @pl.when(pl.program_id(0) == 0)
    def _():
        ref[...] = value

    @pl.when(pl.program_id(0) > 0)
    def _():
        ref[...] += value


def norm_in_kernel(s, x_ref, g_ref, gain_ref, bias_ref, n_ref, sum_ref):
    center, scale = norm_parts(x_ref[...].astype(F32))
    n_ref[...] = (center * scale * gain_ref[...] + bias_ref[...]).astype(BF16)
    accumulate(sum_ref, jnp.sum(g_ref[...].astype(F32), axis=0, keepdims=True))


def norm_in(place, hidden_in, out_grad, gain, bias):
    rows, width = hidden_in.shape
    return call(
        norm_in_kernel,
        grid=(rows // TILE,),
        in_specs=[row_tile(width), row_tile(width), resident(1, width), resident(1, width)],
        out_specs=[row_tile(width), resident(1, width)],
        out_shape=[shape(rows, width), shape(1, width, F32)],
        micros=5,
        name="norm_in",
    )(place, hidden_in, out_grad, gain, bias)


def head_lanes(rows, head):
    lanes = lax.broadcasted_iota(jnp.int32, rows.shape, 1)
    return jnp.where(lanes // HD == head, rows, jnp.zeros_like(rows))


def spread_bias(bias, dims):
    blocks = bias.shape[0]
    tokens = lax.broadcasted_iota(jnp.int32, (blocks, blocks * BLOCK), 1) // BLOCK
    which = lax.broadcasted_iota(jnp.int32, tokens.shape, 0)
    return mm(bias, jnp.where(tokens == which, 1.0, 0.0).astype(BF16), dims)


def add_blocks(scores, bias):
    rows, width = scores.shape
    return (scores.reshape(rows // BLOCK, BLOCK, width) + bias[:, None, :]).reshape(rows, width)


def attend_forward_kernel(s, q_ref, k_ref, v_ref, bias_ref, context_ref, lse_ref):
    scaling = HD ** (-0.5)
    bias = [spread_bias(bias_ref[head], (((1,), (0,)), ((), ()))) for head in range(2)]
    jobs = [(start, head) for start in range(0, q_ref.shape[0], SPAN) for head in range(2)]

    def score(job):
        start, head = job
        queries = q_ref[start : start + SPAN, :] * jnp.asarray(scaling, BF16)
        return mm(head_lanes(queries, head), k_ref[...], NT)

    ahead = score(jobs[0])
    parts = []
    for index, (start, head) in enumerate(jobs):
        rows = slice(start, start + SPAN)
        scores = ahead
        if index + 1 < len(jobs):
            ahead = score(jobs[index + 1])
        scores = add_blocks(scores, bias[head][start // BLOCK : (start + SPAN) // BLOCK])
        highest = jnp.max(scores, axis=1, keepdims=True)
        shifted = jnp.exp(scores - highest)
        totals = jnp.sum(shifted, axis=1, keepdims=True)
        parts.append(mm(shifted.astype(BF16), v_ref[...]) / totals)
        lse_ref[0, head : head + 1, rows] = (highest + jnp.log(totals)).T
        if head == 1:
            lanes = lax.broadcasted_iota(jnp.int32, parts[0].shape, 1)
            context_ref[rows, :] = jnp.where(lanes < HD, parts[0], parts[1]).astype(BF16)
            parts = []


def thin_block(column):
    return pl.BlockSpec((SEQ, PAIR), lambda p, s: (0, column(p)))


def attend_forward(place, which, qkv, bias):
    pairs = 2
    blocks = SEQ // BLOCK
    return call(
        attend_forward_kernel,
        grid=(pairs,),
        in_specs=[
            thin_block(lambda p: p),
            thin_block(lambda p: pairs + p),
            thin_block(lambda p: 2 * pairs + p),
            pl.BlockSpec((2, blocks, blocks), lambda p, s: (s[which % 2] * pairs + p, 0, 0)),
        ],
        out_specs=[thin_block(lambda p: p), pl.BlockSpec((1, 2, SEQ), lambda p, s: (p, 0, 0))],
        out_shape=[shape(SEQ, pairs * PAIR), jax.ShapeDtypeStruct((pairs, 2, SEQ), F32)],
        micros=12,
        name="attend_forward",
    )(place, qkv, qkv, qkv, bias)


def attend_backward_kernel(
    outs,
    s,
    q_ref,
    k_ref,
    v_ref,
    grad_ref,
    context_ref,
    lse_ref,
    bias_ref,
    n_hbm,
    ga_hbm,
    *refs,
):
    *extras, out_ref, w_ref, key_acc, value_acc, flat_ref, n_ref, ga_ref, more_ref, sem = refs
    copies = [pltpu.make_async_copy(n_hbm, n_ref, sem.at[0])]
    if outs:
        all_contexts_ref = extras.pop(0)
        copies.append(pltpu.make_async_copy(ga_hbm, ga_ref, sem.at[1]))
    if extras:
        copies.append(pltpu.make_async_copy(extras[0], more_ref, sem.at[2]))
    for copy in copies:
        copy.start()
    scaling = HD ** (-0.5)
    key_rows = k_ref[...]
    value_rows = v_ref[...]
    keys_t = flipped(key_rows)
    bias = [spread_bias(bias_ref[head], TN) for head in range(2)]
    for start in range(0, q_ref.shape[0], SPAN):
        rows = slice(start, start + SPAN)
        queries = q_ref[rows, :] * jnp.asarray(scaling, BF16)
        grads = grad_ref[rows, :]
        inner_t = (grads.astype(F32) * context_ref[rows, :].astype(F32)).T
        probs, slopes, masked_q, masked_g, parts = [], [], [], [], []
        for head in range(2):
            query_h, grad_h = head_lanes(queries, head), head_lanes(grads, head)
            scores = add_blocks(mm(key_rows, query_h, NT), bias[head][:, rows])
            attn = jnp.exp(scores - lse_ref[0, head : head + 1, rows])
            inner = jnp.sum(inner_t[head * HD : (head + 1) * HD], axis=0, keepdims=True)
            slope = (attn * (mm(value_rows, grad_h, NT) - inner)).astype(BF16)
            parts.append(mm(keys_t[head * HD : (head + 1) * HD], slope) * scaling)
            probs.append(attn.astype(BF16))
            slopes.append(slope)
            masked_q.append(query_h)
            masked_g.append(grad_h)
        grad_q = jnp.concatenate(parts, axis=0)
        flat_ref[:PAIR, rows] = grad_q.astype(BF16)
        out_ref[rows, :PAIR] = grad_q.T.astype(BF16)
        grad_k = mm(jnp.concatenate(slopes, axis=1), jnp.concatenate(masked_q, axis=0))
        grad_v = mm(jnp.concatenate(probs, axis=1), jnp.concatenate(masked_g, axis=0))
        if start == 0:
            key_acc[...] = grad_k
            value_acc[...] = grad_v
        else:
            key_acc[...] += grad_k
            value_acc[...] += grad_v
    for part, acc in ((1, key_acc), (2, value_acc)):
        columns = slice(part * PAIR, (part + 1) * PAIR)
        total = acc[...]
        out_ref[:, columns] = total.astype(BF16)
        flat_ref[columns, :] = total.T.astype(BF16)
    for copy in copies:
        copy.wait()

    def give(lines, product):
        if extras:
            product = product + more_ref[lines, :].astype(F32)
        w_ref[lines, :] = product.astype(BF16)

    for part in range(3):
        lines = slice(part * PAIR, (part + 1) * PAIR)
        give(lines, mm(flat_ref[lines, :], n_ref[...]))
    if outs:
        give(slice(3 * PAIR, w_ref.shape[0]), mm(flipped(all_contexts_ref[...]), ga_ref[...]))


def attend_backward(
    place, which, pair, qkv, grad_context, context, row_lse, bias, normed, grad, more=None
):
    pairs = 2
    blocks = SEQ // BLOCK
    width = normed.shape[1]
    lines = 3 * PAIR + (context.shape[1] if pair == 0 else 0)
    outs = pair == 0
    return call(
        lambda *refs: attend_backward_kernel(outs, *refs),
        grid=(1,),
        in_specs=[
            thin_block(lambda p: pair),
            thin_block(lambda p: pairs + pair),
            thin_block(lambda p: 2 * pairs + pair),
            thin_block(lambda p: pair),
            thin_block(lambda p: pair),
            pl.BlockSpec((1, 2, SEQ), lambda p, s: (pair, 0, 0)),
            pl.BlockSpec((2, blocks, blocks), lambda p, s: (s[which % 2] * pairs + pair, 0, 0)),
            pl.BlockSpec(memory_space=pl.ANY),
            pl.BlockSpec(memory_space=pl.ANY),
        ]
        + [resident(*context.shape)] * outs
        + [pl.BlockSpec(memory_space=pl.ANY)] * (more is not None),
        out_specs=[resident(SEQ, 3 * PAIR), resident(lines, width)],
        out_shape=[shape(SEQ, 3 * PAIR), shape(lines, width)],
        scratch=[
            pltpu.VMEM((SEQ, PAIR), F32),
            pltpu.VMEM((SEQ, PAIR), F32),
            pltpu.VMEM((3 * PAIR, SEQ), BF16),
            pltpu.VMEM(normed.shape, BF16),
            pltpu.VMEM(grad.shape if outs else (16, PAIR), BF16),
            pltpu.VMEM((lines, width) if more is not None else (16, PAIR), BF16),
            pltpu.SemaphoreType.DMA((3,)),
        ],
        micros=10,
        name="attend_backward",
    )(
        place,
        qkv,
        qkv,
        qkv,
        grad_context,
        context,
        row_lse,
        bias,
        normed,
        grad,
        *[context] * outs,
        *[more] * (more is not None),
    )


def project_out_kernel(s, x_ref, *refs):
    contexts, weights = refs[:4], refs[4:8]
    gain_ref, bias_ref, middle_ref, n_ref = refs[8:]
    middle = x_ref[...].astype(F32)
    for context_ref, w_ref in zip(contexts, weights):
        middle = middle + mm(context_ref[...], w_ref[...])
    middle_ref[...] = middle
    center, scale = norm_parts(middle)
    n_ref[...] = (center * scale * gain_ref[...] + bias_ref[...]).astype(BF16)


def own_then_far(block, along):
    specs = []
    for which in range(4):
        if along == 0:
            specs.append(pl.BlockSpec(block, lambda i, s, which=which: (s[which], 0)))
        else:
            specs.append(pl.BlockSpec(block, lambda i, s, which=which: (0, s[which])))
    return specs


def project_out(place, hidden_in, contexts, weights, gain, bias):
    rows, width = hidden_in.shape
    return call(
        project_out_kernel,
        grid=(rows // TILE,),
        in_specs=[row_tile(width)]
        + [row_tile(2 * PAIR)] * 4
        + own_then_far((2 * PAIR, width), 0)
        + [resident(1, width)] * 2,
        out_specs=[row_tile(width), row_tile(width)],
        out_shape=[shape(rows, width, F32), shape(rows, width)],
        micros=7,
        name="project_out",
    )(place, hidden_in, *contexts, *weights, gain, bias)


def gelu_and_slope(pre):
    root, cubic = 0.7978845608028654, 0.044715
    square = pre * pre
    bent = jnp.tanh(root * (pre + cubic * pre * square))
    half = 0.5 * pre
    slope = 0.5 * (1.0 + bent) + half * (1.0 - bent * bent) * (root * (1.0 + 3.0 * cubic * square))
    return half + half * bent, slope


def feed_forward_kernel(tiles, s, n_ref, g_ref, bias_ref, *refs):
    *ups, down_ref, h_ref, gu_ref, sum_ref = refs

    def run(up_ref):
        pre = mm(n_ref[...], up_ref[...]) + bias_ref[...]
        grad_hidden = mm(g_ref[...], down_ref[...], NT)
        value, slope = gelu_and_slope(pre)
        h_ref[...] = value.astype(BF16)
        grad_up = (grad_hidden * slope).astype(BF16)
        gu_ref[...] = grad_up
        sum_ref[...] = jnp.sum(grad_up.astype(F32), axis=0, keepdims=True)

    if len(ups) == 1:
        run(ups[0])
    else:
        mine = pl.program_id(0) // (tiles // 2) == s[4]

        @pl.when(mine)
        def _():
            run(ups[0])

        @pl.when(jnp.logical_not(mine))
        def _():
            run(ups[1])


def wide_tile(height):
    return pl.BlockSpec((height, WIDE), lambda i, s: (0, i))


def feed_forward(place, which, normed, out_grad, w_up, b_up, w_down):
    rows, width = normed.shape
    units = b_up.shape[1] // 2
    tiles = units // WIDE
    if which < 2:
        columns = [lambda i, s: (0, s[which] * tiles + i)]
    else:
        columns = [lambda i, s: (0, i % (tiles // 2))] * 2
    return call(
        lambda *refs: feed_forward_kernel(tiles, *refs),
        grid=(tiles,),
        in_specs=[
            resident(rows, width),
            resident(rows, width),
            pl.BlockSpec((1, WIDE), lambda i, s: (0, s[which % 2] * tiles + i)),
        ]
        + [pl.BlockSpec((width, WIDE), column) for column in columns]
        + [pl.BlockSpec((WIDE, width), lambda i, s: (s[which] * tiles + i, 0))],
        out_specs=[wide_tile(rows), wide_tile(rows), wide_tile(1)],
        out_shape=[shape(rows, units), shape(rows, units), shape(1, units, F32)],
        micros=12,
        name="feed_forward",
    )(place, normed, out_grad, b_up, *w_up, w_down)


def unit_blocks(units, width, halved, along):
    half = units // 2
    rows = [pl.BlockSpec((TILE, units), lambda i, s: (i, 0))] * 2
    if halved:
        rows += [
            pl.BlockSpec((TILE, half), lambda i, s: (i, s[4])),
            pl.BlockSpec((TILE, half), lambda i, s: (i, 1 - s[4])),
        ] * 2
    else:
        rows += rows
    far = half if halved else units
    count = 4 if halved else 2
    if along == 0:
        own = [
            pl.BlockSpec((units, width), lambda i, s, which=which: (s[which], 0)) for which in (0, 1)
        ]
        return rows + own + [resident(far, width)] * count
    own = [pl.BlockSpec((width, units), lambda i, s, which=which: (0, s[which])) for which in (0, 1)]
    return rows + own + [resident(width, far)] * count


def unit_arrays(slices, weights):
    arrays = [each for each, group in zip(slices, weights) for _ in group]
    return arrays + [part for group in weights for part in group]


def middle_back_kernel(s, g_ref, middle_ref, gain_ref, *refs):
    grads, weights, outs = refs[:6], refs[6:12], refs[12:16]
    gm_ref, ga_ref, gain_sum, bias_sum, *context_grads = refs[16:]
    total = mm(grads[0][...], weights[0][...], NT)
    for grad_ref, w_ref in zip(grads[1:], weights[1:]):
        total = total + mm(grad_ref[...], w_ref[...], NT)
    grad_in, gain, bias = norm_backward(middle_ref[...], gain_ref[...], total)
    grad_middle = g_ref[...].astype(F32) + grad_in
    gm_ref[...] = grad_middle
    ga_ref[...] = grad_middle.astype(BF16)
    accumulate(gain_sum, gain)
    accumulate(bias_sum, bias)
    for w_ref, out_ref in zip(outs, context_grads):
        out_ref[...] = mm(ga_ref[...], w_ref[...], NT).astype(BF16)


def middle_back(place, out_grad, middle, gain, grad_up, weights, out_weights):
    rows, width = middle.shape
    units = grad_up[0].shape[1]
    return call(
        middle_back_kernel,
        grid=(rows // TILE,),
        in_specs=[row_tile(width), row_tile(width), resident(1, width)]
        + unit_blocks(units, width, True, 1)
        + own_then_far((2 * PAIR, width), 0),
        out_specs=[row_tile(width), row_tile(width)]
        + [resident(1, width)] * 2
        + [row_tile(2 * PAIR)] * 4,
        out_shape=[shape(rows, width, F32), shape(rows, width)]
        + [shape(1, width, F32)] * 2
        + [shape(rows, 2 * PAIR)] * 4,
        micros=18,
        name="middle_back",
    )(place, out_grad, middle, gain, *unit_arrays(grad_up, weights), *out_weights)


def input_back_kernel(s, x_ref, gm_ref, gain_ref, *refs):
    grads, weights = refs[:8], refs[8:12]
    out_ref, gain_sum, bias_sum = refs[12:]
    total = None
    for group in range(4):
        pair_0, pair_1 = grads[2 * group][...], grads[2 * group + 1][...]
        joined = jnp.concatenate(
            [
                pair[:, part * PAIR : (part + 1) * PAIR]
                for part in range(3)
                for pair in (pair_0, pair_1)
            ],
            axis=1,
        )
        product = mm(joined, weights[group][...], NT)
        total = product if total is None else total + product
    grad_in, gain, bias = norm_backward(x_ref[...].astype(F32), gain_ref[...], total)
    out_ref[...] = gm_ref[...] + grad_in
    accumulate(gain_sum, gain)
    accumulate(bias_sum, bias)


def input_back(place, hidden_in, grad_middle, gain, grads, weights):
    rows, width = hidden_in.shape
    return call(
        input_back_kernel,
        grid=(rows // TILE,),
        in_specs=[row_tile(width), row_tile(width), resident(1, width)]
        + [row_tile(3 * PAIR)] * 8
        + [resident(width, 6 * PAIR)] * 4,
        out_specs=[row_tile(width)] + [resident(1, width)] * 2,
        out_shape=[shape(rows, width, F32)] + [shape(1, width, F32)] * 2,
        micros=15,
        name="input_back",
    )(place, hidden_in, grad_middle, gain, *grads, *weights)


def project_down_kernel(s, middle_ref, bias_ref, *refs):
    hidden, weights, out_ref = refs[:4], refs[4:8], refs[8]
    total = middle_ref[...] + bias_ref[...]
    for h_ref, w_ref in zip(hidden, weights):
        total = total + mm(h_ref[...], w_ref[...])
    out_ref[...] = total.astype(BF16)


def project_down(place, middle, bias, hidden, weights):
    rows, width = middle.shape
    units = hidden[0].shape[1]
    return call(
        project_down_kernel,
        grid=(rows // TILE,),
        in_specs=[row_tile(width), resident(1, width)] + unit_blocks(units, width, False, 0),
        out_specs=row_tile(width),
        out_shape=shape(rows, width),
        micros=15,
        name="project_down",
    )(place, middle, bias, *unit_arrays(hidden, weights))


def block_bias(rand_blocks):
    blocks = SEQ // BLOCK
    row_ids = jnp.arange(blocks)[:, None]
    col_ids = jnp.arange(blocks)[None, :]
    window = (
        (jnp.abs(row_ids - col_ids) <= 1)
        | (col_ids == 0)
        | (col_ids == blocks - 1)
        | (row_ids == 0)
        | (row_ids == blocks - 1)
    )
    picked = jnp.any(rand_blocks[:, :, :, None] == col_ids[None, :, None, :], axis=2)
    return jnp.where(window[None] | picked, 0.0, -1e30).astype(BF16)


def swap(array, axis, bit):
    size = lax.axis_size(axis)
    return lax.ppermute(array, axis, [(place, place ^ bit) for place in range(size)])


def add_up(*terms):
    total = terms[0].astype(F32)
    for term in terms[1:]:
        total = total + term.astype(F32)
    return total.astype(terms[0].dtype)


def tied(*values):
    return lax.optimization_barrier(values)


class Sum:
    def __init__(self, steps):
        self.steps = list(steps)
        self.paired = self.steps[0] != "mp"
        self.state, self.sending, self.moving = None, [], []

    def parts_of(self, terms):
        if not self.steps:
            self.state, self.sending = add_up(*terms), []
        elif self.steps[0] == "mp":
            near, far = zip(*terms)
            self.state, self.sending = add_up(*near), [add_up(*far)]
        else:
            bits = self.steps[0]
            partners = [0]
            for bit in bits:
                partners += [bit | other for other in partners]
            self.partners = partners[1:]
            rows = terms[0][0].shape[0] if isinstance(terms[0], tuple) else terms[0].shape[0]
            rows //= len(partners)
            index = lax.axis_index("dp") // bits[0] % len(partners)

            def cut(term, other):
                start = (index ^ (other // bits[0])) * rows
                return lax.dynamic_slice_in_dim(term, start, rows, 0)

            def summed(other):
                if isinstance(terms[0], tuple):
                    return jnp.concatenate(
                        [add_up(*[cut(term, other) for term in half]) for half in zip(*terms)]
                    )
                return add_up(*[cut(term, other) for term in terms])

            self.state = summed(0)
            self.sending = [summed(other) for other in self.partners]

    def go(self):
        step = self.steps.pop(0)
        if step == "mp":
            self.moving = [swap(part, "mp", 1) for part in self.sending]
        else:
            self.moving = [swap(part, "dp", way) for part, way in zip(self.sending, self.partners)]

    def take(self):
        terms = [self.state] + self.moving
        if self.paired and self.steps[0] == "mp":
            self.paired = False
            rows = terms[0].shape[0] // 2
            terms = [(term[:rows], term[rows:]) for term in terms]
        self.parts_of(terms)


class Tied(dict):
    def tie(self, *names):
        for name, value in zip(names, tied(*[self[name] for name in names])):
            self[name] = value
        return self[names[0]]

    def turn(self, *names, sums=()):
        counts = [len(each.moving) for each in sums]
        flat = [part for each in sums for part in each.moving]
        kept = list(tied(*[self[name] for name in names], *flat))
        for name in names:
            self[name] = kept.pop(0)
        for each, count in zip(sums, counts):
            each.moving = [kept.pop(0) for _ in range(count)]
            if count:
                each.take()
        flat = [self[name] for name in names]
        for each in sums:
            flat += [each.state] + each.sending
        kept = list(tied(*flat))
        for name in names:
            self[name] = kept.pop(0)
        for each in sums:
            each.state = kept.pop(0)
            each.sending = [kept.pop(0) for _ in each.sending]
            each.moving = []
            if each.steps:
                each.go()


class Gather:
    def __init__(self, state, steps):
        self.state, self.steps, self.sending, self.moving = state, list(steps), [], []

    def go(self):
        bits = self.steps.pop(0)
        partners = [0]
        for bit in bits:
            partners += [bit | other for other in partners]
        self.moving = [swap(self.state, "dp", way) for way in partners[1:]]

    def take(self):
        self.state = jnp.concatenate([self.state] + self.moving)


class Butterfly:
    def __init__(self, state, steps):
        self.state, self.steps, self.sending, self.moving = state, list(steps), [], []

    def go(self):
        self.moving = [swap(self.state, *self.steps.pop(0))]

    def take(self):
        self.state = self.state + self.moving[0]


def spread_kernel(s, *refs):
    *parts, out_ref = refs
    height = parts[0].shape[0]
    for index, part in enumerate(parts):
        out_ref[index * height : (index + 1) * height, :] = part[...].astype(F32)


def spread(place, gathered, sources, target, rows, columns):
    width = gathered.shape[1]
    height = rows * columns // width // 4 // len(sources)
    return call(
        spread_kernel,
        grid=(2, 2),
        in_specs=[
            pl.BlockSpec((height, width), lambda c, y, s, source=source: (source(c, y), 0))
            for source in sources
        ],
        out_specs=pl.BlockSpec((height * len(sources), width), lambda c, y, s: target(c, y)),
        out_shape=shape(rows, columns, F32),
        micros=4,
        name="spread",
    )(place, *[gathered] * len(sources))


def spread_joined_kernel(s, one_a, one_b, two_a, two_b, q_ref, k_ref, v_ref, o_ref, flat):
    mine = pl.program_id(0) == s[0]
    first = 0
    for part_a, part_b in ((one_a, one_b), (two_a, two_b)):
        height = part_a.shape[0] // 8
        for y in range(2):
            for z in range(4):
                start = first + (y * 4 + z) * height
                source = ((y ^ s[4]) * 4 + (z ^ s[5])) * height
                lines = pl.ds(pl.multiple_of(source, height), height)
                flat[start : start + height, :] = jnp.where(mine, part_a[lines, :], part_b[lines, :])
        first += 8 * height
    second = one_a.shape[0]
    for part, ref in enumerate((q_ref, k_ref, v_ref)):
        for pair, first in enumerate((0, second)):
            lines = slice(first + part * PAIR, first + (part + 1) * PAIR)
            ref[:, pair * PAIR : (pair + 1) * PAIR] = flat[lines, :].astype(F32).T
    o_ref[...] = flat[3 * PAIR : second, :].astype(F32)


def spread_joined(place, one, two):
    width = one[0].shape[1]
    columns = pl.BlockSpec((width, 2 * PAIR), lambda c, s: (0, c))
    return call(
        spread_joined_kernel,
        grid=(2,),
        in_specs=[resident(*each.shape) for each in (*one, *two)],
        out_specs=[columns] * 3 + [pl.BlockSpec((2 * PAIR, width), lambda c, s: (c, 0))],
        out_shape=[shape(width, 4 * PAIR, F32)] * 3 + [shape(4 * PAIR, width, F32)],
        scratch=[pltpu.VMEM((one[0].shape[0] + two[0].shape[0], width), BF16)],
        micros=4,
        name="spread_joined",
    )(place, *one, *two)


class At:
    (
        out_piece, up_piece, down_piece, far_ja, n1, qkv, ctx, far_jb,
        far_out_a, far_out_b, up_mine, down_a, middle, n2, g, gu,
        down, up, up_other, up_b0, up_b1, down_b, near_down, near_up,
        far_down, far_up, gm, ga, gc, gj, joined, far_b,
        own_b, down_all, up_all, input_grad, output, grad_down_w, grad_up_w, first,
    ) = range(40)


def whole_sequence(
    hidden_in,
    out_grad,
    ln1_gain,
    ln1_bias,
    w_query,
    w_key,
    w_value,
    w_out,
    ln2_gain,
    ln2_bias,
    w_up,
    b_up,
    w_down,
    b_down,
    rand_blocks,
):
    device = lax.axis_index("dp")
    core, over_y, side = device % 2, (device // 2) % 2, lax.axis_index("mp")
    zero = 0 * core
    place = jnp.stack([core, 1 - core, zero, zero, over_y, device // 4]).astype(jnp.int32)

    def part(array, axis, index, count):
        size = array.shape[axis] // count
        return lax.dynamic_slice_in_dim(array, index * size, size, axis)

    def joined(other):
        return jnp.concatenate(
            [part(each, 1, core ^ other, 2) for each in (w_query, w_key, w_value)], axis=1
        )

    def halves_in_order(mine, other, bit):
        return jnp.where(
            bit == 0,
            jnp.concatenate([mine, other], axis=1),
            jnp.concatenate([other, mine], axis=1),
        )

    def row(vector):
        return vector.reshape(1, -1)

    v = Tied()
    own_ja, own_jb = joined(0), joined(1)
    quarter = 2 * core + over_y
    v[At.out_piece], v[At.up_piece] = part(w_out, 0, core, 2), part(w_up, 1, quarter, 4)
    v[At.down_piece] = part(w_down, 0, core, 2)
    v[At.far_ja] = swap(own_ja, "mp", 1)
    far_rand, far_bup = swap(rand_blocks, "mp", 1), swap(b_up, "mp", 1)
    own_bias, far_bias = block_bias(rand_blocks), block_bias(far_rand)
    bias = [own_bias, own_bias, far_bias, far_bias]
    v[At.n1], bias_down = norm_in(place, hidden_in, out_grad, row(ln1_gain), row(ln1_bias))
    row_lse = [None] * 4

    def attend(g, weights):
        v[At.qkv, g] = mm(v[At.n1], weights).astype(BF16)
        v[At.ctx, g], row_lse[g] = attend_forward(place, g, v[At.qkv, g], bias[g])

    attend(0, own_ja)
    v.tie(At.n1, (At.ctx, 0))
    attend(1, own_jb)
    v.tie(At.n1, At.far_ja, At.out_piece, (At.ctx, 1))
    v[At.far_jb], v[At.far_out_a] = swap(v[At.far_ja], "dp", 1), swap(v[At.out_piece], "mp", 1)
    attend(2, v[At.far_ja])
    v.tie(At.n1, At.far_jb, At.far_out_a, At.up_piece, (At.ctx, 2))
    v[At.far_out_b], v[At.up_mine] = swap(v[At.far_out_a], "dp", 1), swap(v[At.up_piece], "mp", 1)
    attend(3, v[At.far_jb])
    v.tie((At.ctx, 3), At.far_out_b, At.down_piece)
    v[At.down_a] = swap(v[At.down_piece], "mp", 1)
    joined_w = [own_ja, own_jb, v[At.far_ja], v[At.far_jb]]
    out_w = [w_out, w_out, v[At.far_out_a], v[At.far_out_b]]
    v[At.middle], v[At.n2] = project_out(
        place, hidden_in, [v[At.ctx, g] for g in range(4)], out_w, row(ln2_gain), row(ln2_bias)
    )

    hidden, bias_up = [None] * 4, [None] * 4
    up_bias = [row(b_up), row(b_up), row(far_bup), row(far_bup)]
    v[At.g] = out_grad

    def feed(g, up, down):
        hidden[g], v[At.gu, g], bias_up[g] = feed_forward(
            place, g, v[At.n2], v[At.g], up, up_bias[g], down
        )

    def down_grad(g):
        v[At.down, g] = mm(hidden[g], v[At.g], TN).astype(BF16)

    def up_grad(g):
        v[At.up, g] = mm(v[At.n2], v[At.gu, g], TN).astype(BF16)

    v.tie(At.n2, At.up_mine)
    v[At.up_other] = swap(v[At.up_mine], "dp", 2)
    feed(1, (w_up,), w_down)
    v.tie(At.n2, (At.gu, 1))
    feed(0, (w_up,), w_down)
    v.tie(At.g, At.n2, At.up_mine, At.up_other, (At.gu, 0))
    v[At.up_b0], v[At.up_b1] = swap(v[At.up_mine], "dp", 1), swap(v[At.up_other], "dp", 1)
    for g in (1, 0):
        down_grad(g)
        up_grad(g)
    v.tie(At.n2, At.g, At.down_a, At.up_b0, At.up_b1, *[(name, g) for name in (At.down, At.up) for g in (0, 1)])
    v[At.down_b] = swap(v[At.down_a], "dp", 1)
    v[At.near_down], v[At.near_up] = swap(v[At.down, 1], "dp", 1), swap(v[At.up, 1], "dp", 1)
    feed(2, (v[At.up_mine], v[At.up_other]), v[At.down_a])
    v.tie(At.n2, At.g, At.down_b, At.near_down, At.near_up, (At.gu, 2))
    feed(3, (v[At.up_b0], v[At.up_b1]), v[At.down_b])
    up_w = [(w_up,), (w_up,), (v[At.up_mine], v[At.up_other]), (v[At.up_b0], v[At.up_b1])]
    down_w = [(w_down,), (w_down,), (v[At.down_a],), (v[At.down_b],)]
    v.tie(At.g, At.n2, (At.gu, 3))
    down_grad(3)
    v.tie(At.g, At.n2, (At.down, 3))
    v[At.far_down] = swap(v[At.down, 3], "dp", 1)
    up_grad(3)
    v.tie(At.g, At.n2, (At.up, 3))
    v[At.far_up] = swap(v[At.up, 3], "dp", 1)
    down_grad(2)
    down_sum = Sum(["mp", (2,), (4,), (8,)])
    down_sum.parts_of([(v[At.down, 0], v[At.down, 2]), (v[At.near_down], v[At.far_down])])
    v.turn(At.g, At.n2, sums=[down_sum])
    up_grad(2)
    up_sum = Sum([(4,), "mp", (2,), (8,)])
    up_sum.parts_of([(v[At.up, 0], v[At.up, 2]), (v[At.near_up], v[At.far_up])])
    v.turn(At.g, sums=[up_sum])

    v[At.gm], v[At.ga], gain_two, bias_two, *context_grads = middle_back(
        place,
        v[At.g],
        v[At.middle],
        row(ln2_gain),
        [v[At.gu, g] for g in range(4)],
        up_w,
        [w_out, w_out, v[At.far_out_a], v[At.far_out_b]],
    )
    for g in range(4):
        v[At.gc, g] = context_grads[g]
    v.tie(At.ga, *[(At.gc, g) for g in range(4)])

    def attend_back(g, pair, more=None):
        v[At.gj, g, pair], v[At.joined, g, pair] = attend_backward(
            place,
            g,
            pair,
            v[At.qkv, g],
            v[At.gc, g],
            v[At.ctx, g],
            row_lse[g],
            bias[g],
            v[At.n1],
            v[At.ga],
            more,
        )

    first, second = Sum(["mp", (2,), (4, 8)]), Sum(["mp", (2,), (4, 8)])
    for each in (first, second):
        each.steps.pop(0)
    attend_back(3, 0)
    v.tie((At.gc, 1), (At.joined, 3, 0))
    v[At.far_b] = swap(v[At.joined, 3, 0], "dp", 1)
    attend_back(1, 0)
    v.turn((At.gc, 2), (At.joined, 1, 0), At.far_b, sums=[down_sum, up_sum])
    v[At.own_b] = swap(v[At.joined, 1, 0], "dp", 1)
    attend_back(2, 0, v[At.far_b])
    v.tie((At.gc, 0), (At.joined, 2, 0), At.own_b)
    first_mp = swap(v[At.joined, 2, 0], "mp", 1)
    attend_back(0, 0, v[At.own_b])
    v.turn((At.gc, 3), (At.joined, 0, 0), sums=[down_sum, up_sum])
    attend_back(3, 1)
    v.turn((At.gc, 1), (At.joined, 3, 1), sums=[down_sum, up_sum])
    v[At.far_b] = swap(v[At.joined, 3, 1], "dp", 1)
    attend_back(1, 1)
    v.turn((At.gc, 2), (At.joined, 1, 1), At.far_b, sums=[down_sum])
    v[At.own_b] = swap(v[At.joined, 1, 1], "dp", 1)
    v[At.down_all] = lax.all_gather(down_sum.state, "dp", tiled=True)
    attend_back(2, 1, v[At.far_b])
    first.state, first.moving = v[At.joined, 0, 0], [first_mp]
    v.turn((At.gc, 0), (At.joined, 2, 1), At.own_b, sums=[up_sum, first])
    second_mp = swap(v[At.joined, 2, 1], "mp", 1)
    v[At.up_all] = lax.all_gather(up_sum.state, "dp", tiled=True)
    attend_back(0, 1, v[At.own_b])
    second.state, second.moving = v[At.joined, 0, 1], [second_mp]
    v.turn(At.gm, (At.joined, 0, 1), sums=[second, first])
    v[At.input_grad], gain_one, bias_one = input_back(
        place,
        hidden_in,
        v[At.gm],
        row(ln1_gain),
        [v[At.gj, g, pair] for g in range(4) for pair in range(2)],
        joined_w,
    )
    own_up = halves_in_order(bias_up[0], bias_up[1], core)
    far_up = halves_in_order(bias_up[2], bias_up[3], core)
    width = hidden_in.shape[1]
    small = Butterfly(
        jnp.concatenate(
            [gain_one, bias_one, gain_two, bias_two, bias_down]
            + [halves_in_order(own_up, far_up, side).reshape(-1, width)]
        ),
        [("dp", 1), ("mp", 1), ("dp", 2), ("dp", 4), ("dp", 8)],
    )
    v.turn(At.middle, At.input_grad, sums=[second, first, small])
    first = Gather(first.state, [(4, 8), (2,), (1,)])
    v.turn(At.middle, sums=[first])
    v[At.output] = project_down(place, v[At.middle], row(b_down), hidden, down_w)
    v.turn(At.output, sums=[second, first, small])
    second = Gather(second.state, [(4, 8), (2,), (1,)])
    v.turn(At.output, sums=[second])
    v.tie(At.down_all, At.output)
    v[At.grad_down_w] = spread(
        place,
        v[At.down_all],
        [lambda c, y, z=z, x=x: (x * 2 + z) * 4 + y * 2 + c for z in range(2) for x in range(2)],
        lambda c, y: (c * 2 + y, 0),
        *w_down.shape,
    )
    v.turn(At.grad_down_w, At.up_all, sums=[second, first, small])
    v[At.grad_up_w] = spread(
        place,
        v[At.up_all],
        [lambda c, z, y=y, x=x: (x * 2 + z) * 4 + y * 2 + c for y in range(2) for x in range(2)],
        lambda c, z: (z, c),
        *w_up.shape,
    )
    v[At.first] = first.moving[0]
    v.turn(At.grad_up_w, At.first, sums=[second, small])
    grad_q, grad_k, grad_v, grad_out_w = spread_joined(
        place, (first.state, v[At.first]), (second.state, second.moving[0])
    )
    small.take()
    if small.steps:
        small.go()
        small.take()
    sums = small.state
    up_rows = b_up.shape[0] // width
    bias_up_sum = lax.dynamic_slice_in_dim(sums, 5 + side * up_rows, up_rows).reshape(-1)
    return (
        v[At.output],
        v[At.input_grad],
        sums[0],
        sums[1],
        grad_q,
        grad_k,
        grad_v,
        grad_out_w,
        sums[2],
        sums[3],
        v[At.grad_up_w],
        bias_up_sum,
        v[At.grad_down_w],
        sums[4],
    )


def solution(mesh):
    in_specs = (
        P(("dp", "mp"), None),
        P(("dp", "mp"), None),
        P(),
        P(),
        P(None, "mp"),
        P(None, "mp"),
        P(None, "mp"),
        P("mp", None),
        P(),
        P(),
        P(None, "mp"),
        P("mp"),
        P("mp", None),
        P(),
        P("mp", None, None),
    )
    out_specs = (
        P(("dp", "mp"), None),
        P(("dp", "mp"), None),
        P(),
        P(),
        P(None, "mp"),
        P(None, "mp"),
        P(None, "mp"),
        P("mp", None),
        P(),
        P(),
        P(None, "mp"),
        P("mp"),
        P("mp", None),
        P(),
    )
    def per_device(hidden_in, *others):
        w_query, w_up, rand_blocks = others[3], others[9], others[13]
        whole = hidden_in.shape[0] == SEQ and mesh.shape["mp"] == 2
        halved = mesh.shape["dp"] == 16 and rand_blocks.shape[0] == 8
        sized = w_query.shape == (1024, 512) and w_up.shape == (1024, 2048)
        layer = whole_sequence if whole and halved and sized else split_sequence
        return layer(hidden_in, *others)

    return jax.shard_map(
        per_device, mesh=mesh, in_specs=in_specs, out_specs=out_specs, check_vma=False
    )
```

```python
import jax
import jax.numpy as jnp
from jax import lax
from jax.experimental import pallas as pl
from jax.experimental.pallas import tpu as pltpu
from jax.sharding import PartitionSpec as P

HD = 64
BLOCK = 64
SEQ = 1024
PAIR = 2 * HD
BF16 = jnp.bfloat16
F32 = jnp.float32
NT = (((1,), (1,)), ((), ()))
TN = (((0,), (0,)), ((), ()))


def layer_norm(values, norm_gain, norm_bias):
    center = values - jnp.mean(values, axis=-1, keepdims=True)
    spread = jnp.mean(center * center, axis=-1, keepdims=True)
    return center * lax.rsqrt(spread + 1e-05) * norm_gain + norm_bias


def block_mask(rand_blocks):
    blocks = SEQ // BLOCK
    row_ids = jnp.arange(blocks)[:, None]
    col_ids = jnp.arange(blocks)[None, :]
    window = (
        (jnp.abs(row_ids - col_ids) <= 1)
        | (col_ids == 0)
        | (col_ids == blocks - 1)
        | (row_ids == 0)
        | (row_ids == blocks - 1)
    )
    picked = jnp.any(rand_blocks[:, :, :, None] == jnp.arange(blocks)[None, None, None, :], axis=2)
    allowed = window[None] | picked
    return jnp.repeat(jnp.repeat(allowed, BLOCK, axis=1), BLOCK, axis=2)


def attend_forward_split(joined_seq, allowed, scaling):
    queries = joined_seq[:, 0]
    key_rows = joined_seq[:, 1]
    value_rows = joined_seq[:, 2]
    scores = (
        jnp.einsum("qhd,khd->hqk", queries, key_rows, preferred_element_type=jnp.float32) * scaling
    )
    scores = jnp.where(allowed, scores, -1e30)
    highest = jnp.max(scores, axis=-1, keepdims=True)
    shifted = jnp.exp(scores - highest)
    row_totals = jnp.sum(shifted, axis=-1, keepdims=True)
    attn_probs = (shifted / row_totals).astype(jnp.bfloat16)
    context = jnp.einsum("hqk,khd->qhd", attn_probs, value_rows, preferred_element_type=jnp.float32)
    return (context.astype(jnp.bfloat16), (highest + jnp.log(row_totals))[..., 0])


def attend_backward_split(seq_items, allowed, scaling):
    joined_seq, grad_context, row_lse = seq_items
    queries = joined_seq[:, 0]
    key_rows = joined_seq[:, 1]
    value_rows = joined_seq[:, 2]
    scores = (
        jnp.einsum("qhd,khd->hqk", queries, key_rows, preferred_element_type=jnp.float32) * scaling
    )
    scores = jnp.where(allowed, scores, -1e30)
    attn_probs = jnp.exp(scores - row_lse[..., None])
    grad_values = jnp.einsum(
        "hqk,qhd->khd",
        attn_probs.astype(jnp.bfloat16),
        grad_context,
        preferred_element_type=jnp.float32,
    ).astype(jnp.bfloat16)
    grad_probs = jnp.einsum(
        "qhd,khd->hqk", grad_context, value_rows, preferred_element_type=jnp.float32
    )
    row_inner = jnp.sum(grad_probs * attn_probs, axis=-1, keepdims=True)
    grad_scores = (attn_probs * (grad_probs - row_inner)).astype(jnp.bfloat16)
    grad_queries = (
        jnp.einsum("hqk,khd->qhd", grad_scores, key_rows, preferred_element_type=jnp.float32)
        * scaling
    ).astype(jnp.bfloat16)
    grad_keys = (
        jnp.einsum("hqk,qhd->khd", grad_scores, queries, preferred_element_type=jnp.float32)
        * scaling
    ).astype(jnp.bfloat16)
    return jnp.stack([grad_queries, grad_keys, grad_values], axis=1)


def split_sequence(
    hidden_in,
    out_grad,
    ln1_gain,
    ln1_bias,
    w_query,
    w_key,
    w_value,
    w_out,
    ln2_gain,
    ln2_bias,
    w_up,
    b_up,
    w_down,
    b_down,
    rand_blocks,
):
    local_heads = rand_blocks.shape[0]
    head_width = local_heads * HD
    local_rows = hidden_in.shape[0]
    seq_count = local_rows * lax.axis_size("mp") // SEQ
    scaling = HD ** (-0.5)
    allowed = block_mask(rand_blocks)
    inputs = hidden_in.astype(jnp.float32)
    w_joined = jnp.concatenate([w_query, w_key, w_value], axis=1)
    normed_one = layer_norm(inputs, ln1_gain, ln1_bias).astype(jnp.bfloat16)
    rows_one = lax.all_gather(normed_one, "mp", axis=0, tiled=True)
    joined = jnp.dot(rows_one, w_joined, preferred_element_type=jnp.float32).astype(jnp.bfloat16)
    joined_seq = joined.reshape(seq_count, SEQ, 3, local_heads, HD)
    context, row_lse = lax.map(
        lambda seq_block: attend_forward_split(seq_block, allowed, scaling), joined_seq
    )
    context_rows = context.reshape(seq_count * SEQ, head_width)
    middle = inputs + lax.psum_scatter(
        jnp.dot(context_rows, w_out, preferred_element_type=jnp.float32).astype(jnp.bfloat16),
        "mp",
        scatter_dimension=0,
        tiled=True,
    ).astype(jnp.float32)
    normed_two = layer_norm(middle, ln2_gain, ln2_bias).astype(jnp.bfloat16)
    rows_two = lax.all_gather(normed_two, "mp", axis=0, tiled=True)
    up_pre = jnp.dot(rows_two, w_up, preferred_element_type=jnp.float32) + b_up
    hidden = jax.nn.gelu(up_pre, approximate=True).astype(jnp.bfloat16)
    output = (
        middle
        + (
            lax.psum_scatter(
                jnp.dot(hidden, w_down, preferred_element_type=jnp.float32).astype(jnp.bfloat16),
                "mp",
                scatter_dimension=0,
                tiled=True,
            ).astype(jnp.float32)
            + b_down
        )
    ).astype(jnp.bfloat16)
    grad_out = out_grad.astype(jnp.float32)
    bias_down = jnp.sum(grad_out, axis=0)
    rows_ffn = lax.all_gather(out_grad, "mp", axis=0, tiled=True)
    grad_hidden = jnp.einsum("nd,fd->nf", rows_ffn, w_down, preferred_element_type=jnp.float32)
    grad_down = jnp.einsum("nf,nd->fd", hidden, rows_ffn, preferred_element_type=jnp.float32)
    gelu_value, gelu_pull = jax.vjp(lambda pre_act: jax.nn.gelu(pre_act, approximate=True), up_pre)
    grad_up = gelu_pull(grad_hidden)[0].astype(jnp.bfloat16)
    bias_up = jnp.sum(grad_up, axis=0, dtype=jnp.float32)
    grad_up_weight = jnp.einsum("nd,nf->df", rows_two, grad_up, preferred_element_type=jnp.float32)
    grad_normed_two = lax.psum_scatter(
        jnp.einsum("nf,df->nd", grad_up, w_up, preferred_element_type=jnp.float32).astype(
            jnp.bfloat16
        ),
        "mp",
        scatter_dimension=0,
        tiled=True,
    ).astype(jnp.float32)
    norm_value_two, norm_pull_two = jax.vjp(layer_norm, middle, ln2_gain, ln2_bias)
    grad_mid_norm, gain_two, bias_two = norm_pull_two(grad_normed_two)
    grad_middle = grad_out + grad_mid_norm
    grad_attn = grad_middle.astype(jnp.bfloat16)
    rows_attn = lax.all_gather(grad_attn, "mp", axis=0, tiled=True)
    grad_context = jnp.einsum(
        "nd,ed->ne", rows_attn, w_out, preferred_element_type=jnp.float32
    ).astype(jnp.bfloat16)
    grad_out_weight = jnp.einsum(
        "ne,nd->ed", context_rows, rows_attn, preferred_element_type=jnp.float32
    )
    grad_joined = lax.map(
        lambda seq_items: attend_backward_split(seq_items, allowed, scaling),
        (joined_seq, grad_context.reshape(seq_count, SEQ, local_heads, HD), row_lse),
    )
    grad_joined = grad_joined.reshape(seq_count * SEQ, 3 * head_width)
    grad_joined_weight = jnp.einsum(
        "nd,ne->de", rows_one, grad_joined, preferred_element_type=jnp.float32
    )
    grad_normed_one = lax.psum_scatter(
        jnp.einsum("ne,de->nd", grad_joined, w_joined, preferred_element_type=jnp.float32).astype(
            jnp.bfloat16
        ),
        "mp",
        scatter_dimension=0,
        tiled=True,
    ).astype(jnp.float32)
    norm_value_one, norm_pull_one = jax.vjp(layer_norm, inputs, ln1_gain, ln1_bias)
    grad_in_norm, gain_one, bias_one = norm_pull_one(grad_normed_one)
    input_grad = grad_middle + grad_in_norm
    grad_joined_weight, grad_out_weight, grad_up_weight, bias_up, grad_down = (
        lax.psum(grad_joined_weight.astype(jnp.bfloat16), "dp").astype(jnp.float32),
        lax.psum(grad_out_weight.astype(jnp.bfloat16), "dp").astype(jnp.float32),
        lax.psum(grad_up_weight.astype(jnp.bfloat16), "dp").astype(jnp.float32),
        lax.psum(bias_up.astype(jnp.bfloat16), "dp").astype(jnp.float32),
        lax.psum(grad_down.astype(jnp.bfloat16), "dp").astype(jnp.float32),
    )
    gain_one, bias_one, gain_two, bias_two, bias_down = lax.psum(
        (gain_one, bias_one, gain_two, bias_two, bias_down), ("dp", "mp")
    )
    grad_query = grad_joined_weight[:, :head_width]
    grad_key = grad_joined_weight[:, head_width : 2 * head_width]
    grad_value = grad_joined_weight[:, 2 * head_width :]
    return (
        output,
        input_grad,
        gain_one,
        bias_one,
        grad_query,
        grad_key,
        grad_value,
        grad_out_weight,
        gain_two,
        bias_two,
        grad_up_weight,
        bias_up,
        grad_down,
        bias_down,
    )


VMEM_LIMIT = 56 << 20
TILE = 256
SPAN = 512
WIDE = 512
PACE = 0.02


def mm(left, right, dims=(((1,), (0,)), ((), ()))):
    return lax.dot_general(left, right, dims, preferred_element_type=F32)


def call(body, *, grid, in_specs, out_specs, out_shape, micros, name, scratch=(), scalars=1):
    return pl.pallas_call(
        body,
        grid_spec=pltpu.PrefetchScalarGridSpec(
            num_scalar_prefetch=scalars,
            grid=grid,
            in_specs=in_specs,
            out_specs=out_specs,
            scratch_shapes=list(scratch),
        ),
        out_shape=out_shape,
        compiler_params=pltpu.CompilerParams(vmem_limit_bytes=VMEM_LIMIT),
        cost_estimate=pl.CostEstimate(
            flops=int(micros * PACE * 1e9), bytes_accessed=0, transcendentals=0
        ),
        name=name,
    )


def shape(rows, columns, dtype=BF16):
    return jax.ShapeDtypeStruct((rows, columns), dtype)


def row_tile(width, dtype=None):
    return pl.BlockSpec((TILE, width), lambda i, s: (i, 0))


def column_tile(height):
    return pl.BlockSpec((height, TILE), lambda i, s: (0, i))


def resident(rows, columns):
    return pl.BlockSpec((rows, columns), lambda i, s: (0, 0))


def norm_parts(values):
    center = values - jnp.mean(values, axis=-1, keepdims=True)
    spread = jnp.mean(center * center, axis=-1, keepdims=True)
    return center, lax.rsqrt(spread + 1e-05)


def norm_backward(values, gain, grads):
    center, scale = norm_parts(values)
    unit = center * scale
    scaled = grads * gain
    mean_g = jnp.mean(scaled, axis=-1, keepdims=True)
    mean_gu = jnp.mean(scaled * unit, axis=-1, keepdims=True)
    grad_in = scale * (scaled - mean_g - unit * mean_gu)
    return (
        grad_in,
        jnp.sum(grads * unit, axis=0, keepdims=True),
        jnp.sum(grads, axis=0, keepdims=True),
    )


def flipped(rows):
    return rows.astype(F32).T.astype(BF16)


def accumulate(ref, value):
    @pl.when(pl.program_id(0) == 0)
    def _():
        ref[...] = value

    @pl.when(pl.program_id(0) > 0)
    def _():
        ref[...] += value


def norm_in_kernel(s, x_ref, g_ref, gain_ref, bias_ref, n_ref, sum_ref):
    center, scale = norm_parts(x_ref[...].astype(F32))
    n_ref[...] = (center * scale * gain_ref[...] + bias_ref[...]).astype(BF16)
    accumulate(sum_ref, jnp.sum(g_ref[...].astype(F32), axis=0, keepdims=True))


def norm_in(place, hidden_in, out_grad, gain, bias):
    rows, width = hidden_in.shape
    return call(
        norm_in_kernel,
        grid=(rows // TILE,),
        in_specs=[row_tile(width), row_tile(width), resident(1, width), resident(1, width)],
        out_specs=[row_tile(width), resident(1, width)],
        out_shape=[shape(rows, width), shape(1, width, F32)],
        micros=5,
        name="norm_in",
    )(place, hidden_in, out_grad, gain, bias)


def head_lanes(rows, head):
    lanes = lax.broadcasted_iota(jnp.int32, rows.shape, 1)
    return jnp.where(lanes // HD == head, rows, jnp.zeros_like(rows))


def spread_bias(bias, dims):
    blocks = bias.shape[0]
    tokens = lax.broadcasted_iota(jnp.int32, (blocks, blocks * BLOCK), 1) // BLOCK
    which = lax.broadcasted_iota(jnp.int32, tokens.shape, 0)
    return mm(bias, jnp.where(tokens == which, 1.0, 0.0).astype(BF16), dims)


def add_blocks(scores, bias):
    rows, width = scores.shape
    return (scores.reshape(rows // BLOCK, BLOCK, width) + bias[:, None, :]).reshape(rows, width)


def attend_forward_kernel(s, q_ref, k_ref, v_ref, bias_ref, context_ref, lse_ref):
    scaling = HD ** (-0.5)
    bias = [spread_bias(bias_ref[head], (((1,), (0,)), ((), ()))) for head in range(2)]
    jobs = [(start, head) for start in range(0, q_ref.shape[0], SPAN) for head in range(2)]

    def score(job):
        start, head = job
        queries = q_ref[start : start + SPAN, :] * jnp.asarray(scaling, BF16)
        return mm(head_lanes(queries, head), k_ref[...], NT)

    ahead = score(jobs[0])
    parts = []
    for index, (start, head) in enumerate(jobs):
        rows = slice(start, start + SPAN)
        scores = ahead
        if index + 1 < len(jobs):
            ahead = score(jobs[index + 1])
        scores = add_blocks(scores, bias[head][start // BLOCK : (start + SPAN) // BLOCK])
        highest = jnp.max(scores, axis=1, keepdims=True)
        shifted = jnp.exp(scores - highest)
        totals = jnp.sum(shifted, axis=1, keepdims=True)
        parts.append(mm(shifted.astype(BF16), v_ref[...]) / totals)
        lse_ref[0, head : head + 1, rows] = (highest + jnp.log(totals)).T
        if head == 1:
            lanes = lax.broadcasted_iota(jnp.int32, parts[0].shape, 1)
            context_ref[rows, :] = jnp.where(lanes < HD, parts[0], parts[1]).astype(BF16)
            parts = []


def thin_block(column):
    return pl.BlockSpec((SEQ, PAIR), lambda p, s: (0, column(p)))


def attend_forward(place, which, qkv, bias):
    pairs = 2
    blocks = SEQ // BLOCK
    return call(
        attend_forward_kernel,
        grid=(pairs,),
        in_specs=[
            thin_block(lambda p: p),
            thin_block(lambda p: pairs + p),
            thin_block(lambda p: 2 * pairs + p),
            pl.BlockSpec((2, blocks, blocks), lambda p, s: (s[which % 2] * pairs + p, 0, 0)),
        ],
        out_specs=[thin_block(lambda p: p), pl.BlockSpec((1, 2, SEQ), lambda p, s: (p, 0, 0))],
        out_shape=[shape(SEQ, pairs * PAIR), jax.ShapeDtypeStruct((pairs, 2, SEQ), F32)],
        micros=12,
        name="attend_forward",
    )(place, qkv, qkv, qkv, bias)


def attend_backward_kernel(
    outs,
    s,
    q_ref,
    k_ref,
    v_ref,
    grad_ref,
    context_ref,
    lse_ref,
    bias_ref,
    n_hbm,
    ga_hbm,
    *refs,
):
    *extras, out_ref, w_ref, key_acc, value_acc, flat_ref, n_ref, ga_ref, more_ref, sem = refs
    copies = [pltpu.make_async_copy(n_hbm, n_ref, sem.at[0])]
    if outs:
        all_contexts_ref = extras.pop(0)
        copies.append(pltpu.make_async_copy(ga_hbm, ga_ref, sem.at[1]))
    if extras:
        copies.append(pltpu.make_async_copy(extras[0], more_ref, sem.at[2]))
    for copy in copies:
        copy.start()
    scaling = HD ** (-0.5)
    key_rows = k_ref[...]
    value_rows = v_ref[...]
    keys_t = flipped(key_rows)
    bias = [spread_bias(bias_ref[head], TN) for head in range(2)]
    for start in range(0, q_ref.shape[0], SPAN):
        rows = slice(start, start + SPAN)
        queries = q_ref[rows, :] * jnp.asarray(scaling, BF16)
        grads = grad_ref[rows, :]
        inner_t = (grads.astype(F32) * context_ref[rows, :].astype(F32)).T
        probs, slopes, masked_q, masked_g, parts = [], [], [], [], []
        for head in range(2):
            query_h, grad_h = head_lanes(queries, head), head_lanes(grads, head)
            scores = add_blocks(mm(key_rows, query_h, NT), bias[head][:, rows])
            attn = jnp.exp(scores - lse_ref[0, head : head + 1, rows])
            inner = jnp.sum(inner_t[head * HD : (head + 1) * HD], axis=0, keepdims=True)
            slope = (attn * (mm(value_rows, grad_h, NT) - inner)).astype(BF16)
            parts.append(mm(keys_t[head * HD : (head + 1) * HD], slope) * scaling)
            probs.append(attn.astype(BF16))
            slopes.append(slope)
            masked_q.append(query_h)
            masked_g.append(grad_h)
        grad_q = jnp.concatenate(parts, axis=0)
        flat_ref[:PAIR, rows] = grad_q.astype(BF16)
        out_ref[rows, :PAIR] = grad_q.T.astype(BF16)
        grad_k = mm(jnp.concatenate(slopes, axis=1), jnp.concatenate(masked_q, axis=0))
        grad_v = mm(jnp.concatenate(probs, axis=1), jnp.concatenate(masked_g, axis=0))
        if start == 0:
            key_acc[...] = grad_k
            value_acc[...] = grad_v
        else:
            key_acc[...] += grad_k
            value_acc[...] += grad_v
    for part, acc in ((1, key_acc), (2, value_acc)):
        columns = slice(part * PAIR, (part + 1) * PAIR)
        total = acc[...]
        out_ref[:, columns] = total.astype(BF16)
        flat_ref[columns, :] = total.T.astype(BF16)
    for copy in copies:
        copy.wait()

    def give(lines, product):
        if extras:
            product = product + more_ref[lines, :].astype(F32)
        w_ref[lines, :] = product.astype(BF16)

    for part in range(3):
        lines = slice(part * PAIR, (part + 1) * PAIR)
        give(lines, mm(flat_ref[lines, :], n_ref[...]))
    if outs:
        give(slice(3 * PAIR, w_ref.shape[0]), mm(flipped(all_contexts_ref[...]), ga_ref[...]))


def attend_backward(
    place, which, pair, qkv, grad_context, context, row_lse, bias, normed, grad, more=None
):
    pairs = 2
    blocks = SEQ // BLOCK
    width = normed.shape[1]
    lines = 3 * PAIR + (context.shape[1] if pair == 0 else 0)
    outs = pair == 0
    return call(
        lambda *refs: attend_backward_kernel(outs, *refs),
        grid=(1,),
        in_specs=[
            thin_block(lambda p: pair),
            thin_block(lambda p: pairs + pair),
            thin_block(lambda p: 2 * pairs + pair),
            thin_block(lambda p: pair),
            thin_block(lambda p: pair),
            pl.BlockSpec((1, 2, SEQ), lambda p, s: (pair, 0, 0)),
            pl.BlockSpec((2, blocks, blocks), lambda p, s: (s[which % 2] * pairs + pair, 0, 0)),
            pl.BlockSpec(memory_space=pl.ANY),
            pl.BlockSpec(memory_space=pl.ANY),
        ]
        + [resident(*context.shape)] * outs
        + [pl.BlockSpec(memory_space=pl.ANY)] * (more is not None),
        out_specs=[resident(SEQ, 3 * PAIR), resident(lines, width)],
        out_shape=[shape(SEQ, 3 * PAIR), shape(lines, width)],
        scratch=[
            pltpu.VMEM((SEQ, PAIR), F32),
            pltpu.VMEM((SEQ, PAIR), F32),
            pltpu.VMEM((3 * PAIR, SEQ), BF16),
            pltpu.VMEM(normed.shape, BF16),
            pltpu.VMEM(grad.shape if outs else (16, PAIR), BF16),
            pltpu.VMEM((lines, width) if more is not None else (16, PAIR), BF16),
            pltpu.SemaphoreType.DMA((3,)),
        ],
        micros=10,
        name="attend_backward",
    )(
        place,
        qkv,
        qkv,
        qkv,
        grad_context,
        context,
        row_lse,
        bias,
        normed,
        grad,
        *[context] * outs,
        *[more] * (more is not None),
    )


def project_out_kernel(s, x_ref, *refs):
    contexts, weights = refs[:4], refs[4:8]
    gain_ref, bias_ref, middle_ref, n_ref = refs[8:]
    middle = x_ref[...].astype(F32)
    for context_ref, w_ref in zip(contexts, weights):
        middle = middle + mm(context_ref[...], w_ref[...])
    middle_ref[...] = middle
    center, scale = norm_parts(middle)
    n_ref[...] = (center * scale * gain_ref[...] + bias_ref[...]).astype(BF16)


def own_then_far(block, along):
    specs = []
    for which in range(4):
        if along == 0:
            specs.append(pl.BlockSpec(block, lambda i, s, which=which: (s[which], 0)))
        else:
            specs.append(pl.BlockSpec(block, lambda i, s, which=which: (0, s[which])))
    return specs


def project_out(place, hidden_in, contexts, weights, gain, bias):
    rows, width = hidden_in.shape
    return call(
        project_out_kernel,
        grid=(rows // TILE,),
        in_specs=[row_tile(width)]
        + [row_tile(2 * PAIR)] * 4
        + own_then_far((2 * PAIR, width), 0)
        + [resident(1, width)] * 2,
        out_specs=[row_tile(width), row_tile(width)],
        out_shape=[shape(rows, width, F32), shape(rows, width)],
        micros=7,
        name="project_out",
    )(place, hidden_in, *contexts, *weights, gain, bias)


def gelu_and_slope(pre):
    root, cubic = 0.7978845608028654, 0.044715
    square = pre * pre
    bent = jnp.tanh(root * (pre + cubic * pre * square))
    half = 0.5 * pre
    slope = 0.5 * (1.0 + bent) + half * (1.0 - bent * bent) * (root * (1.0 + 3.0 * cubic * square))
    return half + half * bent, slope


def feed_forward_kernel(tiles, s, n_ref, g_ref, bias_ref, *refs):
    *ups, down_ref, h_ref, gu_ref, sum_ref = refs

    def run(up_ref):
        pre = mm(n_ref[...], up_ref[...]) + bias_ref[...]
        grad_hidden = mm(g_ref[...], down_ref[...], NT)
        value, slope = gelu_and_slope(pre)
        h_ref[...] = value.astype(BF16)
        grad_up = (grad_hidden * slope).astype(BF16)
        gu_ref[...] = grad_up
        sum_ref[...] = jnp.sum(grad_up.astype(F32), axis=0, keepdims=True)

    if len(ups) == 1:
        run(ups[0])
    else:
        mine = pl.program_id(0) // (tiles // 2) == s[4]

        @pl.when(mine)
        def _():
            run(ups[0])

        @pl.when(jnp.logical_not(mine))
        def _():
            run(ups[1])


def wide_tile(height):
    return pl.BlockSpec((height, WIDE), lambda i, s: (0, i))


def feed_forward(place, which, normed, out_grad, w_up, b_up, w_down):
    rows, width = normed.shape
    units = b_up.shape[1] // 2
    tiles = units // WIDE
    if which < 2:
        columns = [lambda i, s: (0, s[which] * tiles + i)]
    else:
        columns = [lambda i, s: (0, i % (tiles // 2))] * 2
    return call(
        lambda *refs: feed_forward_kernel(tiles, *refs),
        grid=(tiles,),
        in_specs=[
            resident(rows, width),
            resident(rows, width),
            pl.BlockSpec((1, WIDE), lambda i, s: (0, s[which % 2] * tiles + i)),
        ]
        + [pl.BlockSpec((width, WIDE), column) for column in columns]
        + [pl.BlockSpec((WIDE, width), lambda i, s: (s[which] * tiles + i, 0))],
        out_specs=[wide_tile(rows), wide_tile(rows), wide_tile(1)],
        out_shape=[shape(rows, units), shape(rows, units), shape(1, units, F32)],
        micros=12,
        name="feed_forward",
    )(place, normed, out_grad, b_up, *w_up, w_down)


def unit_blocks(units, width, halved, along):
    half = units // 2
    rows = [pl.BlockSpec((TILE, units), lambda i, s: (i, 0))] * 2
    if halved:
        rows += [
            pl.BlockSpec((TILE, half), lambda i, s: (i, s[4])),
            pl.BlockSpec((TILE, half), lambda i, s: (i, 1 - s[4])),
        ] * 2
    else:
        rows += rows
    far = half if halved else units
    count = 4 if halved else 2
    if along == 0:
        own = [
            pl.BlockSpec((units, width), lambda i, s, which=which: (s[which], 0)) for which in (0, 1)
        ]
        return rows + own + [resident(far, width)] * count
    own = [pl.BlockSpec((width, units), lambda i, s, which=which: (0, s[which])) for which in (0, 1)]
    return rows + own + [resident(width, far)] * count


def unit_arrays(slices, weights):
    arrays = [each for each, group in zip(slices, weights) for _ in group]
    return arrays + [part for group in weights for part in group]


def middle_back_kernel(s, g_ref, middle_ref, gain_ref, *refs):
    grads, weights, outs = refs[:6], refs[6:12], refs[12:16]
    gm_ref, ga_ref, gain_sum, bias_sum, *context_grads = refs[16:]
    total = mm(grads[0][...], weights[0][...], NT)
    for grad_ref, w_ref in zip(grads[1:], weights[1:]):
        total = total + mm(grad_ref[...], w_ref[...], NT)
    grad_in, gain, bias = norm_backward(middle_ref[...], gain_ref[...], total)
    grad_middle = g_ref[...].astype(F32) + grad_in
    gm_ref[...] = grad_middle
    ga_ref[...] = grad_middle.astype(BF16)
    accumulate(gain_sum, gain)
    accumulate(bias_sum, bias)
    for w_ref, out_ref in zip(outs, context_grads):
        out_ref[...] = mm(ga_ref[...], w_ref[...], NT).astype(BF16)


def middle_back(place, out_grad, middle, gain, grad_up, weights, out_weights):
    rows, width = middle.shape
    units = grad_up[0].shape[1]
    return call(
        middle_back_kernel,
        grid=(rows // TILE,),
        in_specs=[row_tile(width), row_tile(width), resident(1, width)]
        + unit_blocks(units, width, True, 1)
        + own_then_far((2 * PAIR, width), 0),
        out_specs=[row_tile(width), row_tile(width)]
        + [resident(1, width)] * 2
        + [row_tile(2 * PAIR)] * 4,
        out_shape=[shape(rows, width, F32), shape(rows, width)]
        + [shape(1, width, F32)] * 2
        + [shape(rows, 2 * PAIR)] * 4,
        micros=18,
        name="middle_back",
    )(place, out_grad, middle, gain, *unit_arrays(grad_up, weights), *out_weights)


def input_back_kernel(s, x_ref, gm_ref, gain_ref, *refs):
    grads, weights = refs[:8], refs[8:12]
    out_ref, gain_sum, bias_sum = refs[12:]
    total = None
    for group in range(4):
        pair_0, pair_1 = grads[2 * group][...], grads[2 * group + 1][...]
        joined = jnp.concatenate(
            [
                pair[:, part * PAIR : (part + 1) * PAIR]
                for part in range(3)
                for pair in (pair_0, pair_1)
            ],
            axis=1,
        )
        product = mm(joined, weights[group][...], NT)
        total = product if total is None else total + product
    grad_in, gain, bias = norm_backward(x_ref[...].astype(F32), gain_ref[...], total)
    out_ref[...] = gm_ref[...] + grad_in
    accumulate(gain_sum, gain)
    accumulate(bias_sum, bias)


def input_back(place, hidden_in, grad_middle, gain, grads, weights):
    rows, width = hidden_in.shape
    return call(
        input_back_kernel,
        grid=(rows // TILE,),
        in_specs=[row_tile(width), row_tile(width), resident(1, width)]
        + [row_tile(3 * PAIR)] * 8
        + [resident(width, 6 * PAIR)] * 4,
        out_specs=[row_tile(width)] + [resident(1, width)] * 2,
        out_shape=[shape(rows, width, F32)] + [shape(1, width, F32)] * 2,
        micros=15,
        name="input_back",
    )(place, hidden_in, grad_middle, gain, *grads, *weights)


def project_down_kernel(s, middle_ref, bias_ref, *refs):
    hidden, weights, out_ref = refs[:4], refs[4:8], refs[8]
    total = middle_ref[...] + bias_ref[...]
    for h_ref, w_ref in zip(hidden, weights):
        total = total + mm(h_ref[...], w_ref[...])
    out_ref[...] = total.astype(BF16)


def project_down(place, middle, bias, hidden, weights):
    rows, width = middle.shape
    units = hidden[0].shape[1]
    return call(
        project_down_kernel,
        grid=(rows // TILE,),
        in_specs=[row_tile(width), resident(1, width)] + unit_blocks(units, width, False, 0),
        out_specs=row_tile(width),
        out_shape=shape(rows, width),
        micros=15,
        name="project_down",
    )(place, middle, bias, *unit_arrays(hidden, weights))


def block_bias(rand_blocks):
    blocks = SEQ // BLOCK
    row_ids = jnp.arange(blocks)[:, None]
    col_ids = jnp.arange(blocks)[None, :]
    window = (
        (jnp.abs(row_ids - col_ids) <= 1)
        | (col_ids == 0)
        | (col_ids == blocks - 1)
        | (row_ids == 0)
        | (row_ids == blocks - 1)
    )
    picked = jnp.any(rand_blocks[:, :, :, None] == col_ids[None, :, None, :], axis=2)
    return jnp.where(window[None] | picked, 0.0, -1e30).astype(BF16)


def swap(array, axis, bit):
    size = lax.axis_size(axis)
    return lax.ppermute(array, axis, [(place, place ^ bit) for place in range(size)])


def add_up(*terms):
    total = terms[0].astype(F32)
    for term in terms[1:]:
        total = total + term.astype(F32)
    return total.astype(terms[0].dtype)


def tied(*values):
    return lax.optimization_barrier(values)


class Sum:
    def __init__(self, steps):
        self.steps = list(steps)
        self.paired = self.steps[0] != "mp"
        self.state, self.sending, self.moving = None, [], []

    def parts_of(self, terms):
        if not self.steps:
            self.state, self.sending = add_up(*terms), []
        elif self.steps[0] == "mp":
            near, far = zip(*terms)
            self.state, self.sending = add_up(*near), [add_up(*far)]
        else:
            bits = self.steps[0]
            partners = [0]
            for bit in bits:
                partners += [bit | other for other in partners]
            self.partners = partners[1:]
            rows = terms[0][0].shape[0] if isinstance(terms[0], tuple) else terms[0].shape[0]
            rows //= len(partners)
            index = lax.axis_index("dp") // bits[0] % len(partners)

            def cut(term, other):
                start = (index ^ (other // bits[0])) * rows
                return lax.dynamic_slice_in_dim(term, start, rows, 0)

            def summed(other):
                if isinstance(terms[0], tuple):
                    return jnp.concatenate(
                        [add_up(*[cut(term, other) for term in half]) for half in zip(*terms)]
                    )
                return add_up(*[cut(term, other) for term in terms])

            self.state = summed(0)
            self.sending = [summed(other) for other in self.partners]

    def go(self):
        step = self.steps.pop(0)
        if step == "mp":
            self.moving = [swap(part, "mp", 1) for part in self.sending]
        else:
            self.moving = [swap(part, "dp", way) for part, way in zip(self.sending, self.partners)]

    def take(self):
        terms = [self.state] + self.moving
        if self.paired and self.steps[0] == "mp":
            self.paired = False
            rows = terms[0].shape[0] // 2
            terms = [(term[:rows], term[rows:]) for term in terms]
        self.parts_of(terms)


class Tied(dict):
    def tie(self, *names):
        for name, value in zip(names, tied(*[self[name] for name in names])):
            self[name] = value
        return self[names[0]]

    def turn(self, *names, sums=()):
        counts = [len(each.moving) for each in sums]
        flat = [part for each in sums for part in each.moving]
        kept = list(tied(*[self[name] for name in names], *flat))
        for name in names:
            self[name] = kept.pop(0)
        for each, count in zip(sums, counts):
            each.moving = [kept.pop(0) for _ in range(count)]
            if count:
                each.take()
        flat = [self[name] for name in names]
        for each in sums:
            flat += [each.state] + each.sending
        kept = list(tied(*flat))
        for name in names:
            self[name] = kept.pop(0)
        for each in sums:
            each.state = kept.pop(0)
            each.sending = [kept.pop(0) for _ in each.sending]
            each.moving = []
            if each.steps:
                each.go()


class Gather:
    def __init__(self, state, steps):
        self.state, self.steps, self.sending, self.moving = state, list(steps), [], []

    def go(self):
        bits = self.steps.pop(0)
        partners = [0]
        for bit in bits:
            partners += [bit | other for other in partners]
        self.moving = [swap(self.state, "dp", way) for way in partners[1:]]

    def take(self):
        self.state = jnp.concatenate([self.state] + self.moving)


class Butterfly:
    def __init__(self, state, steps):
        self.state, self.steps, self.sending, self.moving = state, list(steps), [], []

    def go(self):
        self.moving = [swap(self.state, *self.steps.pop(0))]

    def take(self):
        self.state = self.state + self.moving[0]


def spread_kernel(s, *refs):
    *parts, out_ref = refs
    height = parts[0].shape[0]
    for index, part in enumerate(parts):
        out_ref[index * height : (index + 1) * height, :] = part[...].astype(F32)


def spread(place, gathered, sources, target, rows, columns):
    width = gathered.shape[1]
    height = rows * columns // width // 4 // len(sources)
    return call(
        spread_kernel,
        grid=(2, 2),
        in_specs=[
            pl.BlockSpec((height, width), lambda c, y, s, source=source: (source(c, y), 0))
            for source in sources
        ],
        out_specs=pl.BlockSpec((height * len(sources), width), lambda c, y, s: target(c, y)),
        out_shape=shape(rows, columns, F32),
        micros=4,
        name="spread",
    )(place, *[gathered] * len(sources))


def spread_joined_kernel(s, one_a, one_b, two_a, two_b, q_ref, k_ref, v_ref, o_ref, flat):
    mine = pl.program_id(0) == s[0]
    first = 0
    for part_a, part_b in ((one_a, one_b), (two_a, two_b)):
        height = part_a.shape[0] // 8
        for y in range(2):
            for z in range(4):
                start = first + (y * 4 + z) * height
                source = ((y ^ s[4]) * 4 + (z ^ s[5])) * height
                lines = pl.ds(pl.multiple_of(source, height), height)
                flat[start : start + height, :] = jnp.where(mine, part_a[lines, :], part_b[lines, :])
        first += 8 * height
    second = one_a.shape[0]
    for part, ref in enumerate((q_ref, k_ref, v_ref)):
        for pair, first in enumerate((0, second)):
            lines = slice(first + part * PAIR, first + (part + 1) * PAIR)
            ref[:, pair * PAIR : (pair + 1) * PAIR] = flat[lines, :].astype(F32).T
    o_ref[...] = flat[3 * PAIR : second, :].astype(F32)


def spread_joined(place, one, two):
    width = one[0].shape[1]
    columns = pl.BlockSpec((width, 2 * PAIR), lambda c, s: (0, c))
    return call(
        spread_joined_kernel,
        grid=(2,),
        in_specs=[resident(*each.shape) for each in (*one, *two)],
        out_specs=[columns] * 3 + [pl.BlockSpec((2 * PAIR, width), lambda c, s: (c, 0))],
        out_shape=[shape(width, 4 * PAIR, F32)] * 3 + [shape(4 * PAIR, width, F32)],
        scratch=[pltpu.VMEM((one[0].shape[0] + two[0].shape[0], width), BF16)],
        micros=4,
        name="spread_joined",
    )(place, *one, *two)


class At:
    (
        out_piece, up_piece, down_piece, far_ja, far_rand, far_bup, n1, qkv,
        ctx, far_jb, far_out_a, far_out_b, up_mine, down_a, middle, n2,
        g, gu, down, up, up_other, up_b0, up_b1, down_b,
        near_down, near_up, far_down, far_up, gm, ga, gc, gj,
        joined, far_b, own_b, down_all, up_all, input_grad, output, grad_down_w,
        first, grad_up_w,
    ) = range(42)


def whole_sequence(
    hidden_in,
    out_grad,
    ln1_gain,
    ln1_bias,
    w_query,
    w_key,
    w_value,
    w_out,
    ln2_gain,
    ln2_bias,
    w_up,
    b_up,
    w_down,
    b_down,
    rand_blocks,
):
    device = lax.axis_index("dp")
    core, over_y, side = device % 2, (device // 2) % 2, lax.axis_index("mp")
    zero = 0 * core
    place = jnp.stack([core, 1 - core, zero, zero, over_y, device // 4]).astype(jnp.int32)

    def part(array, axis, index, count):
        size = array.shape[axis] // count
        return lax.dynamic_slice_in_dim(array, index * size, size, axis)

    def joined(other):
        return jnp.concatenate(
            [part(each, 1, core ^ other, 2) for each in (w_query, w_key, w_value)], axis=1
        )

    def halves_in_order(mine, other, bit):
        return jnp.where(
            bit == 0,
            jnp.concatenate([mine, other], axis=1),
            jnp.concatenate([other, mine], axis=1),
        )

    def row(vector):
        return vector.reshape(1, -1)

    v = Tied()
    own_ja, own_jb = joined(0), joined(1)
    quarter = 2 * core + over_y
    v[At.out_piece], v[At.up_piece] = part(w_out, 0, core, 2), part(w_up, 1, quarter, 4)
    v[At.down_piece] = part(w_down, 0, core, 2)
    v[At.far_ja] = swap(own_ja, "mp", 1)
    v[At.far_rand], v[At.far_bup] = swap(rand_blocks, "mp", 1), swap(b_up, "mp", 1)
    own_bias = block_bias(rand_blocks)
    v[At.n1], bias_down = norm_in(place, hidden_in, out_grad, row(ln1_gain), row(ln1_bias))
    row_lse = [None] * 4

    def attend(g, weights):
        v[At.qkv, g] = mm(v[At.n1], weights).astype(BF16)
        v[At.ctx, g], row_lse[g] = attend_forward(place, g, v[At.qkv, g], bias[g])

    bias = [own_bias, own_bias]
    attend(0, own_ja)
    v.tie(At.n1, (At.ctx, 0), At.far_rand, At.far_bup)
    bias += [block_bias(v[At.far_rand])] * 2
    attend(1, own_jb)
    v.tie(At.n1, At.far_ja, At.out_piece, (At.ctx, 1))
    v[At.far_jb], v[At.far_out_a] = swap(v[At.far_ja], "dp", 1), swap(v[At.out_piece], "mp", 1)
    attend(2, v[At.far_ja])
    v.tie(At.n1, At.far_jb, At.far_out_a, At.up_piece, (At.ctx, 2))
    v[At.far_out_b], v[At.up_mine] = swap(v[At.far_out_a], "dp", 1), swap(v[At.up_piece], "mp", 1)
    attend(3, v[At.far_jb])
    v.tie((At.ctx, 3), At.far_out_b, At.down_piece)
    v[At.down_a] = swap(v[At.down_piece], "mp", 1)
    joined_w = [own_ja, own_jb, v[At.far_ja], v[At.far_jb]]
    out_w = [w_out, w_out, v[At.far_out_a], v[At.far_out_b]]
    v[At.middle], v[At.n2] = project_out(
        place, hidden_in, [v[At.ctx, g] for g in range(4)], out_w, row(ln2_gain), row(ln2_bias)
    )

    hidden, bias_up = [None] * 4, [None] * 4
    up_bias = [row(b_up), row(b_up), row(v[At.far_bup]), row(v[At.far_bup])]
    v[At.g] = out_grad

    def feed(g, up, down):
        hidden[g], v[At.gu, g], bias_up[g] = feed_forward(
            place, g, v[At.n2], v[At.g], up, up_bias[g], down
        )

    def down_grad(g):
        v[At.down, g] = mm(hidden[g], v[At.g], TN).astype(BF16)

    def up_grad(g):
        v[At.up, g] = mm(v[At.n2], v[At.gu, g], TN).astype(BF16)

    v.tie(At.n2, At.up_mine)
    v[At.up_other] = swap(v[At.up_mine], "dp", 2)
    feed(1, (w_up,), w_down)
    v.tie(At.n2, (At.gu, 1))
    feed(0, (w_up,), w_down)
    v.tie(At.g, At.n2, At.up_mine, At.up_other, (At.gu, 0))
    v[At.up_b0], v[At.up_b1] = swap(v[At.up_mine], "dp", 1), swap(v[At.up_other], "dp", 1)
    for g in (1, 0):
        down_grad(g)
        up_grad(g)
    v.tie(At.n2, At.g, At.down_a, At.up_b0, At.up_b1, *[(name, g) for name in (At.down, At.up) for g in (0, 1)])
    v[At.down_b] = swap(v[At.down_a], "dp", 1)
    v[At.near_down], v[At.near_up] = swap(v[At.down, 1], "dp", 1), swap(v[At.up, 1], "dp", 1)
    feed(2, (v[At.up_mine], v[At.up_other]), v[At.down_a])
    v.tie(At.n2, At.g, At.down_b, At.near_down, At.near_up, (At.gu, 2))
    feed(3, (v[At.up_b0], v[At.up_b1]), v[At.down_b])
    up_w = [(w_up,), (w_up,), (v[At.up_mine], v[At.up_other]), (v[At.up_b0], v[At.up_b1])]
    down_w = [(w_down,), (w_down,), (v[At.down_a],), (v[At.down_b],)]
    v.tie(At.g, At.n2, (At.gu, 3))
    down_grad(3)
    v.tie(At.g, At.n2, (At.down, 3))
    v[At.far_down] = swap(v[At.down, 3], "dp", 1)
    up_grad(3)
    v.tie(At.g, At.n2, (At.up, 3), At.far_down)
    v[At.far_up] = swap(v[At.up, 3], "dp", 1)
    down_sum = Sum(["mp", (2,), (4,), (8,)])
    far = (mm(hidden[2], v[At.g], TN) + v[At.far_down].astype(F32)).astype(BF16)
    down_sum.state, down_sum.sending = v[At.down, 0], [far]
    v.turn(At.n2, At.far_up, sums=[down_sum])
    down_sum.moving.append(v[At.near_down])
    far = (mm(v[At.n2], v[At.gu, 2], TN) + v[At.far_up].astype(F32)).astype(BF16)
    up_sum = Sum([(4,), "mp", (2,), (8,)])
    up_sum.parts_of([(add_up(v[At.up, 0], v[At.near_up]), far)])
    v.turn(At.g, sums=[up_sum])

    v[At.gm], v[At.ga], gain_two, bias_two, *context_grads = middle_back(
        place,
        v[At.g],
        v[At.middle],
        row(ln2_gain),
        [v[At.gu, g] for g in range(4)],
        up_w,
        [w_out, w_out, v[At.far_out_a], v[At.far_out_b]],
    )
    for g in range(4):
        v[At.gc, g] = context_grads[g]
    v.tie(At.ga, *[(At.gc, g) for g in range(4)])

    def attend_back(g, pair, more=None):
        v[At.gj, g, pair], v[At.joined, g, pair] = attend_backward(
            place,
            g,
            pair,
            v[At.qkv, g],
            v[At.gc, g],
            v[At.ctx, g],
            row_lse[g],
            bias[g],
            v[At.n1],
            v[At.ga],
            more,
        )

    first, second = Sum(["mp", (2,), (4, 8)]), Sum(["mp", (2,), (4, 8)])
    for each in (first, second):
        each.steps.pop(0)
    attend_back(3, 0)
    v.tie((At.gc, 1), (At.joined, 3, 0))
    v[At.far_b] = swap(v[At.joined, 3, 0], "dp", 1)
    attend_back(1, 0)
    v.turn((At.gc, 2), (At.joined, 1, 0), At.far_b, sums=[down_sum, up_sum])
    v[At.own_b] = swap(v[At.joined, 1, 0], "dp", 1)
    attend_back(2, 0, v[At.far_b])
    v.tie((At.gc, 0), (At.joined, 2, 0), At.own_b)
    first_mp = swap(v[At.joined, 2, 0], "mp", 1)
    attend_back(0, 0, v[At.own_b])
    v.turn((At.gc, 3), (At.joined, 0, 0), sums=[down_sum, up_sum])
    attend_back(3, 1)
    v.turn((At.gc, 2), (At.joined, 3, 1), sums=[down_sum])
    v[At.far_b] = swap(v[At.joined, 3, 1], "dp", 1)
    attend_back(2, 1)
    v.tie((At.gc, 1), (At.joined, 2, 1), At.far_b)
    v[At.joined, 2, 1] = add_up(v[At.joined, 2, 1], v[At.far_b])
    first.state, first.moving = v[At.joined, 0, 0], [first_mp]
    v.turn((At.gc, 1), (At.joined, 2, 1), sums=[down_sum, up_sum, first])
    second_mp = swap(v[At.joined, 2, 1], "mp", 1)
    v[At.down_all] = lax.all_gather(down_sum.state, "dp", tiled=True)
    attend_back(1, 1)
    v.tie((At.gc, 0), (At.joined, 1, 1))
    v[At.own_b] = swap(v[At.joined, 1, 1], "dp", 1)
    attend_back(0, 1)
    v.tie(At.gm, (At.joined, 0, 1), At.own_b)
    v[At.joined, 0, 1] = add_up(v[At.joined, 0, 1], v[At.own_b])
    second.state, second.moving = v[At.joined, 0, 1], [second_mp]
    v.turn(At.gm, (At.joined, 0, 1), sums=[second, first, up_sum])
    v[At.up_all] = lax.all_gather(up_sum.state, "dp", tiled=True)
    v[At.input_grad], gain_one, bias_one = input_back(
        place,
        hidden_in,
        v[At.gm],
        row(ln1_gain),
        [v[At.gj, g, pair] for g in range(4) for pair in range(2)],
        joined_w,
    )
    own_up = halves_in_order(bias_up[0], bias_up[1], core)
    far_up = halves_in_order(bias_up[2], bias_up[3], core)
    width = hidden_in.shape[1]
    small = Butterfly(
        jnp.concatenate(
            [gain_one, bias_one, gain_two, bias_two, bias_down]
            + [halves_in_order(own_up, far_up, side).reshape(-1, width)]
        ),
        [("dp", 1), ("mp", 1), ("dp", 2), ("dp", 4), ("dp", 8)],
    )
    v.turn(At.middle, At.input_grad, sums=[second, first, small])
    first = Gather(first.state, [(4, 8), (2,), (1,)])
    v.turn(At.middle, sums=[first])
    v[At.output] = project_down(place, v[At.middle], row(b_down), hidden, down_w)
    v.turn(At.output, sums=[second, first, small])
    second = Gather(second.state, [(4, 8), (2,), (1,)])
    v.turn(At.output, sums=[second])
    v.tie(At.down_all, At.output)
    v[At.grad_down_w] = spread(
        place,
        v[At.down_all],
        [lambda c, y, z=z, x=x: (x * 2 + z) * 4 + y * 2 + c for z in range(2) for x in range(2)],
        lambda c, y: (c * 2 + y, 0),
        *w_down.shape,
    )
    v.turn(At.grad_down_w, sums=[second, first, small])
    v[At.first] = first.moving[0]
    v.turn(At.first, At.up_all, sums=[second, small])
    v[At.grad_up_w] = spread(
        place,
        v[At.up_all],
        [lambda c, z, y=y, x=x: (x * 2 + z) * 4 + y * 2 + c for y in range(2) for x in range(2)],
        lambda c, z: (z, c),
        *w_up.shape,
    )
    grad_q, grad_k, grad_v, grad_out_w = spread_joined(
        place, (first.state, v[At.first]), (second.state, second.moving[0])
    )
    small.take()
    if small.steps:
        small.go()
        small.take()
    sums = small.state
    up_rows = b_up.shape[0] // width
    bias_up_sum = lax.dynamic_slice_in_dim(sums, 5 + side * up_rows, up_rows).reshape(-1)
    return (
        v[At.output],
        v[At.input_grad],
        sums[0],
        sums[1],
        grad_q,
        grad_k,
        grad_v,
        grad_out_w,
        sums[2],
        sums[3],
        v[At.grad_up_w],
        bias_up_sum,
        v[At.grad_down_w],
        sums[4],
    )


def solution(mesh):
    in_specs = (
        P(("dp", "mp"), None),
        P(("dp", "mp"), None),
        P(),
        P(),
        P(None, "mp"),
        P(None, "mp"),
        P(None, "mp"),
        P("mp", None),
        P(),
        P(),
        P(None, "mp"),
        P("mp"),
        P("mp", None),
        P(),
        P("mp", None, None),
    )
    out_specs = (
        P(("dp", "mp"), None),
        P(("dp", "mp"), None),
        P(),
        P(),
        P(None, "mp"),
        P(None, "mp"),
        P(None, "mp"),
        P("mp", None),
        P(),
        P(),
        P(None, "mp"),
        P("mp"),
        P("mp", None),
        P(),
    )
    def per_device(hidden_in, *others):
        w_query, w_up, rand_blocks = others[3], others[9], others[13]
        whole = hidden_in.shape[0] == SEQ and mesh.shape["mp"] == 2
        halved = mesh.shape["dp"] == 16 and rand_blocks.shape[0] == 8
        sized = w_query.shape == (1024, 512) and w_up.shape == (1024, 2048)
        layer = whole_sequence if whole and halved and sized else split_sequence
        return layer(hidden_in, *others)

    return jax.shard_map(
        per_device, mesh=mesh, in_specs=in_specs, out_specs=out_specs, check_vma=False
    )
```

```python
import jax
import jax.numpy as jnp
from jax import lax
from jax.experimental import pallas as pl
from jax.experimental.pallas import tpu as pltpu
from jax.sharding import PartitionSpec as P

HD = 64
BLOCK = 64
SEQ = 1024
PAIR = 2 * HD
BF16 = jnp.bfloat16
F32 = jnp.float32
NT = (((1,), (1,)), ((), ()))
TN = (((0,), (0,)), ((), ()))


def layer_norm(values, norm_gain, norm_bias):
    center = values - jnp.mean(values, axis=-1, keepdims=True)
    spread = jnp.mean(center * center, axis=-1, keepdims=True)
    return center * lax.rsqrt(spread + 1e-05) * norm_gain + norm_bias


def block_mask(rand_blocks):
    blocks = SEQ // BLOCK
    row_ids = jnp.arange(blocks)[:, None]
    col_ids = jnp.arange(blocks)[None, :]
    window = (
        (jnp.abs(row_ids - col_ids) <= 1)
        | (col_ids == 0)
        | (col_ids == blocks - 1)
        | (row_ids == 0)
        | (row_ids == blocks - 1)
    )
    picked = jnp.any(rand_blocks[:, :, :, None] == jnp.arange(blocks)[None, None, None, :], axis=2)
    allowed = window[None] | picked
    return jnp.repeat(jnp.repeat(allowed, BLOCK, axis=1), BLOCK, axis=2)


def attend_forward_split(joined_seq, allowed, scaling):
    queries = joined_seq[:, 0]
    key_rows = joined_seq[:, 1]
    value_rows = joined_seq[:, 2]
    scores = (
        jnp.einsum("qhd,khd->hqk", queries, key_rows, preferred_element_type=jnp.float32) * scaling
    )
    scores = jnp.where(allowed, scores, -1e30)
    highest = jnp.max(scores, axis=-1, keepdims=True)
    shifted = jnp.exp(scores - highest)
    row_totals = jnp.sum(shifted, axis=-1, keepdims=True)
    attn_probs = (shifted / row_totals).astype(jnp.bfloat16)
    context = jnp.einsum("hqk,khd->qhd", attn_probs, value_rows, preferred_element_type=jnp.float32)
    return (context.astype(jnp.bfloat16), (highest + jnp.log(row_totals))[..., 0])


def attend_backward_split(seq_items, allowed, scaling):
    joined_seq, grad_context, row_lse = seq_items
    queries = joined_seq[:, 0]
    key_rows = joined_seq[:, 1]
    value_rows = joined_seq[:, 2]
    scores = (
        jnp.einsum("qhd,khd->hqk", queries, key_rows, preferred_element_type=jnp.float32) * scaling
    )
    scores = jnp.where(allowed, scores, -1e30)
    attn_probs = jnp.exp(scores - row_lse[..., None])
    grad_values = jnp.einsum(
        "hqk,qhd->khd",
        attn_probs.astype(jnp.bfloat16),
        grad_context,
        preferred_element_type=jnp.float32,
    ).astype(jnp.bfloat16)
    grad_probs = jnp.einsum(
        "qhd,khd->hqk", grad_context, value_rows, preferred_element_type=jnp.float32
    )
    row_inner = jnp.sum(grad_probs * attn_probs, axis=-1, keepdims=True)
    grad_scores = (attn_probs * (grad_probs - row_inner)).astype(jnp.bfloat16)
    grad_queries = (
        jnp.einsum("hqk,khd->qhd", grad_scores, key_rows, preferred_element_type=jnp.float32)
        * scaling
    ).astype(jnp.bfloat16)
    grad_keys = (
        jnp.einsum("hqk,qhd->khd", grad_scores, queries, preferred_element_type=jnp.float32)
        * scaling
    ).astype(jnp.bfloat16)
    return jnp.stack([grad_queries, grad_keys, grad_values], axis=1)


def split_sequence(
    hidden_in,
    out_grad,
    ln1_gain,
    ln1_bias,
    w_query,
    w_key,
    w_value,
    w_out,
    ln2_gain,
    ln2_bias,
    w_up,
    b_up,
    w_down,
    b_down,
    rand_blocks,
):
    local_heads = rand_blocks.shape[0]
    head_width = local_heads * HD
    local_rows = hidden_in.shape[0]
    seq_count = local_rows * lax.axis_size("mp") // SEQ
    scaling = HD ** (-0.5)
    allowed = block_mask(rand_blocks)
    inputs = hidden_in.astype(jnp.float32)
    w_joined = jnp.concatenate([w_query, w_key, w_value], axis=1)
    normed_one = layer_norm(inputs, ln1_gain, ln1_bias).astype(jnp.bfloat16)
    rows_one = lax.all_gather(normed_one, "mp", axis=0, tiled=True)
    joined = jnp.dot(rows_one, w_joined, preferred_element_type=jnp.float32).astype(jnp.bfloat16)
    joined_seq = joined.reshape(seq_count, SEQ, 3, local_heads, HD)
    context, row_lse = lax.map(
        lambda seq_block: attend_forward_split(seq_block, allowed, scaling), joined_seq
    )
    context_rows = context.reshape(seq_count * SEQ, head_width)
    middle = inputs + lax.psum_scatter(
        jnp.dot(context_rows, w_out, preferred_element_type=jnp.float32).astype(jnp.bfloat16),
        "mp",
        scatter_dimension=0,
        tiled=True,
    ).astype(jnp.float32)
    normed_two = layer_norm(middle, ln2_gain, ln2_bias).astype(jnp.bfloat16)
    rows_two = lax.all_gather(normed_two, "mp", axis=0, tiled=True)
    up_pre = jnp.dot(rows_two, w_up, preferred_element_type=jnp.float32) + b_up
    hidden = jax.nn.gelu(up_pre, approximate=True).astype(jnp.bfloat16)
    output = (
        middle
        + (
            lax.psum_scatter(
                jnp.dot(hidden, w_down, preferred_element_type=jnp.float32).astype(jnp.bfloat16),
                "mp",
                scatter_dimension=0,
                tiled=True,
            ).astype(jnp.float32)
            + b_down
        )
    ).astype(jnp.bfloat16)
    grad_out = out_grad.astype(jnp.float32)
    bias_down = jnp.sum(grad_out, axis=0)
    rows_ffn = lax.all_gather(out_grad, "mp", axis=0, tiled=True)
    grad_hidden = jnp.einsum("nd,fd->nf", rows_ffn, w_down, preferred_element_type=jnp.float32)
    grad_down = jnp.einsum("nf,nd->fd", hidden, rows_ffn, preferred_element_type=jnp.float32)
    gelu_value, gelu_pull = jax.vjp(lambda pre_act: jax.nn.gelu(pre_act, approximate=True), up_pre)
    grad_up = gelu_pull(grad_hidden)[0].astype(jnp.bfloat16)
    bias_up = jnp.sum(grad_up, axis=0, dtype=jnp.float32)
    grad_up_weight = jnp.einsum("nd,nf->df", rows_two, grad_up, preferred_element_type=jnp.float32)
    grad_normed_two = lax.psum_scatter(
        jnp.einsum("nf,df->nd", grad_up, w_up, preferred_element_type=jnp.float32).astype(
            jnp.bfloat16
        ),
        "mp",
        scatter_dimension=0,
        tiled=True,
    ).astype(jnp.float32)
    norm_value_two, norm_pull_two = jax.vjp(layer_norm, middle, ln2_gain, ln2_bias)
    grad_mid_norm, gain_two, bias_two = norm_pull_two(grad_normed_two)
    grad_middle = grad_out + grad_mid_norm
    grad_attn = grad_middle.astype(jnp.bfloat16)
    rows_attn = lax.all_gather(grad_attn, "mp", axis=0, tiled=True)
    grad_context = jnp.einsum(
        "nd,ed->ne", rows_attn, w_out, preferred_element_type=jnp.float32
    ).astype(jnp.bfloat16)
    grad_out_weight = jnp.einsum(
        "ne,nd->ed", context_rows, rows_attn, preferred_element_type=jnp.float32
    )
    grad_joined = lax.map(
        lambda seq_items: attend_backward_split(seq_items, allowed, scaling),
        (joined_seq, grad_context.reshape(seq_count, SEQ, local_heads, HD), row_lse),
    )
    grad_joined = grad_joined.reshape(seq_count * SEQ, 3 * head_width)
    grad_joined_weight = jnp.einsum(
        "nd,ne->de", rows_one, grad_joined, preferred_element_type=jnp.float32
    )
    grad_normed_one = lax.psum_scatter(
        jnp.einsum("ne,de->nd", grad_joined, w_joined, preferred_element_type=jnp.float32).astype(
            jnp.bfloat16
        ),
        "mp",
        scatter_dimension=0,
        tiled=True,
    ).astype(jnp.float32)
    norm_value_one, norm_pull_one = jax.vjp(layer_norm, inputs, ln1_gain, ln1_bias)
    grad_in_norm, gain_one, bias_one = norm_pull_one(grad_normed_one)
    input_grad = grad_middle + grad_in_norm
    grad_joined_weight, grad_out_weight, grad_up_weight, bias_up, grad_down = (
        lax.psum(grad_joined_weight.astype(jnp.bfloat16), "dp").astype(jnp.float32),
        lax.psum(grad_out_weight.astype(jnp.bfloat16), "dp").astype(jnp.float32),
        lax.psum(grad_up_weight.astype(jnp.bfloat16), "dp").astype(jnp.float32),
        lax.psum(bias_up.astype(jnp.bfloat16), "dp").astype(jnp.float32),
        lax.psum(grad_down.astype(jnp.bfloat16), "dp").astype(jnp.float32),
    )
    gain_one, bias_one, gain_two, bias_two, bias_down = lax.psum(
        (gain_one, bias_one, gain_two, bias_two, bias_down), ("dp", "mp")
    )
    grad_query = grad_joined_weight[:, :head_width]
    grad_key = grad_joined_weight[:, head_width : 2 * head_width]
    grad_value = grad_joined_weight[:, 2 * head_width :]
    return (
        output,
        input_grad,
        gain_one,
        bias_one,
        grad_query,
        grad_key,
        grad_value,
        grad_out_weight,
        gain_two,
        bias_two,
        grad_up_weight,
        bias_up,
        grad_down,
        bias_down,
    )


VMEM_LIMIT = 56 << 20
TILE = 256
SPAN = 512
WIDE = 512
PACE = 0.02


def mm(left, right, dims=(((1,), (0,)), ((), ()))):
    return lax.dot_general(left, right, dims, preferred_element_type=F32)


def call(body, *, grid, in_specs, out_specs, out_shape, micros, name, scratch=(), scalars=1):
    return pl.pallas_call(
        body,
        grid_spec=pltpu.PrefetchScalarGridSpec(
            num_scalar_prefetch=scalars,
            grid=grid,
            in_specs=in_specs,
            out_specs=out_specs,
            scratch_shapes=list(scratch),
        ),
        out_shape=out_shape,
        compiler_params=pltpu.CompilerParams(vmem_limit_bytes=VMEM_LIMIT),
        cost_estimate=pl.CostEstimate(
            flops=int(micros * PACE * 1e9), bytes_accessed=0, transcendentals=0
        ),
        name=name,
    )


def shape(rows, columns, dtype=BF16):
    return jax.ShapeDtypeStruct((rows, columns), dtype)


def row_tile(width, dtype=None):
    return pl.BlockSpec((TILE, width), lambda i, s: (i, 0))


def column_tile(height):
    return pl.BlockSpec((height, TILE), lambda i, s: (0, i))


def resident(rows, columns):
    return pl.BlockSpec((rows, columns), lambda i, s: (0, 0))


def norm_parts(values):
    center = values - jnp.mean(values, axis=-1, keepdims=True)
    spread = jnp.mean(center * center, axis=-1, keepdims=True)
    return center, lax.rsqrt(spread + 1e-05)


def norm_backward(values, gain, grads):
    center, scale = norm_parts(values)
    unit = center * scale
    scaled = grads * gain
    mean_g = jnp.mean(scaled, axis=-1, keepdims=True)
    mean_gu = jnp.mean(scaled * unit, axis=-1, keepdims=True)
    grad_in = scale * (scaled - mean_g - unit * mean_gu)
    return (
        grad_in,
        jnp.sum(grads * unit, axis=0, keepdims=True),
        jnp.sum(grads, axis=0, keepdims=True),
    )


def flipped(rows):
    return rows.astype(F32).T.astype(BF16)


def accumulate(ref, value):
    @pl.when(pl.program_id(0) == 0)
    def _():
        ref[...] = value

    @pl.when(pl.program_id(0) > 0)
    def _():
        ref[...] += value


def norm_in_kernel(s, x_ref, g_ref, gain_ref, bias_ref, n_ref, sum_ref):
    center, scale = norm_parts(x_ref[...].astype(F32))
    n_ref[...] = (center * scale * gain_ref[...] + bias_ref[...]).astype(BF16)
    accumulate(sum_ref, jnp.sum(g_ref[...].astype(F32), axis=0, keepdims=True))


def norm_in(place, hidden_in, out_grad, gain, bias):
    rows, width = hidden_in.shape
    return call(
        norm_in_kernel,
        grid=(rows // TILE,),
        in_specs=[row_tile(width), row_tile(width), resident(1, width), resident(1, width)],
        out_specs=[row_tile(width), resident(1, width)],
        out_shape=[shape(rows, width), shape(1, width, F32)],
        micros=5,
        name="norm_in",
    )(place, hidden_in, out_grad, gain, bias)


def head_lanes(rows, head):
    lanes = lax.broadcasted_iota(jnp.int32, rows.shape, 1)
    return jnp.where(lanes // HD == head, rows, jnp.zeros_like(rows))


def spread_bias(bias, dims):
    blocks = bias.shape[0]
    tokens = lax.broadcasted_iota(jnp.int32, (blocks, blocks * BLOCK), 1) // BLOCK
    which = lax.broadcasted_iota(jnp.int32, tokens.shape, 0)
    return mm(bias, jnp.where(tokens == which, 1.0, 0.0).astype(BF16), dims)


def add_blocks(scores, bias):
    rows, width = scores.shape
    return (scores.reshape(rows // BLOCK, BLOCK, width) + bias[:, None, :]).reshape(rows, width)


def attend_forward_kernel(s, q_ref, k_ref, v_ref, bias_ref, context_ref, lse_ref):
    scaling = HD ** (-0.5)
    bias = [spread_bias(bias_ref[head], (((1,), (0,)), ((), ()))) for head in range(2)]
    jobs = [(start, head) for start in range(0, q_ref.shape[0], SPAN) for head in range(2)]

    def score(job):
        start, head = job
        queries = q_ref[start : start + SPAN, :] * jnp.asarray(scaling, BF16)
        return mm(head_lanes(queries, head), k_ref[...], NT)

    ahead = score(jobs[0])
    parts = []
    for index, (start, head) in enumerate(jobs):
        rows = slice(start, start + SPAN)
        scores = ahead
        if index + 1 < len(jobs):
            ahead = score(jobs[index + 1])
        scores = add_blocks(scores, bias[head][start // BLOCK : (start + SPAN) // BLOCK])
        highest = jnp.max(scores, axis=1, keepdims=True)
        shifted = jnp.exp(scores - highest)
        totals = jnp.sum(shifted, axis=1, keepdims=True)
        parts.append(mm(shifted.astype(BF16), v_ref[...]) / totals)
        lse_ref[0, head : head + 1, rows] = (highest + jnp.log(totals)).T
        if head == 1:
            lanes = lax.broadcasted_iota(jnp.int32, parts[0].shape, 1)
            context_ref[rows, :] = jnp.where(lanes < HD, parts[0], parts[1]).astype(BF16)
            parts = []


def thin_block(column):
    return pl.BlockSpec((SEQ, PAIR), lambda p, s: (0, column(p)))


def attend_forward(place, which, qkv, bias):
    pairs = 2
    blocks = SEQ // BLOCK
    return call(
        attend_forward_kernel,
        grid=(pairs,),
        in_specs=[
            thin_block(lambda p: p),
            thin_block(lambda p: pairs + p),
            thin_block(lambda p: 2 * pairs + p),
            pl.BlockSpec((2, blocks, blocks), lambda p, s: (s[which % 2] * pairs + p, 0, 0)),
        ],
        out_specs=[thin_block(lambda p: p), pl.BlockSpec((1, 2, SEQ), lambda p, s: (p, 0, 0))],
        out_shape=[shape(SEQ, pairs * PAIR), jax.ShapeDtypeStruct((pairs, 2, SEQ), F32)],
        micros=12,
        name="attend_forward",
    )(place, qkv, qkv, qkv, bias)


def attend_backward_kernel(
    outs,
    s,
    q_ref,
    k_ref,
    v_ref,
    grad_ref,
    context_ref,
    lse_ref,
    bias_ref,
    n_hbm,
    ga_hbm,
    *refs,
):
    *extras, out_ref, w_ref, key_acc, value_acc, flat_ref, n_ref, ga_ref, more_ref, sem = refs
    copies = [pltpu.make_async_copy(n_hbm, n_ref, sem.at[0])]
    if outs:
        all_contexts_ref = extras.pop(0)
        copies.append(pltpu.make_async_copy(ga_hbm, ga_ref, sem.at[1]))
    if extras:
        copies.append(pltpu.make_async_copy(extras[0], more_ref, sem.at[2]))
    for copy in copies:
        copy.start()
    scaling = HD ** (-0.5)
    key_rows = k_ref[...]
    value_rows = v_ref[...]
    keys_t = flipped(key_rows)
    bias = [spread_bias(bias_ref[head], TN) for head in range(2)]
    for start in range(0, q_ref.shape[0], SPAN):
        rows = slice(start, start + SPAN)
        queries = q_ref[rows, :] * jnp.asarray(scaling, BF16)
        grads = grad_ref[rows, :]
        inner_t = (grads.astype(F32) * context_ref[rows, :].astype(F32)).T
        probs, slopes, masked_q, masked_g, parts = [], [], [], [], []
        for head in range(2):
            query_h, grad_h = head_lanes(queries, head), head_lanes(grads, head)
            scores = add_blocks(mm(key_rows, query_h, NT), bias[head][:, rows])
            attn = jnp.exp(scores - lse_ref[0, head : head + 1, rows])
            inner = jnp.sum(inner_t[head * HD : (head + 1) * HD], axis=0, keepdims=True)
            slope = (attn * (mm(value_rows, grad_h, NT) - inner)).astype(BF16)
            parts.append(mm(keys_t[head * HD : (head + 1) * HD], slope) * scaling)
            probs.append(attn.astype(BF16))
            slopes.append(slope)
            masked_q.append(query_h)
            masked_g.append(grad_h)
        grad_q = jnp.concatenate(parts, axis=0)
        flat_ref[:PAIR, rows] = grad_q.astype(BF16)
        out_ref[rows, :PAIR] = grad_q.T.astype(BF16)
        grad_k = mm(jnp.concatenate(slopes, axis=1), jnp.concatenate(masked_q, axis=0))
        grad_v = mm(jnp.concatenate(probs, axis=1), jnp.concatenate(masked_g, axis=0))
        if start == 0:
            key_acc[...] = grad_k
            value_acc[...] = grad_v
        else:
            key_acc[...] += grad_k
            value_acc[...] += grad_v
    for part, acc in ((1, key_acc), (2, value_acc)):
        columns = slice(part * PAIR, (part + 1) * PAIR)
        total = acc[...]
        out_ref[:, columns] = total.astype(BF16)
        flat_ref[columns, :] = total.T.astype(BF16)
    for copy in copies:
        copy.wait()

    def give(lines, product):
        if extras:
            product = product + more_ref[lines, :].astype(F32)
        w_ref[lines, :] = product.astype(BF16)

    for part in range(3):
        lines = slice(part * PAIR, (part + 1) * PAIR)
        give(lines, mm(flat_ref[lines, :], n_ref[...]))
    if outs:
        give(slice(3 * PAIR, w_ref.shape[0]), mm(flipped(all_contexts_ref[...]), ga_ref[...]))


def attend_backward(
    place, which, pair, qkv, grad_context, context, row_lse, bias, normed, grad, more=None
):
    pairs = 2
    blocks = SEQ // BLOCK
    width = normed.shape[1]
    lines = 3 * PAIR + (context.shape[1] if pair == 0 else 0)
    outs = pair == 0
    return call(
        lambda *refs: attend_backward_kernel(outs, *refs),
        grid=(1,),
        in_specs=[
            thin_block(lambda p: pair),
            thin_block(lambda p: pairs + pair),
            thin_block(lambda p: 2 * pairs + pair),
            thin_block(lambda p: pair),
            thin_block(lambda p: pair),
            pl.BlockSpec((1, 2, SEQ), lambda p, s: (pair, 0, 0)),
            pl.BlockSpec((2, blocks, blocks), lambda p, s: (s[which % 2] * pairs + pair, 0, 0)),
            pl.BlockSpec(memory_space=pl.ANY),
            pl.BlockSpec(memory_space=pl.ANY),
        ]
        + [resident(*context.shape)] * outs
        + [pl.BlockSpec(memory_space=pl.ANY)] * (more is not None),
        out_specs=[resident(SEQ, 3 * PAIR), resident(lines, width)],
        out_shape=[shape(SEQ, 3 * PAIR), shape(lines, width)],
        scratch=[
            pltpu.VMEM((SEQ, PAIR), F32),
            pltpu.VMEM((SEQ, PAIR), F32),
            pltpu.VMEM((3 * PAIR, SEQ), BF16),
            pltpu.VMEM(normed.shape, BF16),
            pltpu.VMEM(grad.shape if outs else (16, PAIR), BF16),
            pltpu.VMEM((lines, width) if more is not None else (16, PAIR), BF16),
            pltpu.SemaphoreType.DMA((3,)),
        ],
        micros=10,
        name="attend_backward",
    )(
        place,
        qkv,
        qkv,
        qkv,
        grad_context,
        context,
        row_lse,
        bias,
        normed,
        grad,
        *[context] * outs,
        *[more] * (more is not None),
    )


def project_out_kernel(s, x_ref, *refs):
    contexts, weights = refs[:4], refs[4:8]
    gain_ref, bias_ref, middle_ref, n_ref = refs[8:]
    middle = x_ref[...].astype(F32)
    for context_ref, w_ref in zip(contexts, weights):
        middle = middle + mm(context_ref[...], w_ref[...])
    middle_ref[...] = middle
    center, scale = norm_parts(middle)
    n_ref[...] = (center * scale * gain_ref[...] + bias_ref[...]).astype(BF16)


def own_then_far(block, along):
    specs = []
    for which in range(4):
        if along == 0:
            specs.append(pl.BlockSpec(block, lambda i, s, which=which: (s[which], 0)))
        else:
            specs.append(pl.BlockSpec(block, lambda i, s, which=which: (0, s[which])))
    return specs


def project_out(place, hidden_in, contexts, weights, gain, bias):
    rows, width = hidden_in.shape
    return call(
        project_out_kernel,
        grid=(rows // TILE,),
        in_specs=[row_tile(width)]
        + [row_tile(2 * PAIR)] * 4
        + own_then_far((2 * PAIR, width), 0)
        + [resident(1, width)] * 2,
        out_specs=[row_tile(width), row_tile(width)],
        out_shape=[shape(rows, width, F32), shape(rows, width)],
        micros=7,
        name="project_out",
    )(place, hidden_in, *contexts, *weights, gain, bias)


def gelu_and_slope(pre):
    root, cubic = 0.7978845608028654, 0.044715
    square = pre * pre
    bent = jnp.tanh(root * (pre + cubic * pre * square))
    half = 0.5 * pre
    slope = 0.5 * (1.0 + bent) + half * (1.0 - bent * bent) * (root * (1.0 + 3.0 * cubic * square))
    return half + half * bent, slope


def feed_forward_kernel(tiles, s, n_ref, g_ref, bias_ref, *refs):
    *ups, down_ref, h_ref, gu_ref, sum_ref = refs

    def run(up_ref):
        pre = mm(n_ref[...], up_ref[...]) + bias_ref[...]
        grad_hidden = mm(g_ref[...], down_ref[...], NT)
        value, slope = gelu_and_slope(pre)
        h_ref[...] = value.astype(BF16)
        grad_up = (grad_hidden * slope).astype(BF16)
        gu_ref[...] = grad_up
        sum_ref[...] = jnp.sum(grad_up.astype(F32), axis=0, keepdims=True)

    if len(ups) == 1:
        run(ups[0])
    else:
        mine = pl.program_id(0) // (tiles // 2) == s[4]

        @pl.when(mine)
        def _():
            run(ups[0])

        @pl.when(jnp.logical_not(mine))
        def _():
            run(ups[1])


def wide_tile(height):
    return pl.BlockSpec((height, WIDE), lambda i, s: (0, i))


def feed_forward(place, which, normed, out_grad, w_up, b_up, w_down):
    rows, width = normed.shape
    units = b_up.shape[1] // 2
    tiles = units // WIDE
    if which < 2:
        columns = [lambda i, s: (0, s[which] * tiles + i)]
    else:
        columns = [lambda i, s: (0, i % (tiles // 2))] * 2
    return call(
        lambda *refs: feed_forward_kernel(tiles, *refs),
        grid=(tiles,),
        in_specs=[
            resident(rows, width),
            resident(rows, width),
            pl.BlockSpec((1, WIDE), lambda i, s: (0, s[which % 2] * tiles + i)),
        ]
        + [pl.BlockSpec((width, WIDE), column) for column in columns]
        + [pl.BlockSpec((WIDE, width), lambda i, s: (s[which] * tiles + i, 0))],
        out_specs=[wide_tile(rows), wide_tile(rows), wide_tile(1)],
        out_shape=[shape(rows, units), shape(rows, units), shape(1, units, F32)],
        micros=12,
        name="feed_forward",
    )(place, normed, out_grad, b_up, *w_up, w_down)


def unit_blocks(units, width, halved, along):
    half = units // 2
    rows = [pl.BlockSpec((TILE, units), lambda i, s: (i, 0))] * 2
    if halved:
        rows += [
            pl.BlockSpec((TILE, half), lambda i, s: (i, s[4])),
            pl.BlockSpec((TILE, half), lambda i, s: (i, 1 - s[4])),
        ] * 2
    else:
        rows += rows
    far = half if halved else units
    count = 4 if halved else 2
    if along == 0:
        own = [
            pl.BlockSpec((units, width), lambda i, s, which=which: (s[which], 0)) for which in (0, 1)
        ]
        return rows + own + [resident(far, width)] * count
    own = [pl.BlockSpec((width, units), lambda i, s, which=which: (0, s[which])) for which in (0, 1)]
    return rows + own + [resident(width, far)] * count


def unit_arrays(slices, weights):
    arrays = [each for each, group in zip(slices, weights) for _ in group]
    return arrays + [part for group in weights for part in group]


def middle_back_kernel(s, g_ref, middle_ref, gain_ref, *refs):
    grads, weights, outs = refs[:6], refs[6:12], refs[12:16]
    gm_ref, ga_ref, gain_sum, bias_sum, *context_grads = refs[16:]
    total = mm(grads[0][...], weights[0][...], NT)
    for grad_ref, w_ref in zip(grads[1:], weights[1:]):
        total = total + mm(grad_ref[...], w_ref[...], NT)
    grad_in, gain, bias = norm_backward(middle_ref[...], gain_ref[...], total)
    grad_middle = g_ref[...].astype(F32) + grad_in
    gm_ref[...] = grad_middle
    ga_ref[...] = grad_middle.astype(BF16)
    accumulate(gain_sum, gain)
    accumulate(bias_sum, bias)
    for w_ref, out_ref in zip(outs, context_grads):
        out_ref[...] = mm(ga_ref[...], w_ref[...], NT).astype(BF16)


def middle_back(place, out_grad, middle, gain, grad_up, weights, out_weights):
    rows, width = middle.shape
    units = grad_up[0].shape[1]
    return call(
        middle_back_kernel,
        grid=(rows // TILE,),
        in_specs=[row_tile(width), row_tile(width), resident(1, width)]
        + unit_blocks(units, width, True, 1)
        + own_then_far((2 * PAIR, width), 0),
        out_specs=[row_tile(width), row_tile(width)]
        + [resident(1, width)] * 2
        + [row_tile(2 * PAIR)] * 4,
        out_shape=[shape(rows, width, F32), shape(rows, width)]
        + [shape(1, width, F32)] * 2
        + [shape(rows, 2 * PAIR)] * 4,
        micros=18,
        name="middle_back",
    )(place, out_grad, middle, gain, *unit_arrays(grad_up, weights), *out_weights)


def input_back_kernel(s, x_ref, gm_ref, gain_ref, *refs):
    grads, weights = refs[:8], refs[8:12]
    out_ref, gain_sum, bias_sum = refs[12:]
    total = None
    for group in range(4):
        pair_0, pair_1 = grads[2 * group][...], grads[2 * group + 1][...]
        joined = jnp.concatenate(
            [
                pair[:, part * PAIR : (part + 1) * PAIR]
                for part in range(3)
                for pair in (pair_0, pair_1)
            ],
            axis=1,
        )
        product = mm(joined, weights[group][...], NT)
        total = product if total is None else total + product
    grad_in, gain, bias = norm_backward(x_ref[...].astype(F32), gain_ref[...], total)
    out_ref[...] = gm_ref[...] + grad_in
    accumulate(gain_sum, gain)
    accumulate(bias_sum, bias)


def input_back(place, hidden_in, grad_middle, gain, grads, weights):
    rows, width = hidden_in.shape
    return call(
        input_back_kernel,
        grid=(rows // TILE,),
        in_specs=[row_tile(width), row_tile(width), resident(1, width)]
        + [row_tile(3 * PAIR)] * 8
        + [resident(width, 6 * PAIR)] * 4,
        out_specs=[row_tile(width)] + [resident(1, width)] * 2,
        out_shape=[shape(rows, width, F32)] + [shape(1, width, F32)] * 2,
        micros=15,
        name="input_back",
    )(place, hidden_in, grad_middle, gain, *grads, *weights)


def project_down_kernel(s, middle_ref, bias_ref, *refs):
    hidden, weights, out_ref = refs[:4], refs[4:8], refs[8]
    total = middle_ref[...] + bias_ref[...]
    for h_ref, w_ref in zip(hidden, weights):
        total = total + mm(h_ref[...], w_ref[...])
    out_ref[...] = total.astype(BF16)


def project_down(place, middle, bias, hidden, weights):
    rows, width = middle.shape
    units = hidden[0].shape[1]
    return call(
        project_down_kernel,
        grid=(rows // TILE,),
        in_specs=[row_tile(width), resident(1, width)] + unit_blocks(units, width, False, 0),
        out_specs=row_tile(width),
        out_shape=shape(rows, width),
        micros=15,
        name="project_down",
    )(place, middle, bias, *unit_arrays(hidden, weights))


def block_bias(rand_blocks):
    blocks = SEQ // BLOCK
    row_ids = jnp.arange(blocks)[:, None]
    col_ids = jnp.arange(blocks)[None, :]
    window = (
        (jnp.abs(row_ids - col_ids) <= 1)
        | (col_ids == 0)
        | (col_ids == blocks - 1)
        | (row_ids == 0)
        | (row_ids == blocks - 1)
    )
    picked = jnp.any(rand_blocks[:, :, :, None] == col_ids[None, :, None, :], axis=2)
    return jnp.where(window[None] | picked, 0.0, -1e30).astype(BF16)


def swap(array, axis, bit):
    size = lax.axis_size(axis)
    return lax.ppermute(array, axis, [(place, place ^ bit) for place in range(size)])


def add_up(*terms):
    total = terms[0].astype(F32)
    for term in terms[1:]:
        total = total + term.astype(F32)
    return total.astype(terms[0].dtype)


def tied(*values):
    return lax.optimization_barrier(values)


class Sum:
    def __init__(self, steps):
        self.steps = list(steps)
        self.paired = self.steps[0] != "mp"
        self.state, self.sending, self.moving = None, [], []

    def parts_of(self, terms):
        if not self.steps:
            self.state, self.sending = add_up(*terms), []
        elif self.steps[0] == "mp":
            near, far = zip(*terms)
            self.state, self.sending = add_up(*near), [add_up(*far)]
        else:
            bits = self.steps[0]
            partners = [0]
            for bit in bits:
                partners += [bit | other for other in partners]
            self.partners = partners[1:]
            rows = terms[0][0].shape[0] if isinstance(terms[0], tuple) else terms[0].shape[0]
            rows //= len(partners)
            index = lax.axis_index("dp") // bits[0] % len(partners)

            def cut(term, other):
                start = (index ^ (other // bits[0])) * rows
                return lax.dynamic_slice_in_dim(term, start, rows, 0)

            def summed(other):
                if isinstance(terms[0], tuple):
                    return jnp.concatenate(
                        [add_up(*[cut(term, other) for term in half]) for half in zip(*terms)]
                    )
                return add_up(*[cut(term, other) for term in terms])

            self.state = summed(0)
            self.sending = [summed(other) for other in self.partners]

    def go(self):
        step = self.steps.pop(0)
        if step == "mp":
            self.moving = [swap(part, "mp", 1) for part in self.sending]
        else:
            self.moving = [swap(part, "dp", way) for part, way in zip(self.sending, self.partners)]

    def take(self):
        terms = [self.state] + self.moving
        if self.paired and self.steps[0] == "mp":
            self.paired = False
            rows = terms[0].shape[0] // 2
            terms = [(term[:rows], term[rows:]) for term in terms]
        self.parts_of(terms)


class Tied(dict):
    def tie(self, *names):
        for name, value in zip(names, tied(*[self[name] for name in names])):
            self[name] = value
        return self[names[0]]

    def turn(self, *names, sums=()):
        counts = [len(each.moving) for each in sums]
        flat = [part for each in sums for part in each.moving]
        kept = list(tied(*[self[name] for name in names], *flat))
        for name in names:
            self[name] = kept.pop(0)
        for each, count in zip(sums, counts):
            each.moving = [kept.pop(0) for _ in range(count)]
            if count:
                each.take()
        flat = [self[name] for name in names]
        for each in sums:
            flat += [each.state] + each.sending
        kept = list(tied(*flat))
        for name in names:
            self[name] = kept.pop(0)
        for each in sums:
            each.state = kept.pop(0)
            each.sending = [kept.pop(0) for _ in each.sending]
            each.moving = []
            if each.steps:
                each.go()


class Gather:
    def __init__(self, state, steps):
        self.state, self.steps, self.sending, self.moving = state, list(steps), [], []

    def go(self):
        bits = self.steps.pop(0)
        partners = [0]
        for bit in bits:
            partners += [bit | other for other in partners]
        self.moving = [swap(self.state, "dp", way) for way in partners[1:]]

    def take(self):
        self.state = jnp.concatenate([self.state] + self.moving)


class Butterfly:
    def __init__(self, state, steps):
        self.state, self.steps, self.sending, self.moving = state, list(steps), [], []

    def go(self):
        self.moving = [swap(self.state, *self.steps.pop(0))]

    def take(self):
        self.state = self.state + self.moving[0]


def gather_ring(array):
    deep = lax.axis_size("dp") // 4
    chips = [(z, 0) for z in range(deep)] + [(z, 1) for z in reversed(range(deep))]
    order = [z * 4 + y * 2 + core for z, y in chips for core in range(2)]
    return lax.all_gather(array, "dp", axis_index_groups=[order], tiled=True)


def ring_place(z, y, core):
    return 2 * (z + y * (7 - 2 * z)) + core


def spread_kernel(s, *refs):
    *parts, out_ref = refs
    height = parts[0].shape[0]
    for index, part in enumerate(parts):
        out_ref[index * height : (index + 1) * height, :] = part[...].astype(F32)


def spread(place, gathered, sources, target, rows, columns):
    width = gathered.shape[1]
    height = rows * columns // width // 4 // len(sources)
    return call(
        spread_kernel,
        grid=(2, 2),
        in_specs=[
            pl.BlockSpec((height, width), lambda c, y, s, source=source: (source(c, y), 0))
            for source in sources
        ],
        out_specs=pl.BlockSpec((height * len(sources), width), lambda c, y, s: target(c, y)),
        out_shape=shape(rows, columns, F32),
        micros=4,
        name="spread",
    )(place, *[gathered] * len(sources))


def spread_joined_kernel(s, one_a, one_b, two_a, two_b, q_ref, k_ref, v_ref, o_ref, flat):
    mine = pl.program_id(0) == s[0]
    first = 0
    for part_a, part_b in ((one_a, one_b), (two_a, two_b)):
        height = part_a.shape[0] // 8
        for y in range(2):
            for z in range(4):
                start = first + (y * 4 + z) * height
                source = ((y ^ s[4]) * 4 + (z ^ s[5])) * height
                lines = pl.ds(pl.multiple_of(source, height), height)
                flat[start : start + height, :] = jnp.where(mine, part_a[lines, :], part_b[lines, :])
        first += 8 * height
    second = one_a.shape[0]
    for part, ref in enumerate((q_ref, k_ref, v_ref)):
        for pair, first in enumerate((0, second)):
            lines = slice(first + part * PAIR, first + (part + 1) * PAIR)
            ref[:, pair * PAIR : (pair + 1) * PAIR] = flat[lines, :].astype(F32).T
    o_ref[...] = flat[3 * PAIR : second, :].astype(F32)


def spread_joined(place, one, two):
    width = one[0].shape[1]
    columns = pl.BlockSpec((width, 2 * PAIR), lambda c, s: (0, c))
    return call(
        spread_joined_kernel,
        grid=(2,),
        in_specs=[resident(*each.shape) for each in (*one, *two)],
        out_specs=[columns] * 3 + [pl.BlockSpec((2 * PAIR, width), lambda c, s: (c, 0))],
        out_shape=[shape(width, 4 * PAIR, F32)] * 3 + [shape(4 * PAIR, width, F32)],
        scratch=[pltpu.VMEM((one[0].shape[0] + two[0].shape[0], width), BF16)],
        micros=4,
        name="spread_joined",
    )(place, *one, *two)


class At:
    (
        out_piece, up_piece, down_piece, far_ja, far_rand, far_bup, n1, qkv,
        ctx, far_jb, far_out_a, far_out_b, up_mine, down_a, middle, n2,
        g, gu, down, up, up_other, up_b0, up_b1, down_b,
        near_down, near_up, far_down, far_up, gm, ga, gc, gj,
        joined, far_b, own_b, both_all, input_grad, output, grad_down_w, first,
        grad_up_w,
    ) = range(41)


def whole_sequence(
    hidden_in,
    out_grad,
    ln1_gain,
    ln1_bias,
    w_query,
    w_key,
    w_value,
    w_out,
    ln2_gain,
    ln2_bias,
    w_up,
    b_up,
    w_down,
    b_down,
    rand_blocks,
):
    device = lax.axis_index("dp")
    core, over_y, side = device % 2, (device // 2) % 2, lax.axis_index("mp")
    zero = 0 * core
    place = jnp.stack([core, 1 - core, zero, zero, over_y, device // 4]).astype(jnp.int32)

    def part(array, axis, index, count):
        size = array.shape[axis] // count
        return lax.dynamic_slice_in_dim(array, index * size, size, axis)

    def joined(other):
        return jnp.concatenate(
            [part(each, 1, core ^ other, 2) for each in (w_query, w_key, w_value)], axis=1
        )

    def halves_in_order(mine, other, bit):
        return jnp.where(
            bit == 0,
            jnp.concatenate([mine, other], axis=1),
            jnp.concatenate([other, mine], axis=1),
        )

    def row(vector):
        return vector.reshape(1, -1)

    v = Tied()
    own_ja, own_jb = joined(0), joined(1)
    quarter = 2 * core + over_y
    v[At.out_piece], v[At.up_piece] = part(w_out, 0, core, 2), part(w_up, 1, quarter, 4)
    v[At.down_piece] = part(w_down, 0, core, 2)
    v[At.far_ja] = swap(own_ja, "mp", 1)
    v[At.far_rand], v[At.far_bup] = swap(rand_blocks, "mp", 1), swap(b_up, "mp", 1)
    own_bias = block_bias(rand_blocks)
    v[At.n1], bias_down = norm_in(place, hidden_in, out_grad, row(ln1_gain), row(ln1_bias))
    row_lse = [None] * 4

    def attend(g, weights):
        v[At.qkv, g] = mm(v[At.n1], weights).astype(BF16)
        v[At.ctx, g], row_lse[g] = attend_forward(place, g, v[At.qkv, g], bias[g])

    bias = [own_bias, own_bias]
    attend(0, own_ja)
    v.tie(At.n1, (At.ctx, 0), At.far_rand, At.far_bup)
    bias += [block_bias(v[At.far_rand])] * 2
    attend(1, own_jb)
    v.tie(At.n1, At.far_ja, At.out_piece, (At.ctx, 1))
    v[At.far_jb], v[At.far_out_a] = swap(v[At.far_ja], "dp", 1), swap(v[At.out_piece], "mp", 1)
    attend(2, v[At.far_ja])
    v.tie(At.n1, At.far_jb, At.far_out_a, At.up_piece, (At.ctx, 2))
    v[At.far_out_b], v[At.up_mine] = swap(v[At.far_out_a], "dp", 1), swap(v[At.up_piece], "mp", 1)
    attend(3, v[At.far_jb])
    v.tie((At.ctx, 3), At.far_out_b, At.down_piece)
    v[At.down_a] = swap(v[At.down_piece], "mp", 1)
    joined_w = [own_ja, own_jb, v[At.far_ja], v[At.far_jb]]
    out_w = [w_out, w_out, v[At.far_out_a], v[At.far_out_b]]
    v[At.middle], v[At.n2] = project_out(
        place, hidden_in, [v[At.ctx, g] for g in range(4)], out_w, row(ln2_gain), row(ln2_bias)
    )

    hidden, bias_up = [None] * 4, [None] * 4
    up_bias = [row(b_up), row(b_up), row(v[At.far_bup]), row(v[At.far_bup])]
    v[At.g] = out_grad

    def feed(g, up, down):
        hidden[g], v[At.gu, g], bias_up[g] = feed_forward(
            place, g, v[At.n2], v[At.g], up, up_bias[g], down
        )

    def down_grad(g):
        v[At.down, g] = mm(hidden[g], v[At.g], TN).astype(BF16)

    def up_grad(g):
        v[At.up, g] = mm(v[At.n2], v[At.gu, g], TN).astype(BF16)

    v.tie(At.n2, At.up_mine)
    v[At.up_other] = swap(v[At.up_mine], "dp", 2)
    feed(1, (w_up,), w_down)
    v.tie(At.n2, (At.gu, 1))
    feed(0, (w_up,), w_down)
    v.tie(At.g, At.n2, At.up_mine, At.up_other, (At.gu, 0))
    v[At.up_b0], v[At.up_b1] = swap(v[At.up_mine], "dp", 1), swap(v[At.up_other], "dp", 1)
    for g in (1, 0):
        down_grad(g)
        up_grad(g)
    v.tie(At.n2, At.g, At.down_a, At.up_b0, At.up_b1, *[(name, g) for name in (At.down, At.up) for g in (0, 1)])
    v[At.down_b] = swap(v[At.down_a], "dp", 1)
    v[At.near_down], v[At.near_up] = swap(v[At.down, 1], "dp", 1), swap(v[At.up, 1], "dp", 1)
    feed(2, (v[At.up_mine], v[At.up_other]), v[At.down_a])
    v.tie(At.n2, At.g, At.down_b, At.near_down, At.near_up, (At.gu, 2))
    feed(3, (v[At.up_b0], v[At.up_b1]), v[At.down_b])
    up_w = [(w_up,), (w_up,), (v[At.up_mine], v[At.up_other]), (v[At.up_b0], v[At.up_b1])]
    down_w = [(w_down,), (w_down,), (v[At.down_a],), (v[At.down_b],)]
    v.tie(At.g, At.n2, (At.gu, 3))
    down_grad(3)
    v.tie(At.g, At.n2, (At.down, 3))
    v[At.far_down] = swap(v[At.down, 3], "dp", 1)
    up_grad(3)
    v.tie(At.g, At.n2, (At.up, 3), At.far_down)
    v[At.far_up] = swap(v[At.up, 3], "dp", 1)
    down_sum = Sum(["mp", (2,), (4,), (8,)])
    far = (mm(hidden[2], v[At.g], TN) + v[At.far_down].astype(F32)).astype(BF16)
    down_sum.state, down_sum.sending = v[At.down, 0], [far]
    v.turn(At.n2, At.far_up, sums=[down_sum])
    down_sum.moving.append(v[At.near_down])
    far = (mm(v[At.n2], v[At.gu, 2], TN) + v[At.far_up].astype(F32)).astype(BF16)
    up_sum = Sum([(4,), "mp", (2,), (8,)])
    up_sum.parts_of([(add_up(v[At.up, 0], v[At.near_up]), far)])
    v.turn(At.g, sums=[up_sum])

    v[At.gm], v[At.ga], gain_two, bias_two, *context_grads = middle_back(
        place,
        v[At.g],
        v[At.middle],
        row(ln2_gain),
        [v[At.gu, g] for g in range(4)],
        up_w,
        [w_out, w_out, v[At.far_out_a], v[At.far_out_b]],
    )
    for g in range(4):
        v[At.gc, g] = context_grads[g]
    v.tie(At.ga, *[(At.gc, g) for g in range(4)])

    def attend_back(g, pair, more=None):
        v[At.gj, g, pair], v[At.joined, g, pair] = attend_backward(
            place,
            g,
            pair,
            v[At.qkv, g],
            v[At.gc, g],
            v[At.ctx, g],
            row_lse[g],
            bias[g],
            v[At.n1],
            v[At.ga],
            more,
        )

    first, second = Sum(["mp", (2,), (4, 8)]), Sum(["mp", (2,), (4, 8)])
    for each in (first, second):
        each.steps.pop(0)
    attend_back(3, 0)
    v.tie((At.gc, 1), (At.joined, 3, 0))
    v[At.far_b] = swap(v[At.joined, 3, 0], "dp", 1)
    attend_back(1, 0)
    v.turn((At.gc, 2), (At.joined, 1, 0), At.far_b, sums=[down_sum, up_sum])
    v[At.own_b] = swap(v[At.joined, 1, 0], "dp", 1)
    attend_back(2, 0, v[At.far_b])
    v.tie((At.gc, 0), (At.joined, 2, 0), At.own_b)
    first_mp = swap(v[At.joined, 2, 0], "mp", 1)
    attend_back(0, 0, v[At.own_b])
    v.turn((At.gc, 3), (At.joined, 0, 0), sums=[down_sum, up_sum])
    attend_back(3, 1)
    v.turn((At.gc, 2), (At.joined, 3, 1), sums=[down_sum, up_sum])
    v[At.far_b] = swap(v[At.joined, 3, 1], "dp", 1)
    attend_back(2, 1)
    v.tie((At.gc, 1), (At.joined, 2, 1), At.far_b)
    v[At.joined, 2, 1] = add_up(v[At.joined, 2, 1], v[At.far_b])
    first.state, first.moving = v[At.joined, 0, 0], [first_mp]
    v.turn((At.gc, 1), (At.joined, 2, 1), sums=[first])
    second_mp = swap(v[At.joined, 2, 1], "mp", 1)
    attend_back(1, 1)
    v.turn((At.gc, 0), (At.joined, 1, 1), sums=[down_sum, up_sum, first])
    both = jnp.concatenate([down_sum.state, up_sum.state])
    v[At.both_all] = gather_ring(both)
    v[At.own_b] = swap(v[At.joined, 1, 1], "dp", 1)
    attend_back(0, 1)
    v.tie(At.gm, (At.joined, 0, 1), At.own_b)
    v[At.joined, 0, 1] = add_up(v[At.joined, 0, 1], v[At.own_b])
    second.state, second.moving = v[At.joined, 0, 1], [second_mp]
    v.turn(At.gm, (At.joined, 0, 1), sums=[second, first])
    first = Gather(first.state, [(4, 8), (2,), (1,)])
    v.turn(At.gm, sums=[first])
    v[At.input_grad], gain_one, bias_one = input_back(
        place,
        hidden_in,
        v[At.gm],
        row(ln1_gain),
        [v[At.gj, g, pair] for g in range(4) for pair in range(2)],
        joined_w,
    )
    own_up = halves_in_order(bias_up[0], bias_up[1], core)
    far_up = halves_in_order(bias_up[2], bias_up[3], core)
    width = hidden_in.shape[1]
    small = Butterfly(
        jnp.concatenate(
            [gain_one, bias_one, gain_two, bias_two, bias_down]
            + [halves_in_order(own_up, far_up, side).reshape(-1, width)]
        ),
        [("dp", 1), ("mp", 1), ("dp", 2), ("dp", 4), ("dp", 8)],
    )
    v.turn(At.middle, At.input_grad, sums=[second, first, small])
    v[At.output] = project_down(place, v[At.middle], row(b_down), hidden, down_w)
    v.turn(At.output, sums=[second, first, small])
    second = Gather(second.state, [(4, 8), (2,), (1,)])
    v.turn(At.output, sums=[second])
    v.tie(At.both_all, At.output)
    v[At.grad_down_w] = spread(
        place,
        v[At.both_all],
        [
            lambda c, y, z=z, x=x: 2 * ring_place(x * 2 + z, y, c)
            for z in range(2)
            for x in range(2)
        ],
        lambda c, y: (c * 2 + y, 0),
        *w_down.shape,
    )
    v[At.first] = first.moving[0]
    v.turn(At.grad_down_w, At.first, sums=[second, small])
    v.turn(At.first, At.both_all, sums=[second, small])
    v[At.grad_up_w] = spread(
        place,
        v[At.both_all],
        [
            lambda c, z, y=y, x=x: 2 * ring_place(x * 2 + z, y, c) + 1
            for y in range(2)
            for x in range(2)
        ],
        lambda c, z: (z, c),
        *w_up.shape,
    )
    grad_q, grad_k, grad_v, grad_out_w = spread_joined(
        place, (first.state, v[At.first]), (second.state, second.moving[0])
    )
    small.take()
    if small.steps:
        small.go()
        small.take()
    sums = small.state
    up_rows = b_up.shape[0] // width
    bias_up_sum = lax.dynamic_slice_in_dim(sums, 5 + side * up_rows, up_rows).reshape(-1)
    return (
        v[At.output],
        v[At.input_grad],
        sums[0],
        sums[1],
        grad_q,
        grad_k,
        grad_v,
        grad_out_w,
        sums[2],
        sums[3],
        v[At.grad_up_w],
        bias_up_sum,
        v[At.grad_down_w],
        sums[4],
    )


def solution(mesh):
    in_specs = (
        P(("dp", "mp"), None),
        P(("dp", "mp"), None),
        P(),
        P(),
        P(None, "mp"),
        P(None, "mp"),
        P(None, "mp"),
        P("mp", None),
        P(),
        P(),
        P(None, "mp"),
        P("mp"),
        P("mp", None),
        P(),
        P("mp", None, None),
    )
    out_specs = (
        P(("dp", "mp"), None),
        P(("dp", "mp"), None),
        P(),
        P(),
        P(None, "mp"),
        P(None, "mp"),
        P(None, "mp"),
        P("mp", None),
        P(),
        P(),
        P(None, "mp"),
        P("mp"),
        P("mp", None),
        P(),
    )
    def per_device(hidden_in, *others):
        w_query, w_up, rand_blocks = others[3], others[9], others[13]
        whole = hidden_in.shape[0] == SEQ and mesh.shape["mp"] == 2
        halved = mesh.shape["dp"] == 16 and rand_blocks.shape[0] == 8
        sized = w_query.shape == (1024, 512) and w_up.shape == (1024, 2048)
        layer = whole_sequence if whole and halved and sized else split_sequence
        return layer(hidden_in, *others)

    return jax.shard_map(
        per_device, mesh=mesh, in_specs=in_specs, out_specs=out_specs, check_vma=False
    )
```

```python
import jax
import jax.numpy as jnp
from jax import lax
from jax.experimental import pallas as pl
from jax.experimental.pallas import tpu as pltpu
from jax.sharding import PartitionSpec as P

HD = 64
BLOCK = 64
SEQ = 1024
PAIR = 2 * HD
BF16 = jnp.bfloat16
F32 = jnp.float32
NT = (((1,), (1,)), ((), ()))
TN = (((0,), (0,)), ((), ()))


def layer_norm(values, norm_gain, norm_bias):
    center = values - jnp.mean(values, axis=-1, keepdims=True)
    spread = jnp.mean(center * center, axis=-1, keepdims=True)
    return center * lax.rsqrt(spread + 1e-05) * norm_gain + norm_bias


def block_mask(rand_blocks):
    blocks = SEQ // BLOCK
    row_ids = jnp.arange(blocks)[:, None]
    col_ids = jnp.arange(blocks)[None, :]
    window = (
        (jnp.abs(row_ids - col_ids) <= 1)
        | (col_ids == 0)
        | (col_ids == blocks - 1)
        | (row_ids == 0)
        | (row_ids == blocks - 1)
    )
    picked = jnp.any(rand_blocks[:, :, :, None] == jnp.arange(blocks)[None, None, None, :], axis=2)
    allowed = window[None] | picked
    return jnp.repeat(jnp.repeat(allowed, BLOCK, axis=1), BLOCK, axis=2)


def attend_forward_split(joined_seq, allowed, scaling):
    queries = joined_seq[:, 0]
    key_rows = joined_seq[:, 1]
    value_rows = joined_seq[:, 2]
    scores = (
        jnp.einsum("qhd,khd->hqk", queries, key_rows, preferred_element_type=jnp.float32) * scaling
    )
    scores = jnp.where(allowed, scores, -1e30)
    highest = jnp.max(scores, axis=-1, keepdims=True)
    shifted = jnp.exp(scores - highest)
    row_totals = jnp.sum(shifted, axis=-1, keepdims=True)
    attn_probs = (shifted / row_totals).astype(jnp.bfloat16)
    context = jnp.einsum("hqk,khd->qhd", attn_probs, value_rows, preferred_element_type=jnp.float32)
    return (context.astype(jnp.bfloat16), (highest + jnp.log(row_totals))[..., 0])


def attend_backward_split(seq_items, allowed, scaling):
    joined_seq, grad_context, row_lse = seq_items
    queries = joined_seq[:, 0]
    key_rows = joined_seq[:, 1]
    value_rows = joined_seq[:, 2]
    scores = (
        jnp.einsum("qhd,khd->hqk", queries, key_rows, preferred_element_type=jnp.float32) * scaling
    )
    scores = jnp.where(allowed, scores, -1e30)
    attn_probs = jnp.exp(scores - row_lse[..., None])
    grad_values = jnp.einsum(
        "hqk,qhd->khd",
        attn_probs.astype(jnp.bfloat16),
        grad_context,
        preferred_element_type=jnp.float32,
    ).astype(jnp.bfloat16)
    grad_probs = jnp.einsum(
        "qhd,khd->hqk", grad_context, value_rows, preferred_element_type=jnp.float32
    )
    row_inner = jnp.sum(grad_probs * attn_probs, axis=-1, keepdims=True)
    grad_scores = (attn_probs * (grad_probs - row_inner)).astype(jnp.bfloat16)
    grad_queries = (
        jnp.einsum("hqk,khd->qhd", grad_scores, key_rows, preferred_element_type=jnp.float32)
        * scaling
    ).astype(jnp.bfloat16)
    grad_keys = (
        jnp.einsum("hqk,qhd->khd", grad_scores, queries, preferred_element_type=jnp.float32)
        * scaling
    ).astype(jnp.bfloat16)
    return jnp.stack([grad_queries, grad_keys, grad_values], axis=1)


def split_sequence(
    hidden_in,
    out_grad,
    ln1_gain,
    ln1_bias,
    w_query,
    w_key,
    w_value,
    w_out,
    ln2_gain,
    ln2_bias,
    w_up,
    b_up,
    w_down,
    b_down,
    rand_blocks,
):
    local_heads = rand_blocks.shape[0]
    head_width = local_heads * HD
    local_rows = hidden_in.shape[0]
    seq_count = local_rows * lax.axis_size("mp") // SEQ
    scaling = HD ** (-0.5)
    allowed = block_mask(rand_blocks)
    inputs = hidden_in.astype(jnp.float32)
    w_joined = jnp.concatenate([w_query, w_key, w_value], axis=1)
    normed_one = layer_norm(inputs, ln1_gain, ln1_bias).astype(jnp.bfloat16)
    rows_one = lax.all_gather(normed_one, "mp", axis=0, tiled=True)
    joined = jnp.dot(rows_one, w_joined, preferred_element_type=jnp.float32).astype(jnp.bfloat16)
    joined_seq = joined.reshape(seq_count, SEQ, 3, local_heads, HD)
    context, row_lse = lax.map(
        lambda seq_block: attend_forward_split(seq_block, allowed, scaling), joined_seq
    )
    context_rows = context.reshape(seq_count * SEQ, head_width)
    middle = inputs + lax.psum_scatter(
        jnp.dot(context_rows, w_out, preferred_element_type=jnp.float32).astype(jnp.bfloat16),
        "mp",
        scatter_dimension=0,
        tiled=True,
    ).astype(jnp.float32)
    normed_two = layer_norm(middle, ln2_gain, ln2_bias).astype(jnp.bfloat16)
    rows_two = lax.all_gather(normed_two, "mp", axis=0, tiled=True)
    up_pre = jnp.dot(rows_two, w_up, preferred_element_type=jnp.float32) + b_up
    hidden = jax.nn.gelu(up_pre, approximate=True).astype(jnp.bfloat16)
    output = (
        middle
        + (
            lax.psum_scatter(
                jnp.dot(hidden, w_down, preferred_element_type=jnp.float32).astype(jnp.bfloat16),
                "mp",
                scatter_dimension=0,
                tiled=True,
            ).astype(jnp.float32)
            + b_down
        )
    ).astype(jnp.bfloat16)
    grad_out = out_grad.astype(jnp.float32)
    bias_down = jnp.sum(grad_out, axis=0)
    rows_ffn = lax.all_gather(out_grad, "mp", axis=0, tiled=True)
    grad_hidden = jnp.einsum("nd,fd->nf", rows_ffn, w_down, preferred_element_type=jnp.float32)
    grad_down = jnp.einsum("nf,nd->fd", hidden, rows_ffn, preferred_element_type=jnp.float32)
    gelu_value, gelu_pull = jax.vjp(lambda pre_act: jax.nn.gelu(pre_act, approximate=True), up_pre)
    grad_up = gelu_pull(grad_hidden)[0].astype(jnp.bfloat16)
    bias_up = jnp.sum(grad_up, axis=0, dtype=jnp.float32)
    grad_up_weight = jnp.einsum("nd,nf->df", rows_two, grad_up, preferred_element_type=jnp.float32)
    grad_normed_two = lax.psum_scatter(
        jnp.einsum("nf,df->nd", grad_up, w_up, preferred_element_type=jnp.float32).astype(
            jnp.bfloat16
        ),
        "mp",
        scatter_dimension=0,
        tiled=True,
    ).astype(jnp.float32)
    norm_value_two, norm_pull_two = jax.vjp(layer_norm, middle, ln2_gain, ln2_bias)
    grad_mid_norm, gain_two, bias_two = norm_pull_two(grad_normed_two)
    grad_middle = grad_out + grad_mid_norm
    grad_attn = grad_middle.astype(jnp.bfloat16)
    rows_attn = lax.all_gather(grad_attn, "mp", axis=0, tiled=True)
    grad_context = jnp.einsum(
        "nd,ed->ne", rows_attn, w_out, preferred_element_type=jnp.float32
    ).astype(jnp.bfloat16)
    grad_out_weight = jnp.einsum(
        "ne,nd->ed", context_rows, rows_attn, preferred_element_type=jnp.float32
    )
    grad_joined = lax.map(
        lambda seq_items: attend_backward_split(seq_items, allowed, scaling),
        (joined_seq, grad_context.reshape(seq_count, SEQ, local_heads, HD), row_lse),
    )
    grad_joined = grad_joined.reshape(seq_count * SEQ, 3 * head_width)
    grad_joined_weight = jnp.einsum(
        "nd,ne->de", rows_one, grad_joined, preferred_element_type=jnp.float32
    )
    grad_normed_one = lax.psum_scatter(
        jnp.einsum("ne,de->nd", grad_joined, w_joined, preferred_element_type=jnp.float32).astype(
            jnp.bfloat16
        ),
        "mp",
        scatter_dimension=0,
        tiled=True,
    ).astype(jnp.float32)
    norm_value_one, norm_pull_one = jax.vjp(layer_norm, inputs, ln1_gain, ln1_bias)
    grad_in_norm, gain_one, bias_one = norm_pull_one(grad_normed_one)
    input_grad = grad_middle + grad_in_norm
    grad_joined_weight, grad_out_weight, grad_up_weight, bias_up, grad_down = (
        lax.psum(grad_joined_weight.astype(jnp.bfloat16), "dp").astype(jnp.float32),
        lax.psum(grad_out_weight.astype(jnp.bfloat16), "dp").astype(jnp.float32),
        lax.psum(grad_up_weight.astype(jnp.bfloat16), "dp").astype(jnp.float32),
        lax.psum(bias_up.astype(jnp.bfloat16), "dp").astype(jnp.float32),
        lax.psum(grad_down.astype(jnp.bfloat16), "dp").astype(jnp.float32),
    )
    gain_one, bias_one, gain_two, bias_two, bias_down = lax.psum(
        (gain_one, bias_one, gain_two, bias_two, bias_down), ("dp", "mp")
    )
    grad_query = grad_joined_weight[:, :head_width]
    grad_key = grad_joined_weight[:, head_width : 2 * head_width]
    grad_value = grad_joined_weight[:, 2 * head_width :]
    return (
        output,
        input_grad,
        gain_one,
        bias_one,
        grad_query,
        grad_key,
        grad_value,
        grad_out_weight,
        gain_two,
        bias_two,
        grad_up_weight,
        bias_up,
        grad_down,
        bias_down,
    )


VMEM_LIMIT = 56 << 20
TILE = 256
SPAN = 512
BACK = 256
WIDE = 512
PACE = 0.02


def mm(left, right, dims=(((1,), (0,)), ((), ()))):
    return lax.dot_general(left, right, dims, preferred_element_type=F32)


def call(body, *, grid, in_specs, out_specs, out_shape, micros, name, scratch=(), scalars=1):
    return pl.pallas_call(
        body,
        grid_spec=pltpu.PrefetchScalarGridSpec(
            num_scalar_prefetch=scalars,
            grid=grid,
            in_specs=in_specs,
            out_specs=out_specs,
            scratch_shapes=list(scratch),
        ),
        out_shape=out_shape,
        compiler_params=pltpu.CompilerParams(vmem_limit_bytes=VMEM_LIMIT),
        cost_estimate=pl.CostEstimate(
            flops=int(micros * PACE * 1e9), bytes_accessed=0, transcendentals=0
        ),
        name=name,
    )


def shape(rows, columns, dtype=BF16):
    return jax.ShapeDtypeStruct((rows, columns), dtype)


def row_tile(width, dtype=None):
    return pl.BlockSpec((TILE, width), lambda i, s: (i, 0))


def column_tile(height):
    return pl.BlockSpec((height, TILE), lambda i, s: (0, i))


def resident(rows, columns):
    return pl.BlockSpec((rows, columns), lambda i, s: (0, 0))


def norm_parts(values):
    center = values - jnp.mean(values, axis=-1, keepdims=True)
    spread = jnp.mean(center * center, axis=-1, keepdims=True)
    return center, lax.rsqrt(spread + 1e-05)


def norm_backward(values, gain, grads):
    center, scale = norm_parts(values)
    unit = center * scale
    scaled = grads * gain
    mean_g = jnp.mean(scaled, axis=-1, keepdims=True)
    mean_gu = jnp.mean(scaled * unit, axis=-1, keepdims=True)
    grad_in = scale * (scaled - mean_g - unit * mean_gu)
    return (
        grad_in,
        jnp.sum(grads * unit, axis=0, keepdims=True),
        jnp.sum(grads, axis=0, keepdims=True),
    )


def flipped(rows):
    return rows.astype(F32).T.astype(BF16)


def accumulate(ref, value):
    @pl.when(pl.program_id(0) == 0)
    def _():
        ref[...] = value

    @pl.when(pl.program_id(0) > 0)
    def _():
        ref[...] += value


def norm_in_kernel(s, x_ref, g_ref, gain_ref, bias_ref, n_ref, sum_ref):
    center, scale = norm_parts(x_ref[...].astype(F32))
    n_ref[...] = (center * scale * gain_ref[...] + bias_ref[...]).astype(BF16)
    accumulate(sum_ref, jnp.sum(g_ref[...].astype(F32), axis=0, keepdims=True))


def norm_in(place, hidden_in, out_grad, gain, bias):
    rows, width = hidden_in.shape
    return call(
        norm_in_kernel,
        grid=(rows // TILE,),
        in_specs=[row_tile(width), row_tile(width), resident(1, width), resident(1, width)],
        out_specs=[row_tile(width), resident(1, width)],
        out_shape=[shape(rows, width), shape(1, width, F32)],
        micros=5,
        name="norm_in",
    )(place, hidden_in, out_grad, gain, bias)


def head_lanes(rows, head):
    lanes = lax.broadcasted_iota(jnp.int32, rows.shape, 1)
    return jnp.where(lanes // HD == head, rows, jnp.zeros_like(rows))


def spread_bias(bias, dims):
    blocks = bias.shape[0]
    tokens = lax.broadcasted_iota(jnp.int32, (blocks, blocks * BLOCK), 1) // BLOCK
    which = lax.broadcasted_iota(jnp.int32, tokens.shape, 0)
    return mm(bias, jnp.where(tokens == which, 1.0, 0.0).astype(BF16), dims)


def add_blocks(scores, bias):
    rows, width = scores.shape
    return (scores.reshape(rows // BLOCK, BLOCK, width) + bias[:, None, :]).reshape(rows, width)


def attend_forward_kernel(s, q_ref, k_ref, v_ref, bias_ref, context_ref, lse_ref):
    scaling = HD ** (-0.5)
    bias = [spread_bias(bias_ref[head], (((1,), (0,)), ((), ()))) for head in range(2)]
    jobs = [(start, head) for start in range(0, q_ref.shape[0], SPAN) for head in range(2)]

    def score(job):
        start, head = job
        queries = q_ref[start : start + SPAN, :] * jnp.asarray(scaling, BF16)
        return mm(head_lanes(queries, head), k_ref[...], NT)

    ahead = score(jobs[0])
    parts = []
    for index, (start, head) in enumerate(jobs):
        rows = slice(start, start + SPAN)
        scores = ahead
        if index + 1 < len(jobs):
            ahead = score(jobs[index + 1])
        scores = add_blocks(scores, bias[head][start // BLOCK : (start + SPAN) // BLOCK])
        highest = jnp.max(scores, axis=1, keepdims=True)
        shifted = jnp.exp(scores - highest)
        totals = jnp.sum(shifted, axis=1, keepdims=True)
        parts.append(mm(shifted.astype(BF16), v_ref[...]) / totals)
        lse_ref[0, head : head + 1, rows] = (highest + jnp.log(totals)).T
        if head == 1:
            lanes = lax.broadcasted_iota(jnp.int32, parts[0].shape, 1)
            context_ref[rows, :] = jnp.where(lanes < HD, parts[0], parts[1]).astype(BF16)
            parts = []


def thin_block(column):
    return pl.BlockSpec((SEQ, PAIR), lambda p, s: (0, column(p)))


def attend_forward(place, which, qkv, bias):
    pairs = 2
    blocks = SEQ // BLOCK
    return call(
        attend_forward_kernel,
        grid=(pairs,),
        in_specs=[
            thin_block(lambda p: p),
            thin_block(lambda p: pairs + p),
            thin_block(lambda p: 2 * pairs + p),
            pl.BlockSpec((2, blocks, blocks), lambda p, s: (s[which % 2] * pairs + p, 0, 0)),
        ],
        out_specs=[thin_block(lambda p: p), pl.BlockSpec((1, 2, SEQ), lambda p, s: (p, 0, 0))],
        out_shape=[shape(SEQ, pairs * PAIR), jax.ShapeDtypeStruct((pairs, 2, SEQ), F32)],
        micros=12,
        name="attend_forward",
    )(place, qkv, qkv, qkv, bias)


def attend_backward_kernel(
    outs,
    s,
    q_ref,
    k_ref,
    v_ref,
    grad_ref,
    context_ref,
    lse_ref,
    bias_ref,
    n_hbm,
    ga_hbm,
    *refs,
):
    *extras, out_ref, w_ref, key_acc, value_acc, flat_ref, n_ref, ga_ref, more_ref, sem = refs
    copies = [pltpu.make_async_copy(n_hbm, n_ref, sem.at[0])]
    if outs:
        all_contexts_ref = extras.pop(0)
        copies.append(pltpu.make_async_copy(ga_hbm, ga_ref, sem.at[1]))
    if extras:
        copies.append(pltpu.make_async_copy(extras[0], more_ref, sem.at[2]))
    for copy in copies:
        copy.start()
    scaling = HD ** (-0.5)
    key_rows = k_ref[...]
    value_rows = v_ref[...]
    keys_t = flipped(key_rows)
    bias = [spread_bias(bias_ref[head], TN) for head in range(2)]
    jobs = [(start, head) for start in range(0, q_ref.shape[0], BACK) for head in range(2)]

    def products(job):
        start, head = job
        rows = slice(start, start + BACK)
        query_h = head_lanes(q_ref[rows, :] * jnp.asarray(scaling, BF16), head)
        grad_h = head_lanes(grad_ref[rows, :], head)
        return query_h, grad_h, mm(key_rows, query_h, NT), mm(value_rows, grad_h, NT)

    ahead = products(jobs[0])
    for index, (start, head) in enumerate(jobs):
        rows = slice(start, start + BACK)
        if head == 0:
            inner_t = (grad_ref[rows, :].astype(F32) * context_ref[rows, :].astype(F32)).T
            probs, slopes, masked_q, masked_g, parts = [], [], [], [], []
        query_h, grad_h, scores, grad_probs = ahead
        if index + 1 < len(jobs):
            ahead = products(jobs[index + 1])
        scores = add_blocks(scores, bias[head][:, rows])
        attn = jnp.exp(scores - lse_ref[0, head : head + 1, rows])
        inner = jnp.sum(inner_t[head * HD : (head + 1) * HD], axis=0, keepdims=True)
        slope = (attn * (grad_probs - inner)).astype(BF16)
        parts.append(mm(keys_t[head * HD : (head + 1) * HD], slope) * scaling)
        probs.append(attn.astype(BF16))
        slopes.append(slope)
        masked_q.append(query_h)
        masked_g.append(grad_h)
        if head == 0:
            continue
        grad_q = jnp.concatenate(parts, axis=0)
        flat_ref[:PAIR, rows] = grad_q.astype(BF16)
        out_ref[rows, :PAIR] = grad_q.T.astype(BF16)
        grad_k = mm(jnp.concatenate(slopes, axis=1), jnp.concatenate(masked_q, axis=0))
        grad_v = mm(jnp.concatenate(probs, axis=1), jnp.concatenate(masked_g, axis=0))
        if start == 0:
            key_acc[...] = grad_k
            value_acc[...] = grad_v
        else:
            key_acc[...] += grad_k
            value_acc[...] += grad_v
    for part, acc in ((1, key_acc), (2, value_acc)):
        columns = slice(part * PAIR, (part + 1) * PAIR)
        total = acc[...]
        out_ref[:, columns] = total.astype(BF16)
        flat_ref[columns, :] = total.T.astype(BF16)
    for copy in copies:
        copy.wait()

    def give(lines, product):
        if extras:
            product = product + more_ref[lines, :].astype(F32)
        w_ref[lines, :] = product.astype(BF16)

    for part in range(3):
        lines = slice(part * PAIR, (part + 1) * PAIR)
        give(lines, mm(flat_ref[lines, :], n_ref[...]))
    if outs:
        give(slice(3 * PAIR, w_ref.shape[0]), mm(flipped(all_contexts_ref[...]), ga_ref[...]))


def attend_backward(
    place, which, pair, qkv, grad_context, context, row_lse, bias, normed, grad, more=None
):
    pairs = 2
    blocks = SEQ // BLOCK
    width = normed.shape[1]
    lines = 3 * PAIR + (context.shape[1] if pair == 0 else 0)
    outs = pair == 0
    return call(
        lambda *refs: attend_backward_kernel(outs, *refs),
        grid=(1,),
        in_specs=[
            thin_block(lambda p: pair),
            thin_block(lambda p: pairs + pair),
            thin_block(lambda p: 2 * pairs + pair),
            thin_block(lambda p: pair),
            thin_block(lambda p: pair),
            pl.BlockSpec((1, 2, SEQ), lambda p, s: (pair, 0, 0)),
            pl.BlockSpec((2, blocks, blocks), lambda p, s: (s[which % 2] * pairs + pair, 0, 0)),
            pl.BlockSpec(memory_space=pl.ANY),
            pl.BlockSpec(memory_space=pl.ANY),
        ]
        + [resident(*context.shape)] * outs
        + [pl.BlockSpec(memory_space=pl.ANY)] * (more is not None),
        out_specs=[resident(SEQ, 3 * PAIR), resident(lines, width)],
        out_shape=[shape(SEQ, 3 * PAIR), shape(lines, width)],
        scratch=[
            pltpu.VMEM((SEQ, PAIR), F32),
            pltpu.VMEM((SEQ, PAIR), F32),
            pltpu.VMEM((3 * PAIR, SEQ), BF16),
            pltpu.VMEM(normed.shape, BF16),
            pltpu.VMEM(grad.shape if outs else (16, PAIR), BF16),
            pltpu.VMEM((lines, width) if more is not None else (16, PAIR), BF16),
            pltpu.SemaphoreType.DMA((3,)),
        ],
        micros=10,
        name="attend_backward",
    )(
        place,
        qkv,
        qkv,
        qkv,
        grad_context,
        context,
        row_lse,
        bias,
        normed,
        grad,
        *[context] * outs,
        *[more] * (more is not None),
    )


def project_out_kernel(s, x_ref, *refs):
    contexts, weights = refs[:4], refs[4:8]
    gain_ref, bias_ref, middle_ref, n_ref = refs[8:]
    middle = x_ref[...].astype(F32)
    for context_ref, w_ref in zip(contexts, weights):
        middle = middle + mm(context_ref[...], w_ref[...])
    middle_ref[...] = middle
    center, scale = norm_parts(middle)
    n_ref[...] = (center * scale * gain_ref[...] + bias_ref[...]).astype(BF16)


def own_then_far(block, along):
    specs = []
    for which in range(4):
        if along == 0:
            specs.append(pl.BlockSpec(block, lambda i, s, which=which: (s[which], 0)))
        else:
            specs.append(pl.BlockSpec(block, lambda i, s, which=which: (0, s[which])))
    return specs


def project_out(place, hidden_in, contexts, weights, gain, bias):
    rows, width = hidden_in.shape
    return call(
        project_out_kernel,
        grid=(rows // TILE,),
        in_specs=[row_tile(width)]
        + [row_tile(2 * PAIR)] * 4
        + own_then_far((2 * PAIR, width), 0)
        + [resident(1, width)] * 2,
        out_specs=[row_tile(width), row_tile(width)],
        out_shape=[shape(rows, width, F32), shape(rows, width)],
        micros=7,
        name="project_out",
    )(place, hidden_in, *contexts, *weights, gain, bias)


def gelu_and_slope(pre):
    root, cubic = 0.7978845608028654, 0.044715
    square = pre * pre
    bent = jnp.tanh(root * (pre + cubic * pre * square))
    half = 0.5 * pre
    slope = 0.5 * (1.0 + bent) + half * (1.0 - bent * bent) * (root * (1.0 + 3.0 * cubic * square))
    return half + half * bent, slope


def feed_forward_kernel(tiles, s, n_ref, g_ref, bias_ref, *refs):
    *ups, down_ref, h_ref, gu_ref, sum_ref = refs

    def run(up_ref):
        pre = mm(n_ref[...], up_ref[...]) + bias_ref[...]
        grad_hidden = mm(g_ref[...], down_ref[...], NT)
        value, slope = gelu_and_slope(pre)
        h_ref[...] = value.astype(BF16)
        grad_up = (grad_hidden * slope).astype(BF16)
        gu_ref[...] = grad_up
        sum_ref[...] = jnp.sum(grad_up.astype(F32), axis=0, keepdims=True)

    if len(ups) == 1:
        run(ups[0])
    else:
        mine = pl.program_id(0) // (tiles // 2) == s[4]

        @pl.when(mine)
        def _():
            run(ups[0])

        @pl.when(jnp.logical_not(mine))
        def _():
            run(ups[1])


def wide_tile(height):
    return pl.BlockSpec((height, WIDE), lambda i, s: (0, i))


def feed_forward(place, which, normed, out_grad, w_up, b_up, w_down):
    rows, width = normed.shape
    units = b_up.shape[1] // 2
    tiles = units // WIDE
    if which < 2:
        columns = [lambda i, s: (0, s[which] * tiles + i)]
    else:
        columns = [lambda i, s: (0, i % (tiles // 2))] * 2
    return call(
        lambda *refs: feed_forward_kernel(tiles, *refs),
        grid=(tiles,),
        in_specs=[
            resident(rows, width),
            resident(rows, width),
            pl.BlockSpec((1, WIDE), lambda i, s: (0, s[which % 2] * tiles + i)),
        ]
        + [pl.BlockSpec((width, WIDE), column) for column in columns]
        + [pl.BlockSpec((WIDE, width), lambda i, s: (s[which] * tiles + i, 0))],
        out_specs=[wide_tile(rows), wide_tile(rows), wide_tile(1)],
        out_shape=[shape(rows, units), shape(rows, units), shape(1, units, F32)],
        micros=12,
        name="feed_forward",
    )(place, normed, out_grad, b_up, *w_up, w_down)


def unit_blocks(units, width, halved, along):
    half = units // 2
    rows = [pl.BlockSpec((TILE, units), lambda i, s: (i, 0))] * 2
    if halved:
        rows += [
            pl.BlockSpec((TILE, half), lambda i, s: (i, s[4])),
            pl.BlockSpec((TILE, half), lambda i, s: (i, 1 - s[4])),
        ] * 2
    else:
        rows += rows
    far = half if halved else units
    count = 4 if halved else 2
    if along == 0:
        own = [
            pl.BlockSpec((units, width), lambda i, s, which=which: (s[which], 0)) for which in (0, 1)
        ]
        return rows + own + [resident(far, width)] * count
    own = [pl.BlockSpec((width, units), lambda i, s, which=which: (0, s[which])) for which in (0, 1)]
    return rows + own + [resident(width, far)] * count


def unit_arrays(slices, weights):
    arrays = [each for each, group in zip(slices, weights) for _ in group]
    return arrays + [part for group in weights for part in group]


def middle_back_kernel(s, g_ref, middle_ref, gain_ref, *refs):
    grads, weights, outs = refs[:6], refs[6:12], refs[12:16]
    gm_ref, ga_ref, gain_sum, bias_sum, *context_grads = refs[16:]
    total = mm(grads[0][...], weights[0][...], NT)
    for grad_ref, w_ref in zip(grads[1:], weights[1:]):
        total = total + mm(grad_ref[...], w_ref[...], NT)
    grad_in, gain, bias = norm_backward(middle_ref[...], gain_ref[...], total)
    grad_middle = g_ref[...].astype(F32) + grad_in
    gm_ref[...] = grad_middle
    ga_ref[...] = grad_middle.astype(BF16)
    accumulate(gain_sum, gain)
    accumulate(bias_sum, bias)
    for w_ref, out_ref in zip(outs, context_grads):
        out_ref[...] = mm(ga_ref[...], w_ref[...], NT).astype(BF16)


def middle_back(place, out_grad, middle, gain, grad_up, weights, out_weights):
    rows, width = middle.shape
    units = grad_up[0].shape[1]
    return call(
        middle_back_kernel,
        grid=(rows // TILE,),
        in_specs=[row_tile(width), row_tile(width), resident(1, width)]
        + unit_blocks(units, width, True, 1)
        + own_then_far((2 * PAIR, width), 0),
        out_specs=[row_tile(width), row_tile(width)]
        + [resident(1, width)] * 2
        + [row_tile(2 * PAIR)] * 4,
        out_shape=[shape(rows, width, F32), shape(rows, width)]
        + [shape(1, width, F32)] * 2
        + [shape(rows, 2 * PAIR)] * 4,
        micros=18,
        name="middle_back",
    )(place, out_grad, middle, gain, *unit_arrays(grad_up, weights), *out_weights)


def input_back_kernel(s, x_ref, gm_ref, gain_ref, *refs):
    grads, weights = refs[:8], refs[8:12]
    out_ref, gain_sum, bias_sum = refs[12:]
    total = None
    for group in range(4):
        pair_0, pair_1 = grads[2 * group][...], grads[2 * group + 1][...]
        joined = jnp.concatenate(
            [
                pair[:, part * PAIR : (part + 1) * PAIR]
                for part in range(3)
                for pair in (pair_0, pair_1)
            ],
            axis=1,
        )
        product = mm(joined, weights[group][...], NT)
        total = product if total is None else total + product
    grad_in, gain, bias = norm_backward(x_ref[...].astype(F32), gain_ref[...], total)
    out_ref[...] = gm_ref[...] + grad_in
    accumulate(gain_sum, gain)
    accumulate(bias_sum, bias)


def input_back(place, hidden_in, grad_middle, gain, grads, weights):
    rows, width = hidden_in.shape
    return call(
        input_back_kernel,
        grid=(rows // TILE,),
        in_specs=[row_tile(width), row_tile(width), resident(1, width)]
        + [row_tile(3 * PAIR)] * 8
        + [resident(width, 6 * PAIR)] * 4,
        out_specs=[row_tile(width)] + [resident(1, width)] * 2,
        out_shape=[shape(rows, width, F32)] + [shape(1, width, F32)] * 2,
        micros=15,
        name="input_back",
    )(place, hidden_in, grad_middle, gain, *grads, *weights)


def project_down_kernel(s, middle_ref, bias_ref, *refs):
    hidden, weights, out_ref = refs[:4], refs[4:8], refs[8]
    total = middle_ref[...] + bias_ref[...]
    for h_ref, w_ref in zip(hidden, weights):
        total = total + mm(h_ref[...], w_ref[...])
    out_ref[...] = total.astype(BF16)


def project_down(place, middle, bias, hidden, weights):
    rows, width = middle.shape
    units = hidden[0].shape[1]
    return call(
        project_down_kernel,
        grid=(rows // TILE,),
        in_specs=[row_tile(width), resident(1, width)] + unit_blocks(units, width, False, 0),
        out_specs=row_tile(width),
        out_shape=shape(rows, width),
        micros=15,
        name="project_down",
    )(place, middle, bias, *unit_arrays(hidden, weights))


def block_bias(rand_blocks):
    blocks = SEQ // BLOCK
    row_ids = jnp.arange(blocks)[:, None]
    col_ids = jnp.arange(blocks)[None, :]
    window = (
        (jnp.abs(row_ids - col_ids) <= 1)
        | (col_ids == 0)
        | (col_ids == blocks - 1)
        | (row_ids == 0)
        | (row_ids == blocks - 1)
    )
    picked = jnp.any(rand_blocks[:, :, :, None] == col_ids[None, :, None, :], axis=2)
    return jnp.where(window[None] | picked, 0.0, -1e30).astype(BF16)


def swap(array, axis, bit):
    size = lax.axis_size(axis)
    return lax.ppermute(array, axis, [(place, place ^ bit) for place in range(size)])


def add_up(*terms):
    total = terms[0].astype(F32)
    for term in terms[1:]:
        total = total + term.astype(F32)
    return total.astype(terms[0].dtype)


def tied(*values):
    return lax.optimization_barrier(values)


def cut_starts(device, cuts):
    starts = {}
    for bits, rows in cuts:
        count = 1 << len(bits)
        index = lax.shift_right_logical(device, jnp.uint32(bits[0].bit_length() - 1))
        index = index & jnp.uint32(count - 1)
        for other in range(count):
            starts[bits, other * bits[0], rows] = (index ^ jnp.uint32(other)) * jnp.uint32(rows)
    return starts


class Sum:
    def __init__(self, steps, starts):
        self.steps, self.starts = list(steps), starts
        self.paired = self.steps[0] != "mp"
        self.state, self.sending, self.moving = None, [], []

    def parts_of(self, terms):
        if not self.steps:
            self.state, self.sending = add_up(*terms), []
        elif self.steps[0] == "mp":
            near, far = zip(*terms)
            self.state, self.sending = add_up(*near), [add_up(*far)]
        else:
            bits = self.steps[0]
            partners = [0]
            for bit in bits:
                partners += [bit | other for other in partners]
            self.partners = partners[1:]
            rows = terms[0][0].shape[0] if isinstance(terms[0], tuple) else terms[0].shape[0]
            rows //= len(partners)

            def cut(term, other):
                return lax.dynamic_slice_in_dim(term, self.starts[bits, other, rows], rows, 0)

            def summed(other):
                if isinstance(terms[0], tuple):
                    return jnp.concatenate(
                        [add_up(*[cut(term, other) for term in half]) for half in zip(*terms)]
                    )
                return add_up(*[cut(term, other) for term in terms])

            self.state = summed(0)
            self.sending = [summed(other) for other in self.partners]

    def go(self):
        step = self.steps.pop(0)
        if step == "mp":
            self.moving = [swap(part, "mp", 1) for part in self.sending]
        else:
            self.moving = [swap(part, "dp", way) for part, way in zip(self.sending, self.partners)]

    def take(self):
        terms = [self.state] + self.moving
        if self.paired and self.steps[0] == "mp":
            self.paired = False
            rows = terms[0].shape[0] // 2
            terms = [(term[:rows], term[rows:]) for term in terms]
        self.parts_of(terms)


class Tied(dict):
    def tie(self, *names):
        for name, value in zip(names, tied(*[self[name] for name in names])):
            self[name] = value
        return self[names[0]]

    def turn(self, *names, sums=()):
        counts = [len(each.moving) for each in sums]
        flat = [part for each in sums for part in each.moving]
        kept = list(tied(*[self[name] for name in names], *flat))
        for name in names:
            self[name] = kept.pop(0)
        for each, count in zip(sums, counts):
            each.moving = [kept.pop(0) for _ in range(count)]
            if count:
                each.take()
        flat = [self[name] for name in names]
        for each in sums:
            flat += [each.state] + each.sending
        kept = list(tied(*flat))
        for name in names:
            self[name] = kept.pop(0)
        for each in sums:
            each.state = kept.pop(0)
            each.sending = [kept.pop(0) for _ in each.sending]
            each.moving = []
            if each.steps:
                each.go()


class Gather:
    def __init__(self, state, steps):
        self.state, self.steps, self.sending, self.moving = state, list(steps), [], []

    def go(self):
        bits = self.steps.pop(0)
        partners = [0]
        for bit in bits:
            partners += [bit | other for other in partners]
        self.moving = [swap(self.state, "dp", way) for way in partners[1:]]

    def take(self):
        self.state = jnp.concatenate([self.state] + self.moving)


class Butterfly:
    def __init__(self, state, steps):
        self.state, self.steps, self.sending, self.moving = state, list(steps), [], []

    def go(self):
        self.moving = [swap(self.state, *self.steps.pop(0))]

    def take(self):
        self.state = self.state + self.moving[0]


def gather_ring(array):
    deep = lax.axis_size("dp") // 4
    chips = [(z, 0) for z in range(deep)] + [(z, 1) for z in reversed(range(deep))]
    order = [z * 4 + y * 2 + core for z, y in chips for core in range(2)]
    return lax.all_gather(array, "dp", axis_index_groups=[order], tiled=True)


def ring_place(z, y, core):
    return 2 * (z + y * (7 - 2 * z)) + core


def spread_kernel(s, *refs):
    *parts, out_ref = refs
    height = parts[0].shape[0]
    for index, part in enumerate(parts):
        out_ref[index * height : (index + 1) * height, :] = part[...].astype(F32)


def spread(place, gathered, sources, target, rows, columns):
    width = gathered.shape[1]
    height = rows * columns // width // 4 // len(sources)
    return call(
        spread_kernel,
        grid=(2, 2),
        in_specs=[
            pl.BlockSpec((height, width), lambda c, y, s, source=source: (source(c, y), 0))
            for source in sources
        ],
        out_specs=pl.BlockSpec((height * len(sources), width), lambda c, y, s: target(c, y)),
        out_shape=shape(rows, columns, F32),
        micros=4,
        name="spread",
    )(place, *[gathered] * len(sources))


def spread_joined_kernel(s, one_a, one_b, two_a, two_b, q_ref, k_ref, v_ref, o_ref, flat):
    mine = pl.program_id(0) == s[0]
    first = 0
    for part_a, part_b in ((one_a, one_b), (two_a, two_b)):
        height = part_a.shape[0] // 8
        for y in range(2):
            for z in range(4):
                start = first + (y * 4 + z) * height
                source = ((y ^ s[4]) * 4 + (z ^ s[5])) * height
                lines = pl.ds(pl.multiple_of(source, height), height)
                flat[start : start + height, :] = jnp.where(mine, part_a[lines, :], part_b[lines, :])
        first += 8 * height
    second = one_a.shape[0]
    for part, ref in enumerate((q_ref, k_ref, v_ref)):
        for pair, first in enumerate((0, second)):
            lines = slice(first + part * PAIR, first + (part + 1) * PAIR)
            ref[:, pair * PAIR : (pair + 1) * PAIR] = flat[lines, :].astype(F32).T
    o_ref[...] = flat[3 * PAIR : second, :].astype(F32)


def spread_joined(place, one, two):
    width = one[0].shape[1]
    columns = pl.BlockSpec((width, 2 * PAIR), lambda c, s: (0, c))
    return call(
        spread_joined_kernel,
        grid=(2,),
        in_specs=[resident(*each.shape) for each in (*one, *two)],
        out_specs=[columns] * 3 + [pl.BlockSpec((2 * PAIR, width), lambda c, s: (c, 0))],
        out_shape=[shape(width, 4 * PAIR, F32)] * 3 + [shape(4 * PAIR, width, F32)],
        scratch=[pltpu.VMEM((one[0].shape[0] + two[0].shape[0], width), BF16)],
        micros=4,
        name="spread_joined",
    )(place, *one, *two)


class At:
    (
        out_piece, up_piece, down_piece, far_ja, far_rand, far_bup, n1, qkv,
        ctx, far_jb, far_out_a, far_out_b, up_mine, down_a, middle, n2,
        g, gu, down, up, up_other, up_b0, up_b1, down_b,
        near_down, near_up, far_down, far_up, bias_up, gm, ga, gc,
        gj, joined, far_b, own_b, both_all, input_grad, output, grad_down_w,
        grad_up_w, first, second,
    ) = range(43)


def whole_sequence(
    hidden_in,
    out_grad,
    ln1_gain,
    ln1_bias,
    w_query,
    w_key,
    w_value,
    w_out,
    ln2_gain,
    ln2_bias,
    w_up,
    b_up,
    w_down,
    b_down,
    rand_blocks,
):
    device = lax.axis_index("dp")
    core, over_y, side = device % 2, (device // 2) % 2, lax.axis_index("mp")
    zero = 0 * core
    place = jnp.stack([core, 1 - core, zero, zero, over_y, device // 4]).astype(jnp.int32)

    def part(array, axis, index, count):
        size = array.shape[axis] // count
        return lax.dynamic_slice_in_dim(array, index * size, size, axis)

    def joined(other):
        return jnp.concatenate(
            [part(each, 1, core ^ other, 2) for each in (w_query, w_key, w_value)], axis=1
        )

    def halves_in_order(mine, other, bit):
        return jnp.where(
            bit == 0,
            jnp.concatenate([mine, other], axis=1),
            jnp.concatenate([other, mine], axis=1),
        )

    def row(vector):
        return vector.reshape(1, -1)

    v = Tied()
    cuts = [((2,), 512), ((4,), 256), ((8,), 128), ((4,), 512), ((2,), 256)]
    cuts += [((2,), 320), ((4, 8), 80), ((2,), 192), ((4, 8), 48)]
    starts = cut_starts(device.astype(jnp.uint32), cuts)
    own_ja, own_jb, *cut_values = tied(joined(0), joined(1), *starts.values())
    starts = dict(zip(starts, cut_values))
    quarter = 2 * core + over_y
    v[At.out_piece], v[At.up_piece] = part(w_out, 0, core, 2), part(w_up, 1, quarter, 4)
    v[At.down_piece] = part(w_down, 0, core, 2)
    v[At.far_ja] = swap(own_ja, "mp", 1)
    v[At.far_rand], v[At.far_bup] = swap(rand_blocks, "mp", 1), swap(b_up, "mp", 1)
    own_bias = block_bias(rand_blocks)
    v[At.n1], bias_down = norm_in(place, hidden_in, out_grad, row(ln1_gain), row(ln1_bias))
    row_lse = [None] * 4

    def attend(g, weights):
        v[At.qkv, g] = mm(v[At.n1], weights).astype(BF16)
        v[At.ctx, g], row_lse[g] = attend_forward(place, g, v[At.qkv, g], bias[g])

    bias = [own_bias, own_bias]
    attend(0, own_ja)
    v.tie(At.n1, (At.ctx, 0), At.far_rand, At.far_bup)
    bias += [block_bias(v[At.far_rand])] * 2
    attend(1, own_jb)
    v.tie(At.n1, At.far_ja, At.out_piece, (At.ctx, 1))
    v[At.far_jb], v[At.far_out_a] = swap(v[At.far_ja], "dp", 1), swap(v[At.out_piece], "mp", 1)
    attend(2, v[At.far_ja])
    v.tie(At.n1, At.far_jb, At.far_out_a, At.up_piece, (At.ctx, 2))
    v[At.far_out_b], v[At.up_mine] = swap(v[At.far_out_a], "dp", 1), swap(v[At.up_piece], "mp", 1)
    attend(3, v[At.far_jb])
    v.tie((At.ctx, 3), At.far_out_b, At.down_piece)
    v[At.down_a] = swap(v[At.down_piece], "mp", 1)
    joined_w = [own_ja, own_jb, v[At.far_ja], v[At.far_jb]]
    out_w = [w_out, w_out, v[At.far_out_a], v[At.far_out_b]]
    v[At.middle], v[At.n2] = project_out(
        place, hidden_in, [v[At.ctx, g] for g in range(4)], out_w, row(ln2_gain), row(ln2_bias)
    )

    hidden, bias_up = [None] * 4, [None] * 4
    up_bias = [row(b_up), row(b_up), row(v[At.far_bup]), row(v[At.far_bup])]
    v[At.g] = out_grad

    def feed(g, up, down):
        hidden[g], v[At.gu, g], bias_up[g] = feed_forward(
            place, g, v[At.n2], v[At.g], up, up_bias[g], down
        )

    def down_grad(g):
        v[At.down, g] = mm(hidden[g], v[At.g], TN).astype(BF16)

    def up_grad(g):
        v[At.up, g] = mm(v[At.n2], v[At.gu, g], TN).astype(BF16)

    v.tie(At.n2, At.up_mine)
    v[At.up_other] = swap(v[At.up_mine], "dp", 2)
    feed(1, (w_up,), w_down)
    v.tie(At.n2, (At.gu, 1))
    feed(0, (w_up,), w_down)
    v.tie(At.g, At.n2, At.up_mine, At.up_other, (At.gu, 0))
    v[At.up_b0], v[At.up_b1] = swap(v[At.up_mine], "dp", 1), swap(v[At.up_other], "dp", 1)
    for g in (1, 0):
        down_grad(g)
        up_grad(g)
    v.tie(At.n2, At.g, At.down_a, At.up_b0, At.up_b1, *[(name, g) for name in (At.down, At.up) for g in (0, 1)])
    v[At.down_b] = swap(v[At.down_a], "dp", 1)
    v[At.near_down], v[At.near_up] = swap(v[At.down, 1], "dp", 1), swap(v[At.up, 1], "dp", 1)
    feed(2, (v[At.up_mine], v[At.up_other]), v[At.down_a])
    v.tie(At.n2, At.g, At.down_b, At.near_down, At.near_up, (At.gu, 2))
    feed(3, (v[At.up_b0], v[At.up_b1]), v[At.down_b])
    up_w = [(w_up,), (w_up,), (v[At.up_mine], v[At.up_other]), (v[At.up_b0], v[At.up_b1])]
    down_w = [(w_down,), (w_down,), (v[At.down_a],), (v[At.down_b],)]
    v.tie(At.g, At.n2, (At.gu, 3))
    down_grad(3)
    v.tie(At.g, At.n2, (At.down, 3))
    v[At.far_down] = swap(v[At.down, 3], "dp", 1)
    up_grad(3)
    v.tie(At.g, At.n2, (At.up, 3), At.far_down)
    v[At.far_up] = swap(v[At.up, 3], "dp", 1)
    down_sum = Sum(["mp", (2,), (4,), (8,)], starts)
    far = (mm(hidden[2], v[At.g], TN) + v[At.far_down].astype(F32)).astype(BF16)
    down_sum.state, down_sum.sending = v[At.down, 0], [far]
    v.turn(At.n2, At.far_up, sums=[down_sum])
    down_sum.moving.append(v[At.near_down])
    far = (mm(v[At.n2], v[At.gu, 2], TN) + v[At.far_up].astype(F32)).astype(BF16)
    up_sum = Sum([(4,), "mp", (2,), (8,)], starts)
    up_sum.parts_of([(add_up(v[At.up, 0], v[At.near_up]), far)])
    own_up = halves_in_order(bias_up[0], bias_up[1], core)
    far_up = halves_in_order(bias_up[2], bias_up[3], core)
    width = hidden_in.shape[1]
    v[At.bias_up] = halves_in_order(own_up, far_up, side).reshape(-1, width)
    v.turn(At.g, At.bias_up, sums=[up_sum])

    v[At.gm], v[At.ga], gain_two, bias_two, *context_grads = middle_back(
        place,
        v[At.g],
        v[At.middle],
        row(ln2_gain),
        [v[At.gu, g] for g in range(4)],
        up_w,
        [w_out, w_out, v[At.far_out_a], v[At.far_out_b]],
    )
    for g in range(4):
        v[At.gc, g] = context_grads[g]
    v.tie(At.ga, *[(At.gc, g) for g in range(4)])

    def attend_back(g, pair, more=None):
        v[At.gj, g, pair], v[At.joined, g, pair] = attend_backward(
            place,
            g,
            pair,
            v[At.qkv, g],
            v[At.gc, g],
            v[At.ctx, g],
            row_lse[g],
            bias[g],
            v[At.n1],
            v[At.ga],
            more,
        )

    first, second = Sum(["mp", (2,), (4, 8)], starts), Sum(["mp", (2,), (4, 8)], starts)
    for each in (first, second):
        each.steps.pop(0)
    attend_back(3, 0)
    v.tie((At.gc, 1), (At.joined, 3, 0))
    v[At.far_b] = swap(v[At.joined, 3, 0], "dp", 1)
    attend_back(1, 0)
    v.turn((At.gc, 2), (At.joined, 1, 0), At.far_b, sums=[down_sum, up_sum])
    v[At.own_b] = swap(v[At.joined, 1, 0], "dp", 1)
    attend_back(2, 0, v[At.far_b])
    v.tie((At.gc, 0), (At.joined, 2, 0), At.own_b)
    first_mp = swap(v[At.joined, 2, 0], "mp", 1)
    attend_back(0, 0, v[At.own_b])
    v.turn((At.gc, 3), (At.joined, 0, 0), sums=[down_sum, up_sum])
    attend_back(3, 1)
    v.turn((At.gc, 2), (At.joined, 3, 1), sums=[down_sum, up_sum])
    v[At.far_b] = swap(v[At.joined, 3, 1], "dp", 1)
    attend_back(2, 1)
    v.tie((At.gc, 1), (At.joined, 2, 1), At.far_b)
    v[At.joined, 2, 1] = add_up(v[At.joined, 2, 1], v[At.far_b])
    first.state, first.moving = v[At.joined, 0, 0], [first_mp]
    v.turn((At.gc, 1), (At.joined, 2, 1), sums=[first])
    second_mp = swap(v[At.joined, 2, 1], "mp", 1)
    attend_back(1, 1)
    v.turn((At.gc, 0), (At.joined, 1, 1), sums=[down_sum, up_sum])
    both = jnp.concatenate([down_sum.state, up_sum.state])
    v[At.both_all] = gather_ring(both)
    v[At.own_b] = swap(v[At.joined, 1, 1], "dp", 1)
    attend_back(0, 1)
    v.tie(At.gm, (At.joined, 0, 1), At.own_b)
    v[At.joined, 0, 1] = add_up(v[At.joined, 0, 1], v[At.own_b])
    second.state, second.moving = v[At.joined, 0, 1], [second_mp]
    v.turn(At.gm, (At.joined, 0, 1), sums=[second, first])
    v[At.input_grad], gain_one, bias_one = input_back(
        place,
        hidden_in,
        v[At.gm],
        row(ln1_gain),
        [v[At.gj, g, pair] for g in range(4) for pair in range(2)],
        joined_w,
    )
    small = Butterfly(
        jnp.concatenate(
            [gain_one, bias_one, gain_two, bias_two, bias_down]
            + [v[At.bias_up]]
        ),
        [("dp", 1), ("mp", 1), ("dp", 2), ("dp", 4), ("dp", 8)],
    )
    v.turn(At.middle, At.input_grad, sums=[second, first, small])
    first = Gather(first.state, [(4, 8), (2,), (1,)])
    v.turn(At.middle, sums=[first])
    v[At.output] = project_down(place, v[At.middle], row(b_down), hidden, down_w)
    v.turn(At.output, sums=[second, first, small])
    second = Gather(second.state, [(4, 8), (2,), (1,)])
    v.turn(At.output, sums=[second])
    v.tie(At.both_all, At.output)
    v[At.grad_down_w] = spread(
        place,
        v[At.both_all],
        [
            lambda c, y, z=z, x=x: 2 * ring_place(x * 2 + z, y, c)
            for z in range(2)
            for x in range(2)
        ],
        lambda c, y: (c * 2 + y, 0),
        *w_down.shape,
    )
    v.turn(At.grad_down_w, At.both_all, sums=[second, first, small])
    v[At.grad_up_w] = spread(
        place,
        v[At.both_all],
        [
            lambda c, z, y=y, x=x: 2 * ring_place(x * 2 + z, y, c) + 1
            for y in range(2)
            for x in range(2)
        ],
        lambda c, z: (z, c),
        *w_up.shape,
    )
    v[At.first] = first.moving[0]
    v.turn(At.first, At.grad_up_w, sums=[second, small])
    v[At.second] = second.moving[0]
    v.turn(At.second, sums=[small])
    grad_q, grad_k, grad_v, grad_out_w = spread_joined(
        place, (first.state, v[At.first]), (second.state, v[At.second])
    )
    small.moving[0], grad_q = tied(small.moving[0], grad_q)
    small.take()
    sums = small.state
    up_rows = b_up.shape[0] // width
    bias_up_sum = lax.dynamic_slice_in_dim(sums, 5 + side * up_rows, up_rows).reshape(-1)
    return (
        v[At.output],
        v[At.input_grad],
        sums[0],
        sums[1],
        grad_q,
        grad_k,
        grad_v,
        grad_out_w,
        sums[2],
        sums[3],
        v[At.grad_up_w],
        bias_up_sum,
        v[At.grad_down_w],
        sums[4],
    )


def solution(mesh):
    in_specs = (
        P(("dp", "mp"), None),
        P(("dp", "mp"), None),
        P(),
        P(),
        P(None, "mp"),
        P(None, "mp"),
        P(None, "mp"),
        P("mp", None),
        P(),
        P(),
        P(None, "mp"),
        P("mp"),
        P("mp", None),
        P(),
        P("mp", None, None),
    )
    out_specs = (
        P(("dp", "mp"), None),
        P(("dp", "mp"), None),
        P(),
        P(),
        P(None, "mp"),
        P(None, "mp"),
        P(None, "mp"),
        P("mp", None),
        P(),
        P(),
        P(None, "mp"),
        P("mp"),
        P("mp", None),
        P(),
    )
    def per_device(hidden_in, *others):
        w_query, w_up, rand_blocks = others[3], others[9], others[13]
        whole = hidden_in.shape[0] == SEQ and mesh.shape["mp"] == 2
        halved = mesh.shape["dp"] == 16 and rand_blocks.shape[0] == 8
        sized = w_query.shape == (1024, 512) and w_up.shape == (1024, 2048)
        layer = whole_sequence if whole and halved and sized else split_sequence
        return layer(hidden_in, *others)

    return jax.shard_map(
        per_device, mesh=mesh, in_specs=in_specs, out_specs=out_specs, check_vma=False
    )
```
